256 devices in a mesh: req: 32 (over z, x_lo, core), tp: 8 (over x_hi, y).
Axes of the slice: x: 4 (x_hi: 2, x_lo: 2; x = x_hi * 2 + x_lo), y: 4, z: 8, core: 2. Of those that a mesh axis runs over, the one named last changes fastest.
Arguments:
- suffix_query: bfloat16 [8192, 5120], P('req', 'tp')
- suffix_key: bfloat16 [8192, 1024], P('req', 'tp')
- suffix_value: bfloat16 [8192, 1024], P('req', 'tp'), may hold values from -6 to 6
- prefix_key: bfloat16 [32, 1024, 1024], P('req', None, 'tp')
- prefix_value: bfloat16 [32, 1024, 1024], P('req', None, 'tp'), may hold values from -6 to 6
- residual: bfloat16 [8192, 5120], P('req'), may hold values from -6 to 6
- out_weight: bfloat16 [5120, 5120], P('tp'), may hold values from -0.15625 to 0.15625
- norm_gain: bfloat16 [5120], P('tp'), may hold values from 0.099609375 to 1.8984375
- lengths: int32 [32], replicated, may hold values from 1 to 256, 4915 in all
- request_slot: int32 [32], replicated, may hold values from 0 to 31, each once
- prefix_owner: int32 [32], replicated, may hold values from 0 to 31, each once
- request_group: int32 [32, 1], replicated, may hold values from 0 to 3
Outputs:
- hidden: bfloat16 [8192, 5120], P('req', 'tp')
- normed: bfloat16 [8192, 5120], P('req', 'tp')
- cache_key: bfloat16 [8192, 1024], P('req', 'tp')
The draws below stay inside these ranges and needn't reach their ends.
Inputs may be any that keep to these rules, and one draw needn't show every extreme that they name: `request_slot`: a permutation. `prefix_owner`: a permutation. `request_group`: every group has one request or more. `lengths`: some request has all 256 slots live.
All inputs are finite; a program needn't handle non-finite values.
Results may differ from the reference program's by a relative error of at most 0.0067.
Values may be sent and summed in bfloat16 or wider, within the bound.
No kernel may reach another device: no remote copies, remote signals or barrier semaphores. Data moves between devices by JAX's collectives and lax.ppermute only.
A program may use at most 128 MiB of HBM per device.

```python
import math
import jax
import jax.numpy as jnp
import numpy as np
from jax import lax

D = 5120
QH = 40
KVH = 8
HD = 128
GROUPS = 4
SLOTS = 256
PBLK = 1024
REQS = 32
PREFIX = 8192
ROWS = 8192
N_REQ = 32


def draw_prefix_key(key, part):
    noise = jax.random.normal(jax.random.fold_in(key, 1), (N_REQ, PBLK, KVH * HD), jnp.float32)
    values = noise
    return jnp.clip(values, -6.0, 6.0).astype(jnp.bfloat16)


def draw_suffix_key(key, part):
    noise = jax.random.normal(jax.random.fold_in(key, 5), (N_REQ * SLOTS, KVH * HD), jnp.float32)
    values = 1.4 * noise
    return jnp.clip(values, -8.0, 8.0).astype(jnp.bfloat16)


def draw_suffix_query(key, part):
    noise = jax.random.normal(jax.random.fold_in(key, 3), (N_REQ * SLOTS, QH * HD), jnp.float32)
    values = 3.0 * noise
    return jnp.clip(values, -12.0, 12.0).astype(jnp.bfloat16)


def shard_levels(own_key, shape, cuts, least, top_value):
    level, own = 1.0, jax.random.fold_in(own_key, 6)
    for dim, shards_of in cuts:
        steps = jnp.exp(jax.random.uniform(jax.random.fold_in(own, dim), (shards_of,), jnp.float32, least / len(cuts), top_value / len(cuts)))
        level = level * jnp.repeat(steps, shape[dim] // shards_of).reshape([-1 if axis == dim else 1 for axis in range(len(shape))])
    return level


def different_ones(key, rows, amount, top, lift):
    order = jax.random.permutation(jax.random.fold_in(key, 1), amount)
    favour = order
    for power in range(3):
        favour = favour * favour // amount
    favour = favour * lift // amount
    lots = jax.random.randint(jax.random.fold_in(key, 2), (rows, amount), 0, 4096) + favour
    sure = jax.random.permutation(jax.random.fold_in(key, 3), rows)[jnp.arange(amount) % rows]
    lots = jnp.where(jnp.arange(rows)[:, None] == sure[None, :], 1 << 14, lots)
    merit = lots * amount + jnp.arange(amount)
    return lax.top_k(merit.astype(jnp.int32), top)[1].astype(jnp.int32)


def profile(amount, total, limit, slope):
    portions = [(1 << 20) // math.isqrt(rank ** slope) + 1 for rank in range(2, amount + 1)]
    surplus, given = total - limit - (amount - 1), [1] * (amount - 1)
    while surplus > 0:
        free = [i for i in range(amount - 1) if given[i] < limit]
        mass, left = sum([portions[i] for i in free]), surplus
        for i in free:
            addition = min(limit - given[i], max(1, left * portions[i] // mass), surplus)
            given[i] = given[i] + addition
            surplus = surplus - addition
    return np.array([limit] + given)


def ragged_sizes(own_key, amount, total, limit, lean):
    if amount == 2:
        one = jax.random.randint(own_key, (), max(1, total - limit), min(limit, total - 1) + 1)
        return jnp.stack([one, total - one])
    sizes = jnp.asarray(profile(amount, total, limit, lean), jnp.int32)
    couples = (amount - 1) // 2
    source_of, taker = sizes[1:1 + 2 * couples:2], sizes[2:2 + 2 * couples:2]
    margin = jnp.minimum(source_of - 1, limit - taker)
    moved = jax.random.randint(jax.random.fold_in(own_key, 1), (couples,), 0, 1 << 20) % (margin + 1)
    sizes = sizes.at[1:1 + 2 * couples:2].set(source_of - moved).at[2:2 + 2 * couples:2].set(taker + moved)
    return sizes[jax.random.permutation(jax.random.fold_in(own_key, 2), amount)]


def scatter_about(own_key, shape, deviation, bound, pieces=(), dtype=jnp.bfloat16):
    factor_of = shard_levels(own_key, shape, pieces, -0.22, 0.18) if pieces else 1.0
    array = jax.random.normal(own_key, shape, jnp.float32) * deviation * factor_of
    return jnp.minimum(jnp.maximum(array, -bound), bound).astype(dtype)


def setup_inputs(seed: int = 0) -> dict:
    key_list = jax.random.split(jax.random.key(seed), 13)
    suffix_query = draw_suffix_query(jax.random.fold_in(key_list[12], 71), 0)
    suffix_key = draw_suffix_key(jax.random.fold_in(key_list[12], 71), 0)
    suffix_value = scatter_about(key_list[2], (ROWS, KVH * HD), 1.0, 6.0, ((0, 32), (1, 8)))
    prefix_key = draw_prefix_key(jax.random.fold_in(key_list[12], 71), 0)
    prefix_value = scatter_about(key_list[4], (N_REQ, PBLK, KVH * HD), 1.0, 6.0, ((0, 32), (2, 8)))
    residual = scatter_about(key_list[5], (ROWS, D), 1.0, 6.0, ((0, 32),))
    out_weight = scatter_about(key_list[6], (QH * HD, D), (QH * HD // 4) ** -0.5, 0.15625, ((0, 8),))
    norm_gain = jnp.clip(1.0 + 0.18 * jax.random.normal(key_list[7], (D,), jnp.float32), 0.099609375, 1.8984375).astype(jnp.bfloat16)
    lengths = ragged_sizes(key_list[8], REQS, REQS * SLOTS * 3 // 5, SLOTS, 2).astype(jnp.int32)
    request_slot = jax.random.permutation(key_list[9], N_REQ).astype(jnp.int32)
    prefix_owner = jax.random.permutation(key_list[10], N_REQ).astype(jnp.int32)
    request_group = different_ones(key_list[11], REQS, GROUPS, 1, 4096)
    return {"suffix_query": suffix_query, "suffix_key": suffix_key, "suffix_value": suffix_value, "prefix_key": prefix_key, "prefix_value": prefix_value, "residual": residual, "out_weight": out_weight, "norm_gain": norm_gain, "lengths": lengths, "request_slot": request_slot, "prefix_owner": prefix_owner, "request_group": request_group}


THETA = 1000000.0
NEGATIVE = -1e+30
EPSILON = 1e-06

def rotate(values, head_count, position_base):
    row_count = values.shape[0]
    half_dim = HD // 2
    positions = (position_base + jnp.arange(row_count)).astype(jnp.float32)
    frequency = THETA ** (-(jnp.arange(half_dim).astype(jnp.float32) * 2.0 / HD))
    angles = positions[:, None] * frequency[None, :]
    cosines = jnp.cos(angles)[:, None, :]
    sines = jnp.sin(angles)[:, None, :]
    per_head = values.reshape(row_count, head_count, HD)
    front_half = per_head[..., :half_dim]
    back_half = per_head[..., half_dim:]
    joined = jnp.concatenate([front_half * cosines - back_half * sines, back_half * cosines + front_half * sines], axis=-1)
    return joined.reshape(row_count, head_count * HD)

def attend(queries, keys_in, values_in, visible):
    row_count = queries.shape[0]
    kv_count = keys_in.shape[-1] // HD
    ratio = queries.shape[1] // HD // kv_count
    query_heads = queries.reshape(row_count, kv_count, ratio, HD).astype(jnp.float32)
    key_heads = keys_in.reshape(-1, kv_count, HD).astype(jnp.float32)
    value_heads = values_in.reshape(-1, kv_count, HD).astype(jnp.float32)
    scores = jnp.einsum('sgrd,kgd->sgrk', query_heads, key_heads) * HD ** (-0.5)
    if visible is not None:
        scores = jnp.where(visible[:, None, None, :], scores, NEGATIVE)
    block_max = lax.optimization_barrier(jnp.max(scores, axis=-1))
    weights = jnp.exp(scores - block_max[..., None])
    block_sum = lax.optimization_barrier(jnp.sum(weights, axis=-1))
    probs = weights.astype(jnp.bfloat16).astype(jnp.float32)
    block_out = jnp.einsum('sgrk,kgd->sgrd', probs, value_heads) / block_sum[..., None]
    heads = kv_count * ratio
    return (block_max.reshape(row_count, heads), block_sum.reshape(row_count, heads), block_out.reshape(row_count, heads, HD))

def reference(suffix_query, suffix_key, suffix_value, prefix_key, prefix_value, residual, out_weight, norm_gain, lengths, request_slot, prefix_owner, request_group):
    per_group = N_REQ // GROUPS
    owner_table = prefix_owner.reshape(GROUPS, per_group)
    positions = jnp.arange(SLOTS).astype(jnp.int32)

    def one_request(place):
        request = request_slot[place]
        group_now = request_group[request, 0]
        length_now = lengths[request]
        first_row = (place * SLOTS).astype(jnp.int32)
        query_rows = lax.dynamic_slice_in_dim(suffix_query, first_row, SLOTS, 0)
        key_rows = lax.dynamic_slice_in_dim(suffix_key, first_row, SLOTS, 0)
        value_rows = lax.dynamic_slice_in_dim(suffix_value, first_row, SLOTS, 0)
        queries = rotate(query_rows.astype(jnp.float32), QH, PREFIX).astype(jnp.bfloat16)
        keys_rot = rotate(key_rows.astype(jnp.float32), KVH, PREFIX)
        live_rows = positions < length_now
        cache_rows = jnp.where(live_rows[:, None], keys_rot, 0.0).astype(jnp.bfloat16)
        visible = (positions[None, :] <= positions[:, None]) & (positions[None, :] < length_now)
        own_max, own_sum, own_out = attend(queries, cache_rows, value_rows, visible)
        blocks = owner_table[group_now]

        def one_block(device):
            part_max, part_sum, part_out = attend(queries, prefix_key[device], prefix_value[device], None)
            rounded = lax.optimization_barrier(part_out.astype(jnp.bfloat16)).astype(jnp.float32)
            return (part_max, part_sum, rounded)
        part_maxes, part_sums, part_outs = lax.map(one_block, blocks)
        overall = jnp.maximum(own_max, lax.optimization_barrier(jnp.max(part_maxes, axis=0)))
        own_weight = own_sum * jnp.exp(own_max - overall)
        part_weights = part_sums * jnp.exp(part_maxes - overall[None])
        numerator = own_weight[..., None] * own_out + lax.optimization_barrier(jnp.sum(part_weights[..., None] * part_outs, axis=0))
        denominator = own_weight + lax.optimization_barrier(jnp.sum(part_weights, axis=0))
        mixed = jnp.where(live_rows[:, None, None], numerator / denominator[..., None], 0.0)
        return (mixed.astype(jnp.bfloat16).reshape(SLOTS, QH * HD), cache_rows)
    attn, cache_rows = lax.map(one_request, jnp.arange(N_REQ).astype(jnp.int32))
    attn = attn.reshape(N_REQ * SLOTS, QH * HD)
    cache_key = cache_rows.reshape(N_REQ * SLOTS, KVH * HD)
    hidden = (residual.astype(jnp.float32) + jnp.dot(attn, out_weight, preferred_element_type=jnp.float32)).astype(jnp.bfloat16)
    widened = hidden.astype(jnp.float32)
    scale_rows = lax.rsqrt(lax.optimization_barrier(jnp.mean(widened * widened, axis=1, keepdims=True)) + EPSILON)
    normed = (widened * scale_rows * norm_gain.astype(jnp.float32)[None, :]).astype(jnp.bfloat16)
    return (hidden, normed, cache_key)
```

```python
import jax
import jax.numpy as jnp
from jax import lax
from jax.experimental import pallas as pl
from jax.experimental.pallas import tpu as pltpu
from jax.sharding import PartitionSpec as P

HD = 128
GROUPS = 4
PLANE = 4
TILE = 128
THETA = 1000000.0
NEGATIVE = -1e30
EPSILON = 1e-06
LOG2E = 1.4426950408889634


SMEM = pltpu.SMEM
VMEM = pltpu.VMEM


def full(space=VMEM):
    return pl.BlockSpec(memory_space=space)


def params():
    return pltpu.CompilerParams(vmem_limit_bytes=40 * 1024 * 1024)


def turn(x, cosines, sines):
    return x * cosines + pltpu.roll(x, HD // 2, 1) * sines


def fold(q, k, v, acc_ref, ml_ref, at, rows, h, visible):
    scores = lax.dot_general(
        q, k, (((1,), (1,)), ((), ())), preferred_element_type=jnp.float32
    )
    if visible is not None:
        scores = jnp.where(visible, scores, NEGATIVE)
    old_max = ml_ref[at + (rows, slice(h, h + 1))]
    old_sum = ml_ref[at + (rows, slice(8 + h, 9 + h))]
    new_max = jnp.maximum(old_max, jnp.max(scores, axis=1, keepdims=True))
    rate = HD ** (-0.5) * LOG2E
    weights = jnp.exp2((scores - new_max) * rate)
    keep = jnp.exp2((old_max - new_max) * rate)
    ml_ref[at + (rows, slice(h, h + 1))] = new_max
    ml_ref[at + (rows, slice(8 + h, 9 + h))] = old_sum * keep + jnp.sum(
        weights, axis=1, keepdims=True
    )
    acc_ref[at + (h, rows)] = acc_ref[at + (h, rows)] * keep + jnp.dot(
        weights.astype(jnp.bfloat16), v, preferred_element_type=jnp.float32
    )


def clear(acc_ref, ml_ref):
    acc_ref[...] = jnp.zeros_like(acc_ref)
    lane = lax.broadcasted_iota(jnp.int32, ml_ref.shape, ml_ref.ndim - 1)
    ml_ref[...] = jnp.where(lane < 8, NEGATIVE, 0.0)


def own_kernel(meta, q_in, k_in, v_in, cos_in, sin_in, q_out, key_out, acc_ref, ml_ref):
    heads = q_out.shape[0]
    slots = k_in.shape[0]
    length = meta[0]
    cosines = cos_in[...]
    sines = sin_in[...]
    for h in range(heads):
        x = q_in[:, h * HD : (h + 1) * HD].astype(jnp.float32)
        q_out[h] = turn(x, cosines, sines).astype(jnp.bfloat16)
    turned = turn(k_in[...].astype(jnp.float32), cosines, sines)
    place = lax.broadcasted_iota(jnp.int32, turned.shape, 0)
    key_out[...] = jnp.where(place < length, turned, 0.0).astype(jnp.bfloat16)
    clear(acc_ref, ml_ref)

    def step(j, carry):
        rows = pl.ds(pl.multiple_of(j * TILE, TILE), TILE)
        t = j * TILE + lax.broadcasted_iota(jnp.int32, (TILE, slots), 0)
        u = lax.broadcasted_iota(jnp.int32, (TILE, slots), 1)
        visible = (u <= t) & (u < length)
        k = key_out[...]
        v = v_in[...]
        for h in range(heads):
            fold(q_out[h, rows], k, v, acc_ref, ml_ref, (), rows, h, visible)
        return carry

    lax.fori_loop(0, meta[PLANE], step, 0)


def visit(meta, base, q_ref, kv_refs, acc_ref, ml_ref):
    heads = q_ref.shape[1]
    for e, kv in enumerate(kv_refs):

        def request(i, carry, e=e, kv=kv):
            @pl.when(meta[2 * PLANE + (base + e) * PLANE + i] == 1)
            def _():
                def step(j, inner):
                    rows = pl.ds(pl.multiple_of(j * TILE, TILE), TILE)
                    k = kv[0]
                    v = kv[1]
                    for h in range(heads):
                        fold(q_ref[i, h, rows], k, v, acc_ref, ml_ref, (i,), rows, h, None)
                    return inner

                lax.fori_loop(0, meta[PLANE + i], step, 0)

            return carry

        lax.fori_loop(0, PLANE, request, 0)


def make_first(base, count):
    def kernel(meta, q_own, acc_own, ml_own, q1, q2, q3, cos_in, sin_in, *rest):
        kv_refs = rest[:count]
        q_ref, acc_ref, ml_ref = rest[count:]
        heads = q_own.shape[0]
        cosines = cos_in[...]
        sines = sin_in[...]
        clear(acc_ref, ml_ref)
        q_ref[0] = q_own[...]
        acc_ref[0] = acc_own[...]
        ml_ref[0] = ml_own[...]
        for i, q_in in enumerate((q1, q2, q3)):
            for h in range(heads):
                x = q_in[:, h * HD : (h + 1) * HD].astype(jnp.float32)
                q_ref[i + 1, h] = turn(x, cosines, sines).astype(jnp.bfloat16)
        visit(meta, base, q_ref, kv_refs, acc_ref, ml_ref)

    return kernel


def make_middle(base, count):
    def kernel(meta, q_ref, acc_in, ml_in, *rest):
        kv_refs = rest[:count]
        acc_ref, ml_ref = rest[count:]
        acc_ref[...] = acc_in[...]
        ml_ref[...] = ml_in[...]
        visit(meta, base, q_ref, kv_refs, acc_ref, ml_ref)

    return kernel


def make_last(base, count):
    def kernel(meta, q_ref, acc_in, ml_in, *rest):
        kv_refs = rest[:count]
        acc_own, ml_own, o1, o2, o3, acc_ref, ml_ref = rest[count:]
        heads, slots = acc_own.shape[:2]
        acc_ref[...] = acc_in[...]
        ml_ref[...] = ml_in[...]
        visit(meta, base, q_ref, kv_refs, acc_ref, ml_ref)
        acc_own[...] = acc_ref[0]
        ml_own[...] = ml_ref[0]
        for i, out in enumerate((o1, o2, o3)):
            stats = ml_ref[i + 1]
            for h in range(heads):
                total = stats[:, 8 + h : 9 + h]
                inverse = jnp.where(total > 0, 1.0 / jnp.where(total > 0, total, 1.0), 0.0)
                out[h * slots : (h + 1) * slots] = (acc_ref[i + 1, h] * inverse).astype(
                    jnp.bfloat16
                )
            flat = jnp.transpose(stats)[:16]
            high = flat.astype(jnp.bfloat16)
            left = flat - high.astype(jnp.float32)
            middle = left.astype(jnp.bfloat16)
            low = (left - middle.astype(jnp.float32)).astype(jnp.bfloat16)
            first = heads * slots
            for n, piece in enumerate((high, middle, low)):
                for half in range(slots // HD):
                    at = first + (n * (slots // HD) + half) * 16
                    out[at : at + 16] = piece[:, half * HD : (half + 1) * HD]

    return kernel


def combine_kernel(meta, acc_own, ml_own, o1, o2, o3, attn_ref):
    heads, slots = acc_own.shape[:2]
    own = ml_own[...]
    stats = [own]
    first = heads * slots
    for part in (o1, o2, o3):
        pieces = []
        for n in range(3):
            halves = []
            for half in range(slots // HD):
                at = first + (n * (slots // HD) + half) * 16
                halves.append(part[at : at + 16].astype(jnp.float32))
            pieces.append(jnp.concatenate(halves, axis=1))
        flat = pieces[0] + pieces[1] + pieces[2]
        wide = jnp.concatenate([flat, jnp.zeros((HD - 16, slots), jnp.float32)], axis=0)
        stats.append(jnp.transpose(wide))
    rate = HD ** (-0.5) * LOG2E
    live = lax.broadcasted_iota(jnp.int32, (slots, HD), 0) < meta[0]
    for h in range(heads):
        maxima = [s[:, h : h + 1] for s in stats]
        sums = [s[:, 8 + h : 9 + h] for s in stats]
        top = jnp.maximum(jnp.maximum(maxima[0], maxima[1]), jnp.maximum(maxima[2], maxima[3]))
        factor = [jnp.exp2((m - top) * rate) for m in maxima]
        mass = [f * s for f, s in zip(factor, sums)]
        total = mass[0] + mass[1] + mass[2] + mass[3]
        value = acc_own[h] * factor[0]
        for w, part in zip(mass[1:], (o1, o2, o3)):
            value = value + w * part[h * slots : (h + 1) * slots].astype(jnp.float32)
        attn_ref[:, h * HD : (h + 1) * HD] = jnp.where(live, value / total, 0.0).astype(
            jnp.bfloat16
        )


def project_kernel(where, attn_ref, weight_ref, out_ref):
    del where
    out_ref[...] = jnp.dot(
        attn_ref[...], weight_ref[...], preferred_element_type=jnp.float32
    ).astype(out_ref.dtype)


def project(where, attn, weight, columns, dtype):
    slots, inner = attn.shape
    return pl.pallas_call(
        project_kernel,
        out_shape=jax.ShapeDtypeStruct((slots, columns), dtype),
        grid_spec=pltpu.PrefetchScalarGridSpec(
            num_scalar_prefetch=1,
            grid=(1,),
            in_specs=[
                pl.BlockSpec((slots, inner), lambda n, w: (0, 0)),
                pl.BlockSpec((inner, columns), lambda n, w: (0, w[0])),
            ],
            out_specs=pl.BlockSpec((slots, columns), lambda n, w: (0, 0)),
        ),
        cost_estimate=pl.CostEstimate(
            flops=2 * slots * inner * columns,
            bytes_accessed=2 * (slots * inner + inner * columns + slots * columns),
            transcendentals=0,
        ),
        compiler_params=params(),
        name="project",
    )(where, attn, weight)


def cost(blocks, bytes_accessed):
    pairs = blocks * 1280 * 512
    return pl.CostEstimate(
        flops=4 * pairs * HD, bytes_accessed=bytes_accessed, transcendentals=pairs
    )


def shards(
    suffix_query,
    suffix_key,
    suffix_value,
    prefix_key,
    prefix_value,
    residual,
    out_weight,
    norm_gain,
    lengths,
    request_slot,
    prefix_owner,
    request_group,
):
    slots = suffix_query.shape[0]
    heads = suffix_query.shape[1] // HD
    devices = lax.axis_size("req")
    planes = devices // PLANE
    place = lax.axis_index("req")
    tensor = lax.axis_index("tp")
    ways = lax.axis_size("tp")
    per_group = devices // GROUPS
    block = prefix_key.shape[1]
    part = block // 2
    prefix_length = block * per_group
    bf16 = jnp.bfloat16
    f32 = jnp.float32

    def beside(k):
        return [(i, i ^ k) for i in range(devices)]

    up_pairs = [(i, (i + PLANE) % devices) for i in range(devices)]
    down_pairs = [(i, (i - PLANE) % devices) for i in range(devices)]

    core = place % 2
    both = jnp.concatenate([prefix_key, prefix_value], axis=0)
    mine = lax.dynamic_slice_in_dim(both, core * part, part, 1)
    theirs = lax.dynamic_slice_in_dim(both, (1 - core) * part, part, 1)
    lanes = [mine, lax.ppermute(theirs, "req", beside(1))]
    queries = [lax.ppermute(suffix_query, "req", beside(k)) for k in range(1, PLANE)]

    entries = {(0, 0): lanes[0], (0, 1): lanes[1]}
    half_way = planes // 2
    for lane in range(2):
        moving_up = lanes[lane]
        moving_down = lanes[lane]
        for step in range(1, half_way):
            moving_up = lax.ppermute(moving_up, "req", up_pairs)
            moving_down = lax.ppermute(moving_down, "req", down_pairs)
            entries[(-step, lane)] = moving_up
            entries[(step, lane)] = moving_down
        if lane == 0:
            entries[(-half_way, 0)] = lax.ppermute(moving_up, "req", up_pairs)
        else:
            entries[(half_way, 1)] = lax.ppermute(moving_down, "req", down_pairs)

    batches = [
        [(0, 0), (0, 1), (-1, 0), (1, 0), (-1, 1), (1, 1)],
        [(-2, 0), (2, 0), (-2, 1), (2, 1)],
        [(-3, 0), (3, 0), (-3, 1), (3, 1)],
        [(-half_way, 0), (half_way, 1)],
    ]
    order = [key for batch in batches for key in batch]

    numbers = jnp.arange(devices, dtype=jnp.int32)
    owner_match = prefix_owner[None, :] == numbers[:, None]
    holder_group = jnp.sum(jnp.where(owner_match, numbers[None, :], 0), axis=1) // per_group
    slot_match = request_slot[:, None] == numbers[None, :]
    asker_group = jnp.sum(jnp.where(slot_match, request_group[:, 0][None, :], 0), axis=1)
    asker_length = jnp.sum(jnp.where(slot_match, lengths[None, :], 0), axis=1)
    nearby = place ^ jnp.arange(PLANE, dtype=jnp.int32)
    near = nearby[:, None] == numbers[None, :]
    near_group = jnp.sum(jnp.where(near, asker_group[None, :], 0), axis=1)
    near_length = jnp.sum(jnp.where(near, asker_length[None, :], 0), axis=1)
    shift = jnp.array([key[0] for key in order], jnp.int32)
    twist = jnp.array([key[1] for key in order], jnp.int32)
    source = ((place // PLANE + shift) % planes) * PLANE + ((place % PLANE) ^ twist)
    from_there = source[:, None] == numbers[None, :]
    source_group = jnp.sum(jnp.where(from_there, holder_group[None, :], 0), axis=1)
    match = (source_group[:, None] == near_group[None, :]).astype(jnp.int32)
    tiles = (near_length + TILE - 1) // TILE
    meta = jnp.concatenate([near_length, tiles, match.reshape(-1)])

    half_dim = HD // 2
    positions = (prefix_length + jnp.arange(slots)).astype(f32)
    frequency = THETA ** (-(jnp.arange(half_dim).astype(f32) * 2.0 / HD))
    angles = positions[:, None] * frequency[None, :]
    cosines = jnp.cos(angles)
    sines = jnp.sin(angles)
    cosines = jnp.concatenate([cosines, cosines], axis=1)
    sines = jnp.concatenate([-sines, sines], axis=1)

    q_own, cache_key, acc_own, ml_own = pl.pallas_call(
        own_kernel,
        out_shape=(
            jax.ShapeDtypeStruct((heads, slots, HD), bf16),
            jax.ShapeDtypeStruct((slots, HD), bf16),
            jax.ShapeDtypeStruct((heads, slots, HD), f32),
            jax.ShapeDtypeStruct((slots, HD), f32),
        ),
        in_specs=[full(SMEM)] + [full()] * 5,
        out_specs=(full(),) * 4,
        cost_estimate=cost(1, 3 << 20),
        compiler_params=params(),
        name="own",
    )(meta, suffix_query, suffix_key, suffix_value, cosines, sines)

    state_shapes = (
        jax.ShapeDtypeStruct((PLANE, heads, slots, HD), f32),
        jax.ShapeDtypeStruct((PLANE, slots, HD), f32),
    )
    base = 0
    parts = [entries[key] for key in batches[0]]
    q_all, acc, ml = pl.pallas_call(
        make_first(base, len(parts)),
        out_shape=(jax.ShapeDtypeStruct((PLANE, heads, slots, HD), bf16),) + state_shapes,
        in_specs=[full(SMEM)] + [full()] * (8 + len(parts)),
        out_specs=(full(),) * 3,
        cost_estimate=cost(len(parts), 8 << 20),
        compiler_params=params(),
        name="first",
    )(meta, q_own, acc_own, ml_own, *queries, cosines, sines, *parts)
    base += len(parts)
    for batch in batches[1:-1]:
        parts = [entries[key] for key in batch]
        acc, ml = pl.pallas_call(
            make_middle(base, len(parts)),
            out_shape=state_shapes,
            in_specs=[full(SMEM)] + [full()] * (3 + len(parts)),
            out_specs=(full(),) * 2,
            cost_estimate=cost(len(parts), 8 << 20),
            compiler_params=params(),
            name="middle",
        )(meta, q_all, acc, ml, *parts)
        base += len(parts)
    parts = [entries[key] for key in batches[-1]]
    packed = heads * slots + 3 * 16 * (slots // HD)
    last = pl.pallas_call(
        make_last(base, len(parts)),
        out_shape=(
            jax.ShapeDtypeStruct((heads, slots, HD), f32),
            jax.ShapeDtypeStruct((slots, HD), f32),
        )
        + (jax.ShapeDtypeStruct((packed, HD), bf16),) * (PLANE - 1),
        in_specs=[full(SMEM)] + [full()] * (3 + len(parts)),
        out_specs=(full(),) * (PLANE + 1),
        scratch_shapes=[
            pltpu.VMEM((PLANE, heads, slots, HD), f32),
            pltpu.VMEM((PLANE, slots, HD), f32),
        ],
        cost_estimate=cost(len(parts), 8 << 20),
        compiler_params=params(),
        name="last",
    )(meta, q_all, acc, ml, *parts)
    acc_own, ml_own = last[:2]
    returned = [
        lax.ppermute(out, "req", beside(k)) for k, out in zip(range(1, PLANE), last[2:])
    ]
    attn = pl.pallas_call(
        combine_kernel,
        out_shape=jax.ShapeDtypeStruct((slots, heads * HD), bf16),
        in_specs=[full(SMEM)] + [full()] * 5,
        out_specs=full(),
        cost_estimate=cost(1, 3 << 20),
        compiler_params=params(),
        name="combine",
    )(meta, acc_own, ml_own, *returned)

    width = residual.shape[1]
    columns = width // ways
    shared = None
    sent = []
    for k in list(range(1, ways)) + [0]:
        where = (tensor ^ k).astype(jnp.int32).reshape(1)
        piece = project(where, attn, out_weight, columns, bf16 if k else f32)
        if k:
            sent.append(lax.ppermute(piece, "tp", [(i, i ^ k) for i in range(ways)]))
        else:
            shared = piece
    for piece in sent:
        shared = shared + piece.astype(f32)
    own_residual = lax.dynamic_slice_in_dim(residual, tensor * columns, columns, 1)
    hidden = (own_residual.astype(f32) + shared).astype(bf16)
    widened = hidden.astype(f32)
    squares = jnp.sum(widened * widened, axis=1).reshape(slots // HD, HD)
    squares = jnp.pad(squares, ((0, 8 - slots // HD), (0, 0)))
    spread = lax.all_to_all(jnp.broadcast_to(squares[None], (ways, 8, HD)), "tp", 0, 0)
    row_squares = jnp.sum(spread, axis=0)[: slots // HD].reshape(slots)
    scale_rows = lax.rsqrt(row_squares / width + EPSILON)
    normed = (widened * scale_rows[:, None] * norm_gain.astype(f32)[None, :]).astype(bf16)
    return (hidden, normed, cache_key)


def solution(mesh):
    return jax.shard_map(
        shards,
        mesh=mesh,
        in_specs=(
            P("req", "tp"),
            P("req", "tp"),
            P("req", "tp"),
            P("req", None, "tp"),
            P("req", None, "tp"),
            P("req", None),
            P("tp", None),
            P("tp"),
            P(),
            P(),
            P(),
            P(),
        ),
        out_specs=(P("req", "tp"), P("req", "tp"), P("req", "tp")),
        check_vma=False,
    )
```

```python
import jax
import jax.numpy as jnp
from jax import lax
from jax.experimental import pallas as pl
from jax.experimental.pallas import tpu as pltpu
from jax.sharding import PartitionSpec as P

HD = 128
GROUPS = 4
PLANE = 4
TILE = 128
THETA = 1000000.0
NEGATIVE = -1e30
EPSILON = 1e-06
LOG2E = 1.4426950408889634


SMEM = pltpu.SMEM
VMEM = pltpu.VMEM


def full(space=VMEM):
    return pl.BlockSpec(memory_space=space)


def params(limit=40):
    return pltpu.CompilerParams(vmem_limit_bytes=limit * 1024 * 1024)


RATE = HD ** (-0.5) * LOG2E
NT = (((1,), (1,)), ((), ()))


def turn(x, cosines, sines):
    return x * cosines + pltpu.roll(x, HD // 2, 1) * sines


def turn_tiles(q_in, q_ref, at, cosines, sines):
    for j in range(q_in.shape[0] // TILE):
        rows = slice(j * TILE, (j + 1) * TILE)
        for h in range(q_ref.shape[1]):
            x = q_in[rows, h * HD : (h + 1) * HD].astype(jnp.float32)
            q_ref[at + j, h] = turn(x, cosines[rows], sines[rows]).astype(jnp.bfloat16)


def own_kernel(meta, q_in, k_in, v_in, cos_in, sin_in, q_out, key_out, acc_ref, max_ref, sum_ref):
    tiles, heads = q_out.shape[:2]
    slots = k_in.shape[0]
    length = meta[0]
    cosines = cos_in[...]
    sines = sin_in[...]
    turn_tiles(q_in, q_out, 0, cosines, sines)
    turned = turn(k_in[...].astype(jnp.float32), cosines, sines)
    place = lax.broadcasted_iota(jnp.int32, turned.shape, 0)
    key_out[...] = jnp.where(place < length, turned, 0.0).astype(jnp.bfloat16)
    max_ref[...] = jnp.zeros_like(max_ref)
    sum_ref[...] = jnp.ones_like(sum_ref)
    k = key_out[...]
    v = v_in[...].T
    u = lax.broadcasted_iota(jnp.int32, (slots, TILE), 0)
    t = lax.broadcasted_iota(jnp.int32, (slots, TILE), 1)
    for j in range(tiles):
        visible = (u <= t + j * TILE) & (u < length)
        for h in range(heads):
            scores = lax.dot_general(k, q_out[j, h], NT, preferred_element_type=jnp.float32)
            scores = jnp.where(visible, scores, NEGATIVE)
            top = jnp.max(scores, axis=0, keepdims=True)
            weights = jnp.exp2((scores - top) * RATE)
            max_ref[j, h : h + 1] = top
            sum_ref[j, h : h + 1] = jnp.sum(weights, axis=0, keepdims=True)
            acc_ref[j, h] = jnp.dot(v, weights.astype(jnp.bfloat16), preferred_element_type=jnp.float32)


def visit(meta, base, count, q_ref, kv_ref, vt_ref, s_ref, p_ref, top_ref, keep_ref, acc_ref, max_ref, sum_ref, items):
    heads = q_ref.shape[1]
    spare = q_ref.shape[0] - 1
    tiles = spare // PLANE
    part = kv_ref.shape[2]
    for e in range(count):
        vt_ref[e, :HD] = kv_ref[e, 1].T
        vt_ref[e, HD:] = jnp.ones((16, part), jnp.bfloat16)
    n = jnp.int32(0)
    for e in range(count):
        for i in range(PLANE):
            for j in range(tiles):
                live = (meta[2 * PLANE + (base + e) * PLANE + i] == 1) & (j < meta[PLANE + i])

                @pl.when(live)
                def _(n=n, e=e, i=i, j=j):
                    items[n, 0] = e
                    items[n, 1] = i * tiles + j

                n = n + live.astype(jnp.int32)
    for x in range(4):
        items[n + x, 0] = 0
        items[n + x, 1] = spare

    def score(step, slot):
        k = kv_ref[items[step, 0], 0]
        at = items[step, 1]
        for h in range(heads):
            scores = lax.dot_general(k, q_ref[at, h], NT, preferred_element_type=jnp.float32)
            s_ref[slot, h] = scores
            top_ref[slot, h : h + 1] = jnp.max(scores, axis=0, keepdims=True)

    def weigh(step, slot):
        at = items[step, 1]
        old = max_ref[at]
        new = jnp.maximum(old, top_ref[slot])
        max_ref[at] = new
        keep_ref[slot] = jnp.exp2((old - new) * RATE)
        for h in range(heads):
            p_ref[slot, h] = jnp.exp2((s_ref[slot, h] - new[h : h + 1]) * RATE).astype(jnp.bfloat16)

    def gather(step, slot):
        v = vt_ref[items[step, 0]]
        at = items[step, 1]
        keep = keep_ref[slot]
        for h in range(heads):
            mixed = jnp.dot(v, p_ref[slot, h], preferred_element_type=jnp.float32)
            acc_ref[at, h] = acc_ref[at, h] * keep[h : h + 1] + mixed[:HD]
            sum_ref[at, h : h + 1] = sum_ref[at, h : h + 1] * keep[h : h + 1] + mixed[HD : HD + 1]

    @pl.when(n > 0)
    def _():
        score(0, 0)
        score(1, 1)
        weigh(0, 0)

        def body(t, carry):
            for x in range(2):
                step = 2 * t + x
                score_slot = x
                gather(step, x)
                weigh(step + 1, 1 - x)
                score(step + 2, score_slot)
            return carry

        lax.fori_loop(0, (n + 1) // 2, body, 0)


def fetch(pairs, sems):
    copies = [
        pltpu.make_async_copy(source, target, sems.at[n])
        for n, (source, target) in enumerate(pairs)
    ]
    for copy in copies:
        copy.start()
    return copies


def make_first(base, count):
    def kernel(meta, q_own, acc_own, max_own, sum_own, q1, q2, q3, cos_in, sin_in, *rest):
        kv_in = rest[:count]
        q_ref, acc_ref, max_ref, sum_ref, sems, kv_ref, vt_ref, s_ref, p_ref, top_ref, keep_ref, items = rest[count:]
        copies = fetch([(kv, kv_ref.at[e]) for e, kv in enumerate(kv_in)], sems)
        tiles = q_own.shape[0]
        acc_ref[tiles:] = jnp.zeros_like(acc_ref[tiles:])
        max_ref[tiles:] = jnp.full_like(max_ref[tiles:], NEGATIVE)
        sum_ref[tiles:] = jnp.zeros_like(sum_ref[tiles:])
        top_ref[...] = jnp.zeros_like(top_ref)
        q_ref[:tiles] = q_own[...]
        q_ref[PLANE * tiles] = q_own[0]
        acc_ref[:tiles] = acc_own[...]
        max_ref[:tiles] = max_own[...]
        sum_ref[:tiles] = sum_own[...]
        cosines = cos_in[...]
        sines = sin_in[...]
        for i, q_in in enumerate((q1, q2, q3)):
            turn_tiles(q_in, q_ref, (i + 1) * tiles, cosines, sines)
        for copy in copies:
            copy.wait()
        visit(meta, base, count, q_ref, kv_ref, vt_ref, s_ref, p_ref, top_ref, keep_ref, acc_ref, max_ref, sum_ref, items)

    return kernel


def make_middle(base, count):
    def kernel(meta, q_ref, acc_in, max_in, sum_in, *rest):
        kv_in = rest[:count]
        acc_ref, max_ref, sum_ref, sems, kv_ref, vt_ref, s_ref, p_ref, top_ref, keep_ref, items = rest[count:]
        pairs = [(kv, kv_ref.at[e]) for e, kv in enumerate(kv_in)]
        copies = fetch(pairs + [(acc_in, acc_ref)], sems)
        max_ref[...] = max_in[...]
        sum_ref[...] = sum_in[...]
        top_ref[...] = jnp.zeros_like(top_ref)
        for copy in copies:
            copy.wait()
        visit(meta, base, count, q_ref, kv_ref, vt_ref, s_ref, p_ref, top_ref, keep_ref, acc_ref, max_ref, sum_ref, items)

    return kernel


def split(x):
    high = x.astype(jnp.bfloat16)
    left = x - high.astype(jnp.float32)
    middle = left.astype(jnp.bfloat16)
    low = (left - middle.astype(jnp.float32)).astype(jnp.bfloat16)
    return high, middle, low


def make_last(base, count):
    def kernel(meta, q_ref, acc_in, max_in, sum_in, *rest):
        kv_in = rest[:count]
        acc_own, max_own, sum_own, o1, o2, o3 = rest[count : count + 6]
        acc_ref, max_ref, sum_ref, sems, kv_ref, vt_ref, s_ref, p_ref, top_ref, keep_ref, items = rest[count + 6 :]
        pairs = [(kv, kv_ref.at[e]) for e, kv in enumerate(kv_in)]
        copies = fetch(pairs + [(acc_in, acc_ref)], sems)
        max_ref[...] = max_in[...]
        sum_ref[...] = sum_in[...]
        top_ref[...] = jnp.zeros_like(top_ref)
        for copy in copies:
            copy.wait()
        visit(meta, base, count, q_ref, kv_ref, vt_ref, s_ref, p_ref, top_ref, keep_ref, acc_ref, max_ref, sum_ref, items)
        tiles, heads = acc_own.shape[:2]
        acc_own[...] = acc_ref[:tiles]
        max_own[...] = max_ref[:tiles]
        sum_own[...] = sum_ref[:tiles]
        for i, out in enumerate((o1, o2, o3)):
            first = (i + 1) * tiles
            for j in range(tiles):
                total = sum_ref[first + j]
                inverse = jnp.where(total > 0, 1.0 / jnp.where(total > 0, total, 1.0), 0.0)
                for h in range(heads):
                    at = (j * heads + h) * HD
                    out[at : at + HD] = (acc_ref[first + j, h] * inverse[h : h + 1]).astype(jnp.bfloat16)
            at = tiles * heads * HD
            for stats in (max_ref, sum_ref):
                flat = jnp.concatenate([stats[first + j] for j in range(tiles)], axis=0)
                for piece in split(flat):
                    out[at : at + 8 * tiles] = piece
                    at = at + 8 * tiles

    return kernel


def combine_kernel(meta, acc_own, max_own, sum_own, o1, o2, o3, attn_ref):
    tiles, heads = acc_own.shape[:2]
    rows = 8 * tiles
    maxima = [jnp.concatenate([max_own[j] for j in range(tiles)], axis=0)]
    sums = [jnp.concatenate([sum_own[j] for j in range(tiles)], axis=0)]
    for part in (o1, o2, o3):
        at = tiles * heads * HD
        found = []
        for _ in range(2):
            pieces = [
                part[at + n * rows : at + (n + 1) * rows].astype(jnp.float32) for n in range(3)
            ]
            found.append(pieces[0] + pieces[1] + pieces[2])
            at = at + 3 * rows
        maxima.append(found[0])
        sums.append(found[1])
    top = jnp.maximum(jnp.maximum(maxima[0], maxima[1]), jnp.maximum(maxima[2], maxima[3]))
    factor = [jnp.exp2((m - top) * RATE) for m in maxima]
    mass = [f * s for f, s in zip(factor, sums)]
    inverse = 1.0 / (mass[0] + mass[1] + mass[2] + mass[3])
    lane = lax.broadcasted_iota(jnp.int32, (HD, TILE), 1)
    shares = [factor[0] * inverse] + [m * inverse for m in mass[1:]]
    for j in range(tiles):
        live = lane + j * TILE < meta[0]
        for h in range(heads):
            r = j * 8 + h
            value = acc_own[j, h] * shares[0][r : r + 1]
            for w, part in zip(shares[1:], (o1, o2, o3)):
                at = (j * heads + h) * HD
                value = value + w[r : r + 1] * part[at : at + HD].astype(jnp.float32)
            value = jnp.transpose(jnp.where(live, value, 0.0))
            attn_ref[j * TILE : (j + 1) * TILE, h * HD : (h + 1) * HD] = value.astype(jnp.bfloat16)


def project_kernel(where, attn_ref, weight_ref, out_ref):
    del where
    out_ref[...] = jnp.dot(
        attn_ref[...], weight_ref[...], preferred_element_type=jnp.float32
    ).astype(out_ref.dtype)


def project(where, attn, weight, columns, dtype):
    slots, inner = attn.shape
    return pl.pallas_call(
        project_kernel,
        out_shape=jax.ShapeDtypeStruct((slots, columns), dtype),
        grid_spec=pltpu.PrefetchScalarGridSpec(
            num_scalar_prefetch=1,
            grid=(1,),
            in_specs=[
                pl.BlockSpec((slots, inner), lambda n, w: (0, 0)),
                pl.BlockSpec((inner, columns), lambda n, w: (0, w[0])),
            ],
            out_specs=pl.BlockSpec((slots, columns), lambda n, w: (0, 0)),
        ),
        cost_estimate=pl.CostEstimate(
            flops=2 * slots * inner * columns,
            bytes_accessed=2 * (slots * inner + inner * columns + slots * columns),
            transcendentals=0,
        ),
        compiler_params=params(60),
        name="project",
    )(where, attn, weight)


def cost(blocks, bytes_accessed):
    pairs = blocks * 1280 * 512
    return pl.CostEstimate(
        flops=4 * pairs * HD, bytes_accessed=bytes_accessed, transcendentals=pairs
    )


def shards(
    suffix_query,
    suffix_key,
    suffix_value,
    prefix_key,
    prefix_value,
    residual,
    out_weight,
    norm_gain,
    lengths,
    request_slot,
    prefix_owner,
    request_group,
):
    slots = suffix_query.shape[0]
    heads = suffix_query.shape[1] // HD
    devices = lax.axis_size("req")
    planes = devices // PLANE
    place = lax.axis_index("req")
    tensor = lax.axis_index("tp")
    ways = lax.axis_size("tp")
    per_group = devices // GROUPS
    block = prefix_key.shape[1]
    part = block // 2
    prefix_length = block * per_group
    bf16 = jnp.bfloat16
    f32 = jnp.float32

    def beside(k):
        return [(i, i ^ k) for i in range(devices)]

    up_pairs = [(i, (i + PLANE) % devices) for i in range(devices)]
    down_pairs = [(i, (i - PLANE) % devices) for i in range(devices)]

    core = place % 2
    both = jnp.concatenate([prefix_key, prefix_value], axis=0)
    mine = lax.dynamic_slice_in_dim(both, core * part, part, 1)
    theirs = lax.dynamic_slice_in_dim(both, (1 - core) * part, part, 1)
    lanes = [mine, lax.ppermute(theirs, "req", beside(1))]
    queries = [lax.ppermute(suffix_query, "req", beside(k)) for k in range(1, PLANE)]

    entries = {(0, 0): lanes[0], (0, 1): lanes[1]}
    half_way = planes // 2
    for lane in range(2):
        moving_up = lanes[lane]
        moving_down = lanes[lane]
        for step in range(1, half_way):
            moving_up = lax.ppermute(moving_up, "req", up_pairs)
            moving_down = lax.ppermute(moving_down, "req", down_pairs)
            entries[(-step, lane)] = moving_up
            entries[(step, lane)] = moving_down
        if lane == 0:
            entries[(-half_way, 0)] = lax.ppermute(moving_up, "req", up_pairs)
        else:
            entries[(half_way, 1)] = lax.ppermute(moving_down, "req", down_pairs)

    batches = [
        [(0, 0), (0, 1), (-1, 0), (1, 0), (-1, 1), (1, 1)],
        [(-2, 0), (2, 0), (-2, 1), (2, 1)],
        [(-3, 0), (3, 0), (-3, 1), (3, 1)],
        [(-half_way, 0), (half_way, 1)],
    ]
    order = [key for batch in batches for key in batch]

    numbers = jnp.arange(devices, dtype=jnp.int32)
    owner_match = prefix_owner[None, :] == numbers[:, None]
    holder_group = jnp.sum(jnp.where(owner_match, numbers[None, :], 0), axis=1) // per_group
    slot_match = request_slot[:, None] == numbers[None, :]
    asker_group = jnp.sum(jnp.where(slot_match, request_group[:, 0][None, :], 0), axis=1)
    asker_length = jnp.sum(jnp.where(slot_match, lengths[None, :], 0), axis=1)
    nearby = place ^ jnp.arange(PLANE, dtype=jnp.int32)
    near = nearby[:, None] == numbers[None, :]
    near_group = jnp.sum(jnp.where(near, asker_group[None, :], 0), axis=1)
    near_length = jnp.sum(jnp.where(near, asker_length[None, :], 0), axis=1)
    shift = jnp.array([key[0] for key in order], jnp.int32)
    twist = jnp.array([key[1] for key in order], jnp.int32)
    source = ((place // PLANE + shift) % planes) * PLANE + ((place % PLANE) ^ twist)
    from_there = source[:, None] == numbers[None, :]
    source_group = jnp.sum(jnp.where(from_there, holder_group[None, :], 0), axis=1)
    match = (source_group[:, None] == near_group[None, :]).astype(jnp.int32)
    tiles = (near_length + TILE - 1) // TILE
    meta = jnp.concatenate([near_length, tiles, match.reshape(-1)])

    half_dim = HD // 2
    positions = (prefix_length + jnp.arange(slots)).astype(f32)
    frequency = THETA ** (-(jnp.arange(half_dim).astype(f32) * 2.0 / HD))
    angles = positions[:, None] * frequency[None, :]
    cosines = jnp.cos(angles)
    sines = jnp.sin(angles)
    cosines = jnp.concatenate([cosines, cosines], axis=1)
    sines = jnp.concatenate([-sines, sines], axis=1)

    tiles_each = slots // TILE
    shape = jax.ShapeDtypeStruct
    q_own, cache_key, acc_own, max_own, sum_own = pl.pallas_call(
        own_kernel,
        out_shape=(
            shape((tiles_each, heads, TILE, HD), bf16),
            shape((slots, HD), bf16),
            shape((tiles_each, heads, HD, TILE), f32),
            shape((tiles_each, 8, TILE), f32),
            shape((tiles_each, 8, TILE), f32),
        ),
        in_specs=[full(SMEM)] + [full()] * 5,
        out_specs=(full(),) * 5,
        cost_estimate=cost(1, 3 << 20),
        compiler_params=params(),
        name="own",
    )(meta, suffix_query, suffix_key, suffix_value, cosines, sines)

    every = PLANE * tiles_each + 1
    state_shapes = (
        shape((every, heads, HD, TILE), f32),
        shape((every, 8, TILE), f32),
        shape((every, 8, TILE), f32),
    )

    def work(count):
        return [
            pltpu.SemaphoreType.DMA((count + 1,)),
            pltpu.VMEM((count, 2, part, HD), bf16),
            pltpu.VMEM((count, HD + 16, part), bf16),
            pltpu.VMEM((2, heads, part, TILE), f32),
            pltpu.VMEM((2, heads, part, TILE), bf16),
            pltpu.VMEM((2, 8, TILE), f32),
            pltpu.VMEM((2, 8, TILE), f32),
            pltpu.SMEM((count * PLANE * tiles_each + 4, 2), jnp.int32),
        ]

    base = 0
    parts = [entries[key] for key in batches[0]]
    q_all, *state = pl.pallas_call(
        make_first(base, len(parts)),
        out_shape=(shape((every, heads, TILE, HD), bf16),) + state_shapes,
        in_specs=[full(SMEM)] + [full()] * 9 + [full(pl.ANY)] * len(parts),
        out_specs=(full(),) * 4,
        scratch_shapes=work(len(parts)),
        cost_estimate=cost(len(parts), 8 << 20),
        compiler_params=params(),
        name="first",
    )(meta, q_own, acc_own, max_own, sum_own, *queries, cosines, sines, *parts)
    base += len(parts)
    for batch in batches[1:-1]:
        parts = [entries[key] for key in batch]
        state = pl.pallas_call(
            make_middle(base, len(parts)),
            out_shape=state_shapes,
            in_specs=[full(SMEM), full(), full(pl.ANY), full(), full()] + [full(pl.ANY)] * len(parts),
            out_specs=(full(),) * 3,
            scratch_shapes=work(len(parts)),
            cost_estimate=cost(len(parts), 8 << 20),
            compiler_params=params(),
            name="middle",
        )(meta, q_all, *state, *parts)
        base += len(parts)
    parts = [entries[key] for key in batches[-1]]
    packed = heads * slots + 2 * 3 * 8 * tiles_each
    last = pl.pallas_call(
        make_last(base, len(parts)),
        out_shape=(
            shape((tiles_each, heads, HD, TILE), f32),
            shape((tiles_each, 8, TILE), f32),
            shape((tiles_each, 8, TILE), f32),
        )
        + (shape((packed, HD), bf16),) * (PLANE - 1),
        in_specs=[full(SMEM), full(), full(pl.ANY), full(), full()] + [full(pl.ANY)] * len(parts),
        out_specs=(full(),) * (PLANE + 2),
        scratch_shapes=[
            pltpu.VMEM((every, heads, HD, TILE), f32),
            pltpu.VMEM((every, 8, TILE), f32),
            pltpu.VMEM((every, 8, TILE), f32),
        ]
        + work(len(parts)),
        cost_estimate=cost(len(parts), 8 << 20),
        compiler_params=params(),
        name="last",
    )(meta, q_all, *state, *parts)
    returned = [
        lax.ppermute(out, "req", beside(k)) for k, out in zip(range(1, PLANE), last[3:])
    ]
    attn = pl.pallas_call(
        combine_kernel,
        out_shape=shape((slots, heads * HD), bf16),
        in_specs=[full(SMEM)] + [full()] * 6,
        out_specs=full(),
        cost_estimate=cost(1, 3 << 20),
        compiler_params=params(),
        name="combine",
    )(meta, *last[:3], *returned)

    width = residual.shape[1]
    columns = width // ways
    shared = None
    sent = []
    for k in list(range(1, ways)) + [0]:
        where = (tensor ^ k).astype(jnp.int32).reshape(1)
        piece = project(where, attn, out_weight, columns, bf16 if k else f32)
        if k:
            sent.append(lax.ppermute(piece, "tp", [(i, i ^ k) for i in range(ways)]))
        else:
            shared = piece
    for piece in sent:
        shared = shared + piece.astype(f32)
    own_residual = lax.dynamic_slice_in_dim(residual, tensor * columns, columns, 1)
    hidden = (own_residual.astype(f32) + shared).astype(bf16)
    widened = hidden.astype(f32)
    squares = jnp.sum(widened * widened, axis=1).reshape(slots // HD, HD)
    squares = jnp.pad(squares, ((0, 8 - slots // HD), (0, 0)))
    spread = lax.all_to_all(jnp.broadcast_to(squares[None], (ways, 8, HD)), "tp", 0, 0)
    row_squares = jnp.sum(spread, axis=0)[: slots // HD].reshape(slots)
    scale_rows = lax.rsqrt(row_squares / width + EPSILON)
    normed = (widened * scale_rows[:, None] * norm_gain.astype(f32)[None, :]).astype(bf16)
    return (hidden, normed, cache_key)


def solution(mesh):
    return jax.shard_map(
        shards,
        mesh=mesh,
        in_specs=(
            P("req", "tp"),
            P("req", "tp"),
            P("req", "tp"),
            P("req", None, "tp"),
            P("req", None, "tp"),
            P("req", None),
            P("tp", None),
            P("tp"),
            P(),
            P(),
            P(),
            P(),
        ),
        out_specs=(P("req", "tp"), P("req", "tp"), P("req", "tp")),
        check_vma=False,
    )
```

```python
import jax
import jax.numpy as jnp
from jax import lax
from jax.experimental import pallas as pl
from jax.experimental.pallas import tpu as pltpu
from jax.sharding import PartitionSpec as P


HD = 128
GROUPS = 4
PLANE = 4
TILE = 128
THETA = 1000000.0
NEGATIVE = -1e30
EPSILON = 1e-06
LOG2E = 1.4426950408889634


SMEM = pltpu.SMEM
VMEM = pltpu.VMEM


def full(space=VMEM):
    return pl.BlockSpec(memory_space=space)


def params(limit=40):
    return pltpu.CompilerParams(vmem_limit_bytes=limit * 1024 * 1024)


RATE = HD ** (-0.5) * LOG2E
NT = (((1,), (1,)), ((), ()))


def turn(x, cosines, sines):
    return x * cosines + pltpu.roll(x, HD // 2, 1) * sines


def turn_tiles(q_in, q_ref, at, cosines, sines):
    for j in range(q_in.shape[0] // TILE):
        rows = slice(j * TILE, (j + 1) * TILE)
        for h in range(q_ref.shape[1]):
            x = q_in[rows, h * HD : (h + 1) * HD].astype(jnp.float32)
            q_ref[at + j, h] = turn(x, cosines[rows], sines[rows]).astype(jnp.bfloat16)


def own_kernel(meta, q_in, k_in, v_in, cos_in, sin_in, q_out, key_out, acc_ref, max_ref, sum_ref):
    tiles, heads = q_out.shape[:2]
    slots = k_in.shape[0]
    length = meta[0]
    cosines = cos_in[...]
    sines = sin_in[...]
    turn_tiles(q_in, q_out, 0, cosines, sines)
    turned = turn(k_in[...].astype(jnp.float32), cosines, sines)
    place = lax.broadcasted_iota(jnp.int32, turned.shape, 0)
    key_out[...] = jnp.where(place < length, turned, 0.0).astype(jnp.bfloat16)
    max_ref[...] = jnp.zeros_like(max_ref)
    sum_ref[...] = jnp.ones_like(sum_ref)
    k = key_out[...]
    v = v_in[...].T
    u = lax.broadcasted_iota(jnp.int32, (slots, TILE), 0)
    t = lax.broadcasted_iota(jnp.int32, (slots, TILE), 1)
    for j in range(tiles):
        visible = (u <= t + j * TILE) & (u < length)
        for h in range(heads):
            scores = lax.dot_general(k, q_out[j, h], NT, preferred_element_type=jnp.float32)
            scores = jnp.where(visible, scores, NEGATIVE)
            top = jnp.max(scores, axis=0, keepdims=True)
            weights = jnp.exp2((scores - top) * RATE)
            max_ref[j, h : h + 1] = top
            sum_ref[j, h : h + 1] = jnp.sum(weights, axis=0, keepdims=True)
            acc_ref[j, h] = jnp.dot(v, weights.astype(jnp.bfloat16), preferred_element_type=jnp.float32)


def visit(meta, base, count, q_ref, kv_ref, vt_ref, s_ref, p_ref, top_ref, keep_ref, acc_ref, max_ref, sum_ref, items):
    heads = q_ref.shape[1]
    spare = q_ref.shape[0] - 1
    tiles = spare // PLANE
    part = kv_ref.shape[2]
    for e in range(count):
        vt_ref[e, :HD] = kv_ref[e, 1].T
        vt_ref[e, HD:] = jnp.ones((16, part), jnp.bfloat16)
    n = jnp.int32(0)
    for e in range(count):
        for i in range(PLANE):
            for j in range(tiles):
                live = (meta[2 * PLANE + (base + e) * PLANE + i] == 1) & (j < meta[PLANE + i])

                @pl.when(live)
                def _(n=n, e=e, i=i, j=j):
                    items[n, 0] = e
                    items[n, 1] = i * tiles + j

                n = n + live.astype(jnp.int32)
    for x in range(4):
        items[n + x, 0] = 0
        items[n + x, 1] = spare

    def score(step, slot):
        k = kv_ref[items[step, 0], 0]
        at = items[step, 1]
        for h in range(heads):
            scores = lax.dot_general(k, q_ref[at, h], NT, preferred_element_type=jnp.float32)
            s_ref[slot, h] = scores
            top_ref[slot, h : h + 1] = jnp.max(scores, axis=0, keepdims=True)

    def weigh(step, slot):
        at = items[step, 1]
        old = max_ref[at]
        new = jnp.maximum(old, top_ref[slot])
        max_ref[at] = new
        keep_ref[slot] = jnp.exp2((old - new) * RATE)
        for h in range(heads):
            p_ref[slot, h] = jnp.exp2((s_ref[slot, h] - new[h : h + 1]) * RATE).astype(jnp.bfloat16)

    def gather(step, slot):
        v = vt_ref[items[step, 0]]
        at = items[step, 1]
        keep = keep_ref[slot]
        for h in range(heads):
            mixed = jnp.dot(v, p_ref[slot, h], preferred_element_type=jnp.float32)
            acc_ref[at, h] = acc_ref[at, h] * keep[h : h + 1] + mixed[:HD]
            sum_ref[at, h : h + 1] = sum_ref[at, h : h + 1] * keep[h : h + 1] + mixed[HD : HD + 1]

    @pl.when(n > 0)
    def _():
        score(0, 0)
        score(1, 1)
        weigh(0, 0)

        def body(t, carry):
            for x in range(2):
                step = 2 * t + x
                score_slot = x
                gather(step, x)
                weigh(step + 1, 1 - x)
                score(step + 2, score_slot)
            return carry

        lax.fori_loop(0, (n + 1) // 2, body, 0)


def fetch(pairs, sems):
    copies = [
        pltpu.make_async_copy(source, target, sems.at[n])
        for n, (source, target) in enumerate(pairs)
    ]
    for copy in copies:
        copy.start()
    return copies


def make_first(base, count):
    def kernel(meta, q_own, acc_own, max_own, sum_own, q1, q2, q3, cos_in, sin_in, *rest):
        kv_in = rest[:count]
        q_ref, acc_ref, max_ref, sum_ref, sems, kv_ref, vt_ref, s_ref, p_ref, top_ref, keep_ref, items = rest[count:]
        copies = fetch([(kv, kv_ref.at[e]) for e, kv in enumerate(kv_in)], sems)
        tiles = q_own.shape[0]
        acc_ref[tiles:] = jnp.zeros_like(acc_ref[tiles:])
        max_ref[tiles:] = jnp.full_like(max_ref[tiles:], NEGATIVE)
        sum_ref[tiles:] = jnp.zeros_like(sum_ref[tiles:])
        top_ref[...] = jnp.zeros_like(top_ref)
        q_ref[:tiles] = q_own[...]
        q_ref[PLANE * tiles] = q_own[0]
        acc_ref[:tiles] = acc_own[...]
        max_ref[:tiles] = max_own[...]
        sum_ref[:tiles] = sum_own[...]
        cosines = cos_in[...]
        sines = sin_in[...]
        for i, q_in in enumerate((q1, q2, q3)):
            turn_tiles(q_in, q_ref, (i + 1) * tiles, cosines, sines)
        for copy in copies:
            copy.wait()
        visit(meta, base, count, q_ref, kv_ref, vt_ref, s_ref, p_ref, top_ref, keep_ref, acc_ref, max_ref, sum_ref, items)

    return kernel


def make_middle(base, count):
    def kernel(meta, q_ref, acc_in, max_in, sum_in, *rest):
        kv_in = rest[:count]
        acc_ref, max_ref, sum_ref, sems, kv_ref, vt_ref, s_ref, p_ref, top_ref, keep_ref, items = rest[count:]
        pairs = [(kv, kv_ref.at[e]) for e, kv in enumerate(kv_in)]
        copies = fetch(pairs + [(acc_in, acc_ref)], sems)
        max_ref[...] = max_in[...]
        sum_ref[...] = sum_in[...]
        top_ref[...] = jnp.zeros_like(top_ref)
        for copy in copies:
            copy.wait()
        visit(meta, base, count, q_ref, kv_ref, vt_ref, s_ref, p_ref, top_ref, keep_ref, acc_ref, max_ref, sum_ref, items)

    return kernel


def split(x):
    high = x.astype(jnp.bfloat16)
    left = x - high.astype(jnp.float32)
    middle = left.astype(jnp.bfloat16)
    low = (left - middle.astype(jnp.float32)).astype(jnp.bfloat16)
    return high, middle, low


def make_last(base, count):
    def kernel(meta, q_ref, acc_in, max_in, sum_in, *rest):
        kv_in = rest[:count]
        acc_own, max_own, sum_own, o1, o2, o3 = rest[count : count + 6]
        acc_ref, max_ref, sum_ref, sems, kv_ref, vt_ref, s_ref, p_ref, top_ref, keep_ref, items = rest[count + 6 :]
        pairs = [(kv, kv_ref.at[e]) for e, kv in enumerate(kv_in)]
        copies = fetch(pairs + [(acc_in, acc_ref)], sems)
        max_ref[...] = max_in[...]
        sum_ref[...] = sum_in[...]
        top_ref[...] = jnp.zeros_like(top_ref)
        for copy in copies:
            copy.wait()
        visit(meta, base, count, q_ref, kv_ref, vt_ref, s_ref, p_ref, top_ref, keep_ref, acc_ref, max_ref, sum_ref, items)
        tiles, heads = acc_own.shape[:2]
        acc_own[...] = acc_ref[:tiles]
        max_own[...] = max_ref[:tiles]
        sum_own[...] = sum_ref[:tiles]
        for i, out in enumerate((o1, o2, o3)):
            first = (i + 1) * tiles
            for j in range(tiles):
                total = sum_ref[first + j]
                inverse = jnp.where(total > 0, 1.0 / jnp.where(total > 0, total, 1.0), 0.0)
                for h in range(heads):
                    at = (j * heads + h) * HD
                    out[at : at + HD] = (acc_ref[first + j, h] * inverse[h : h + 1]).astype(jnp.bfloat16)
            at = tiles * heads * HD
            for stats in (max_ref, sum_ref):
                flat = jnp.concatenate([stats[first + j] for j in range(tiles)], axis=0)
                for piece in split(flat):
                    out[at : at + 8 * tiles] = piece
                    at = at + 8 * tiles

    return kernel


def combine_kernel(meta, where, acc_own, max_own, sum_own, o1, o2, o3, weight_in, *rest):
    ways = (len(rest) - 3)
    outs = rest[:ways]
    attn_ref, weight_ref, sems = rest[ways:]
    columns = weight_ref.shape[2]
    copies = []
    for k in range(ways):
        at = pl.multiple_of((where[0] ^ k) * columns, HD)
        copies.append(
            pltpu.make_async_copy(
                weight_in.at[:, pl.ds(at, columns)], weight_ref.at[k], sems.at[k]
            )
        )
    for copy in copies[1:] + copies[:1]:
        copy.start()
    tiles, heads = acc_own.shape[:2]
    rows = 8 * tiles
    maxima = [jnp.concatenate([max_own[j] for j in range(tiles)], axis=0)]
    sums = [jnp.concatenate([sum_own[j] for j in range(tiles)], axis=0)]
    for part in (o1, o2, o3):
        at = tiles * heads * HD
        found = []
        for _ in range(2):
            pieces = [
                part[at + n * rows : at + (n + 1) * rows].astype(jnp.float32) for n in range(3)
            ]
            found.append(pieces[0] + pieces[1] + pieces[2])
            at = at + 3 * rows
        maxima.append(found[0])
        sums.append(found[1])
    top = jnp.maximum(jnp.maximum(maxima[0], maxima[1]), jnp.maximum(maxima[2], maxima[3]))
    factor = [jnp.exp2((m - top) * RATE) for m in maxima]
    mass = [f * s for f, s in zip(factor, sums)]
    inverse = 1.0 / (mass[0] + mass[1] + mass[2] + mass[3])
    lane = lax.broadcasted_iota(jnp.int32, (HD, TILE), 1)
    shares = [factor[0] * inverse] + [m * inverse for m in mass[1:]]
    for j in range(tiles):
        live = lane + j * TILE < meta[0]
        for h in range(heads):
            r = j * 8 + h
            value = acc_own[j, h] * shares[0][r : r + 1]
            for w, part in zip(shares[1:], (o1, o2, o3)):
                at = (j * heads + h) * HD
                value = value + w[r : r + 1] * part[at : at + HD].astype(jnp.float32)
            value = jnp.transpose(jnp.where(live, value, 0.0))
            attn_ref[j * TILE : (j + 1) * TILE, h * HD : (h + 1) * HD] = value.astype(jnp.bfloat16)
    for k in list(range(1, ways)) + [0]:
        copies[k].wait()
        outs[k][...] = jnp.dot(
            attn_ref[...], weight_ref[k], preferred_element_type=jnp.float32
        ).astype(outs[k].dtype)


def cost(blocks, bytes_accessed):
    pairs = blocks * 1280 * 512
    return pl.CostEstimate(
        flops=4 * pairs * HD, bytes_accessed=bytes_accessed, transcendentals=pairs
    )


def shards(
    suffix_query,
    suffix_key,
    suffix_value,
    prefix_key,
    prefix_value,
    residual,
    out_weight,
    norm_gain,
    lengths,
    request_slot,
    prefix_owner,
    request_group,
):
    slots = suffix_query.shape[0]
    heads = suffix_query.shape[1] // HD
    devices = lax.axis_size("req")
    planes = devices // PLANE
    place = lax.axis_index("req")
    tensor = lax.axis_index("tp")
    ways = lax.axis_size("tp")
    per_group = devices // GROUPS
    block = prefix_key.shape[1]
    part = block // 2
    prefix_length = block * per_group
    bf16 = jnp.bfloat16
    f32 = jnp.float32

    def beside(k):
        return [(i, i ^ k) for i in range(devices)]

    up_pairs = [(i, (i + PLANE) % devices) for i in range(devices)]
    down_pairs = [(i, (i - PLANE) % devices) for i in range(devices)]

    core = place % 2
    both = jnp.concatenate([prefix_key, prefix_value], axis=0)
    mine = lax.dynamic_slice_in_dim(both, core * part, part, 1)
    theirs = lax.dynamic_slice_in_dim(both, (1 - core) * part, part, 1)
    lanes = [mine, lax.ppermute(theirs, "req", beside(1))]
    queries = [lax.ppermute(suffix_query, "req", beside(k)) for k in range(1, PLANE)]

    entries = {(0, 0): lanes[0], (0, 1): lanes[1]}
    half_way = planes // 2
    for lane in range(2):
        moving_up = lanes[lane]
        moving_down = lanes[lane]
        for step in range(1, half_way):
            moving_up = lax.ppermute(moving_up, "req", up_pairs)
            moving_down = lax.ppermute(moving_down, "req", down_pairs)
            entries[(-step, lane)] = moving_up
            entries[(step, lane)] = moving_down
        if lane == 0:
            entries[(-half_way, 0)] = lax.ppermute(moving_up, "req", up_pairs)
        else:
            entries[(half_way, 1)] = lax.ppermute(moving_down, "req", down_pairs)

    batches = [
        [(0, 0), (0, 1), (-1, 0), (1, 0), (-1, 1), (1, 1)],
        [(-2, 0), (2, 0), (-2, 1), (2, 1)],
        [(-3, 0), (3, 0), (-3, 1), (3, 1)],
        [(-half_way, 0), (half_way, 1)],
    ]
    order = [key for batch in batches for key in batch]

    numbers = jnp.arange(devices, dtype=jnp.int32)
    owner_match = prefix_owner[None, :] == numbers[:, None]
    holder_group = jnp.sum(jnp.where(owner_match, numbers[None, :], 0), axis=1) // per_group
    slot_match = request_slot[:, None] == numbers[None, :]
    asker_group = jnp.sum(jnp.where(slot_match, request_group[:, 0][None, :], 0), axis=1)
    asker_length = jnp.sum(jnp.where(slot_match, lengths[None, :], 0), axis=1)
    nearby = place ^ jnp.arange(PLANE, dtype=jnp.int32)
    near = nearby[:, None] == numbers[None, :]
    near_group = jnp.sum(jnp.where(near, asker_group[None, :], 0), axis=1)
    near_length = jnp.sum(jnp.where(near, asker_length[None, :], 0), axis=1)
    shift = jnp.array([key[0] for key in order], jnp.int32)
    twist = jnp.array([key[1] for key in order], jnp.int32)
    source = ((place // PLANE + shift) % planes) * PLANE + ((place % PLANE) ^ twist)
    from_there = source[:, None] == numbers[None, :]
    source_group = jnp.sum(jnp.where(from_there, holder_group[None, :], 0), axis=1)
    match = (source_group[:, None] == near_group[None, :]).astype(jnp.int32)
    tiles = (near_length + TILE - 1) // TILE
    meta = jnp.concatenate([near_length, tiles, match.reshape(-1)])

    half_dim = HD // 2
    positions = (prefix_length + jnp.arange(slots)).astype(f32)
    frequency = THETA ** (-(jnp.arange(half_dim).astype(f32) * 2.0 / HD))
    angles = positions[:, None] * frequency[None, :]
    cosines = jnp.cos(angles)
    sines = jnp.sin(angles)
    cosines = jnp.concatenate([cosines, cosines], axis=1)
    sines = jnp.concatenate([-sines, sines], axis=1)

    tiles_each = slots // TILE
    shape = jax.ShapeDtypeStruct
    q_own, cache_key, acc_own, max_own, sum_own = pl.pallas_call(
        own_kernel,
        out_shape=(
            shape((tiles_each, heads, TILE, HD), bf16),
            shape((slots, HD), bf16),
            shape((tiles_each, heads, HD, TILE), f32),
            shape((tiles_each, 8, TILE), f32),
            shape((tiles_each, 8, TILE), f32),
        ),
        in_specs=[full(SMEM)] + [full()] * 5,
        out_specs=(full(),) * 5,
        cost_estimate=cost(1, 3 << 20),
        compiler_params=params(),
        name="own",
    )(meta, suffix_query, suffix_key, suffix_value, cosines, sines)

    every = PLANE * tiles_each + 1
    state_shapes = (
        shape((every, heads, HD, TILE), f32),
        shape((every, 8, TILE), f32),
        shape((every, 8, TILE), f32),
    )

    def work(count):
        return [
            pltpu.SemaphoreType.DMA((count + 1,)),
            pltpu.VMEM((count, 2, part, HD), bf16),
            pltpu.VMEM((count, HD + 16, part), bf16),
            pltpu.VMEM((2, heads, part, TILE), f32),
            pltpu.VMEM((2, heads, part, TILE), bf16),
            pltpu.VMEM((2, 8, TILE), f32),
            pltpu.VMEM((2, 8, TILE), f32),
            pltpu.SMEM((count * PLANE * tiles_each + 4, 2), jnp.int32),
        ]

    base = 0
    parts = [entries[key] for key in batches[0]]
    q_all, *state = pl.pallas_call(
        make_first(base, len(parts)),
        out_shape=(shape((every, heads, TILE, HD), bf16),) + state_shapes,
        in_specs=[full(SMEM)] + [full()] * 9 + [full(pl.ANY)] * len(parts),
        out_specs=(full(),) * 4,
        scratch_shapes=work(len(parts)),
        cost_estimate=cost(len(parts), 8 << 20),
        compiler_params=params(),
        name="first",
    )(meta, q_own, acc_own, max_own, sum_own, *queries, cosines, sines, *parts)
    base += len(parts)
    for batch in batches[1:-1]:
        parts = [entries[key] for key in batch]
        state = pl.pallas_call(
            make_middle(base, len(parts)),
            out_shape=state_shapes,
            in_specs=[full(SMEM), full(), full(pl.ANY), full(), full()] + [full(pl.ANY)] * len(parts),
            out_specs=(full(),) * 3,
            scratch_shapes=work(len(parts)),
            cost_estimate=cost(len(parts), 8 << 20),
            compiler_params=params(),
            name="middle",
        )(meta, q_all, *state, *parts)
        base += len(parts)
    parts = [entries[key] for key in batches[-1]]
    packed = heads * slots + 2 * 3 * 8 * tiles_each
    last = pl.pallas_call(
        make_last(base, len(parts)),
        out_shape=(
            shape((tiles_each, heads, HD, TILE), f32),
            shape((tiles_each, 8, TILE), f32),
            shape((tiles_each, 8, TILE), f32),
        )
        + (shape((packed, HD), bf16),) * (PLANE - 1),
        in_specs=[full(SMEM), full(), full(pl.ANY), full(), full()] + [full(pl.ANY)] * len(parts),
        out_specs=(full(),) * (PLANE + 2),
        scratch_shapes=[
            pltpu.VMEM((every, heads, HD, TILE), f32),
            pltpu.VMEM((every, 8, TILE), f32),
            pltpu.VMEM((every, 8, TILE), f32),
        ]
        + work(len(parts)),
        cost_estimate=cost(len(parts), 8 << 20),
        compiler_params=params(),
        name="last",
    )(meta, q_all, *state, *parts)
    returned = [
        lax.ppermute(out, "req", beside(k)) for k, out in zip(range(1, PLANE), last[3:])
    ]
    width = residual.shape[1]
    columns = width // ways
    where = tensor.astype(jnp.int32).reshape(1)
    pieces = pl.pallas_call(
        combine_kernel,
        out_shape=tuple(shape((slots, columns), bf16 if k else f32) for k in range(ways)),
        in_specs=[full(SMEM)] * 2 + [full()] * 6 + [full(pl.ANY)],
        out_specs=(full(),) * ways,
        scratch_shapes=[
            pltpu.VMEM((slots, heads * HD), bf16),
            pltpu.VMEM((ways, heads * HD, columns), bf16),
            pltpu.SemaphoreType.DMA((ways,)),
        ],
        cost_estimate=pl.CostEstimate(
            flops=2 * slots * heads * HD * width, bytes_accessed=12 << 20, transcendentals=0
        ),
        compiler_params=params(60),
        name="combine",
    )(meta, where, *last[:3], *returned, out_weight)
    sent = [
        lax.ppermute(pieces[k], "tp", [(i, i ^ k) for i in range(ways)])
        for k in range(1, ways)
    ]
    shared = pieces[0]
    for piece in sent:
        shared = shared + piece.astype(f32)
    own_residual = lax.dynamic_slice_in_dim(residual, tensor * columns, columns, 1)
    hidden = (own_residual.astype(f32) + shared).astype(bf16)
    widened = hidden.astype(f32)
    squares = jnp.sum(widened * widened, axis=1).reshape(slots // HD, HD)
    squares = jnp.pad(squares, ((0, 8 - slots // HD), (0, 0)))
    spread = lax.all_to_all(jnp.broadcast_to(squares[None], (ways, 8, HD)), "tp", 0, 0)
    row_squares = jnp.sum(spread, axis=0)[: slots // HD].reshape(slots)
    scale_rows = lax.rsqrt(row_squares / width + EPSILON)
    normed = (widened * scale_rows[:, None] * norm_gain.astype(f32)[None, :]).astype(bf16)
    return (hidden, normed, cache_key)


def solution(mesh):
    return jax.shard_map(
        shards,
        mesh=mesh,
        in_specs=(
            P("req", "tp"),
            P("req", "tp"),
            P("req", "tp"),
            P("req", None, "tp"),
            P("req", None, "tp"),
            P("req", None),
            P("tp", None),
            P("tp"),
            P(),
            P(),
            P(),
            P(),
        ),
        out_specs=(P("req", "tp"), P("req", "tp"), P("req", "tp")),
        check_vma=False,
    )
```

```python
import jax
import jax.numpy as jnp
from jax import lax
from jax.experimental import pallas as pl
from jax.experimental.pallas import tpu as pltpu
from jax.sharding import PartitionSpec as P


HD = 128
GROUPS = 4
PLANE = 4
TILE = 128
THETA = 1000000.0
NEGATIVE = -1e30
EPSILON = 1e-06
LOG2E = 1.4426950408889634


SMEM = pltpu.SMEM
VMEM = pltpu.VMEM


def full(space=VMEM):
    return pl.BlockSpec(memory_space=space)


def params(limit=26):
    return pltpu.CompilerParams(vmem_limit_bytes=limit * 1024 * 1024)


RATE = HD ** (-0.5) * LOG2E
NT = (((1,), (1,)), ((), ()))


def turn(x, cosines, sines):
    return x * cosines + pltpu.roll(x, HD // 2, 1) * sines


def turn_tiles(q_in, q_ref, at, cosines, sines):
    for j in range(q_in.shape[0] // TILE):
        rows = slice(j * TILE, (j + 1) * TILE)
        for h in range(q_ref.shape[1]):
            x = q_in[rows, h * HD : (h + 1) * HD].astype(jnp.float32)
            q_ref[at + j, h] = turn(x, cosines[rows], sines[rows]).astype(jnp.bfloat16)


def own_kernel(meta, q_in, k_in, v_in, cos_in, sin_in, q_out, key_out, acc_ref, max_ref, sum_ref):
    tiles, heads = q_out.shape[:2]
    slots = k_in.shape[0]
    length = meta[0]
    cosines = cos_in[...]
    sines = sin_in[...]
    turn_tiles(q_in, q_out, 0, cosines, sines)
    turned = turn(k_in[...].astype(jnp.float32), cosines, sines)
    place = lax.broadcasted_iota(jnp.int32, turned.shape, 0)
    key_out[...] = jnp.where(place < length, turned, 0.0).astype(jnp.bfloat16)
    max_ref[...] = jnp.zeros_like(max_ref)
    sum_ref[...] = jnp.ones_like(sum_ref)
    k = key_out[...]
    v = v_in[...].T
    u = lax.broadcasted_iota(jnp.int32, (slots, TILE), 0)
    t = lax.broadcasted_iota(jnp.int32, (slots, TILE), 1)
    for j in range(tiles):
        visible = (u <= t + j * TILE) & (u < length)
        for h in range(heads):
            scores = lax.dot_general(k, q_out[j, h], NT, preferred_element_type=jnp.float32)
            scores = jnp.where(visible, scores, NEGATIVE)
            top = jnp.max(scores, axis=0, keepdims=True)
            weights = jnp.exp2((scores - top) * RATE)
            max_ref[j, h : h + 1] = top
            sum_ref[j, h : h + 1] = jnp.sum(weights, axis=0, keepdims=True)
            acc_ref[j, h] = jnp.dot(v, weights.astype(jnp.bfloat16), preferred_element_type=jnp.float32)


def visit(meta, base, count, q_ref, kv_ref, vt_ref, s_ref, p_ref, top_ref, keep_ref, acc_ref, max_ref, sum_ref, items):
    heads = q_ref.shape[1]
    spare = q_ref.shape[0] - 1
    tiles = spare // PLANE
    part = kv_ref.shape[2]
    for e in range(count):
        vt_ref[e, :HD] = kv_ref[e, 1].T
        vt_ref[e, HD:] = jnp.ones((16, part), jnp.bfloat16)
    n = jnp.int32(0)
    for e in range(count):
        for i in range(PLANE):
            for j in range(tiles):
                live = (meta[2 * PLANE + (base + e) * PLANE + i] == 1) & (j < meta[PLANE + i])

                @pl.when(live)
                def _(n=n, e=e, i=i, j=j):
                    items[n, 0] = e
                    items[n, 1] = i * tiles + j

                n = n + live.astype(jnp.int32)
    for x in range(4):
        items[n + x, 0] = 0
        items[n + x, 1] = spare

    def score(step, slot):
        k = kv_ref[items[step, 0], 0]
        at = items[step, 1]
        for h in range(heads):
            scores = lax.dot_general(k, q_ref[at, h], NT, preferred_element_type=jnp.float32)
            s_ref[slot, h] = scores
            top_ref[slot, h : h + 1] = jnp.max(scores, axis=0, keepdims=True)

    def weigh(step, slot):
        at = items[step, 1]
        old = max_ref[at]
        new = jnp.maximum(old, top_ref[slot])
        max_ref[at] = new
        keep_ref[slot] = jnp.exp2((old - new) * RATE)
        for h in range(heads):
            p_ref[slot, h] = jnp.exp2((s_ref[slot, h] - new[h : h + 1]) * RATE).astype(jnp.bfloat16)

    def gather(step, slot):
        v = vt_ref[items[step, 0]]
        at = items[step, 1]
        keep = keep_ref[slot]
        for h in range(heads):
            mixed = jnp.dot(v, p_ref[slot, h], preferred_element_type=jnp.float32)
            acc_ref[at, h] = acc_ref[at, h] * keep[h : h + 1] + mixed[:HD]
            sum_ref[at, h : h + 1] = sum_ref[at, h : h + 1] * keep[h : h + 1] + mixed[HD : HD + 1]

    @pl.when(n > 0)
    def _():
        score(0, 0)
        score(1, 1)
        weigh(0, 0)

        def body(t, carry):
            for x in range(2):
                step = 2 * t + x
                score_slot = x
                gather(step, x)
                weigh(step + 1, 1 - x)
                score(step + 2, score_slot)
            return carry

        lax.fori_loop(0, (n + 1) // 2, body, 0)


def fetch(pairs, sems):
    copies = [
        pltpu.make_async_copy(source, target, sems.at[n])
        for n, (source, target) in enumerate(pairs)
    ]
    for copy in copies:
        copy.start()
    return copies


def make_first(base, count):
    def kernel(meta, q_own, acc_own, max_own, sum_own, q1, q2, q3, cos_in, sin_in, *rest):
        kv_in = rest[:count]
        q_ref, acc_ref, max_ref, sum_ref, sems, kv_ref, vt_ref, s_ref, p_ref, top_ref, keep_ref, items = rest[count:]
        copies = fetch([(kv, kv_ref.at[e]) for e, kv in enumerate(kv_in)], sems)
        tiles = q_own.shape[0]
        acc_ref[tiles:] = jnp.zeros_like(acc_ref[tiles:])
        max_ref[tiles:] = jnp.full_like(max_ref[tiles:], NEGATIVE)
        sum_ref[tiles:] = jnp.zeros_like(sum_ref[tiles:])
        top_ref[...] = jnp.zeros_like(top_ref)
        q_ref[:tiles] = q_own[...]
        q_ref[PLANE * tiles] = q_own[0]
        acc_ref[:tiles] = acc_own[...]
        max_ref[:tiles] = max_own[...]
        sum_ref[:tiles] = sum_own[...]
        cosines = cos_in[...]
        sines = sin_in[...]
        for i, q_in in enumerate((q1, q2, q3)):
            turn_tiles(q_in, q_ref, (i + 1) * tiles, cosines, sines)
        for copy in copies:
            copy.wait()
        visit(meta, base, count, q_ref, kv_ref, vt_ref, s_ref, p_ref, top_ref, keep_ref, acc_ref, max_ref, sum_ref, items)

    return kernel


def make_middle(base, count):
    def kernel(meta, q_ref, acc_in, max_in, sum_in, *rest):
        kv_in = rest[:count]
        acc_ref, max_ref, sum_ref, sems, kv_ref, vt_ref, s_ref, p_ref, top_ref, keep_ref, items = rest[count:]
        pairs = [(kv, kv_ref.at[e]) for e, kv in enumerate(kv_in)]
        copies = fetch(pairs + [(acc_in, acc_ref)], sems)
        max_ref[...] = max_in[...]
        sum_ref[...] = sum_in[...]
        top_ref[...] = jnp.zeros_like(top_ref)
        for copy in copies:
            copy.wait()
        visit(meta, base, count, q_ref, kv_ref, vt_ref, s_ref, p_ref, top_ref, keep_ref, acc_ref, max_ref, sum_ref, items)

    return kernel


def split(x):
    high = x.astype(jnp.bfloat16)
    left = x - high.astype(jnp.float32)
    middle = left.astype(jnp.bfloat16)
    low = (left - middle.astype(jnp.float32)).astype(jnp.bfloat16)
    return high, middle, low


def make_last(base, count):
    def kernel(meta, q_ref, acc_in, max_in, sum_in, *rest):
        kv_in = rest[:count]
        acc_own, max_own, sum_own, o1, o2, o3 = rest[count : count + 6]
        acc_ref, max_ref, sum_ref, sems, kv_ref, vt_ref, s_ref, p_ref, top_ref, keep_ref, items = rest[count + 6 :]
        pairs = [(kv, kv_ref.at[e]) for e, kv in enumerate(kv_in)]
        copies = fetch(pairs + [(acc_in, acc_ref)], sems)
        max_ref[...] = max_in[...]
        sum_ref[...] = sum_in[...]
        top_ref[...] = jnp.zeros_like(top_ref)
        for copy in copies:
            copy.wait()
        visit(meta, base, count, q_ref, kv_ref, vt_ref, s_ref, p_ref, top_ref, keep_ref, acc_ref, max_ref, sum_ref, items)
        tiles, heads = acc_own.shape[:2]
        acc_own[...] = acc_ref[:tiles]
        max_own[...] = max_ref[:tiles]
        sum_own[...] = sum_ref[:tiles]
        for i, out in enumerate((o1, o2, o3)):
            first = (i + 1) * tiles
            for j in range(tiles):
                total = sum_ref[first + j]
                inverse = jnp.where(total > 0, 1.0 / jnp.where(total > 0, total, 1.0), 0.0)
                for h in range(heads):
                    at = (j * heads + h) * HD
                    out[at : at + HD] = (acc_ref[first + j, h] * inverse[h : h + 1]).astype(jnp.bfloat16)
            at = tiles * heads * HD
            for stats in (max_ref, sum_ref):
                flat = jnp.concatenate([stats[first + j] for j in range(tiles)], axis=0)
                for piece in split(flat):
                    out[at : at + 8 * tiles] = piece
                    at = at + 8 * tiles

    return kernel


def combine_kernel(meta, where, acc_in, max_in, sum_in, r1, r2, r3, weight_in, *rest):
    received = (r1, r2, r3)
    ways = len(rest) - 10
    outs = rest[:ways]
    attn_ref, weight_ref, sems, part_sems, acc_own, max_own, sum_own, o1, o2, o3 = rest[ways:]
    columns = weight_ref.shape[2]
    parts = (acc_in, max_in, sum_in, *received)
    held = (acc_own, max_own, sum_own, o1, o2, o3)
    early = [
        pltpu.make_async_copy(source, target, part_sems.at[n])
        for n, (source, target) in enumerate(zip(parts, held))
    ]
    for copy in early:
        copy.start()
    copies = []
    for k in range(ways):
        at = pl.multiple_of((where[0] ^ k) * columns, HD)
        copies.append(
            pltpu.make_async_copy(
                weight_in.at[:, pl.ds(at, columns)], weight_ref.at[k], sems.at[k]
            )
        )
    for copy in copies[1:] + copies[:1]:
        copy.start()
    for copy in early:
        copy.wait()
    tiles, heads = acc_own.shape[:2]
    rows = 8 * tiles
    maxima = [jnp.concatenate([max_own[j] for j in range(tiles)], axis=0)]
    sums = [jnp.concatenate([sum_own[j] for j in range(tiles)], axis=0)]
    for part in (o1, o2, o3):
        at = tiles * heads * HD
        found = []
        for _ in range(2):
            pieces = [
                part[at + n * rows : at + (n + 1) * rows].astype(jnp.float32) for n in range(3)
            ]
            found.append(pieces[0] + pieces[1] + pieces[2])
            at = at + 3 * rows
        maxima.append(found[0])
        sums.append(found[1])
    top = jnp.maximum(jnp.maximum(maxima[0], maxima[1]), jnp.maximum(maxima[2], maxima[3]))
    factor = [jnp.exp2((m - top) * RATE) for m in maxima]
    mass = [f * s for f, s in zip(factor, sums)]
    inverse = 1.0 / (mass[0] + mass[1] + mass[2] + mass[3])
    lane = lax.broadcasted_iota(jnp.int32, (HD, TILE), 1)
    shares = [factor[0] * inverse] + [m * inverse for m in mass[1:]]
    for j in range(tiles):
        live = lane + j * TILE < meta[0]
        for h in range(heads):
            r = j * 8 + h
            value = acc_own[j, h] * shares[0][r : r + 1]
            for w, part in zip(shares[1:], (o1, o2, o3)):
                at = (j * heads + h) * HD
                value = value + w[r : r + 1] * part[at : at + HD].astype(jnp.float32)
            value = jnp.transpose(jnp.where(live, value, 0.0))
            attn_ref[j * TILE : (j + 1) * TILE, h * HD : (h + 1) * HD] = value.astype(jnp.bfloat16)
    for k in list(range(1, ways)) + [0]:
        copies[k].wait()
        outs[k][...] = jnp.dot(
            attn_ref[...], weight_ref[k], preferred_element_type=jnp.float32
        ).astype(outs[k].dtype)


def cost(blocks, bytes_accessed):
    pairs = blocks * 1280 * 512
    return pl.CostEstimate(
        flops=4 * pairs * HD, bytes_accessed=bytes_accessed, transcendentals=pairs
    )


def shards(
    suffix_query,
    suffix_key,
    suffix_value,
    prefix_key,
    prefix_value,
    residual,
    out_weight,
    norm_gain,
    lengths,
    request_slot,
    prefix_owner,
    request_group,
):
    slots = suffix_query.shape[0]
    heads = suffix_query.shape[1] // HD
    devices = lax.axis_size("req")
    planes = devices // PLANE
    place = lax.axis_index("req")
    tensor = lax.axis_index("tp")
    ways = lax.axis_size("tp")
    per_group = devices // GROUPS
    block = prefix_key.shape[1]
    part = block // 2
    prefix_length = block * per_group
    bf16 = jnp.bfloat16
    f32 = jnp.float32

    def beside(k):
        return [(i, i ^ k) for i in range(devices)]

    up_pairs = [(i, (i + PLANE) % devices) for i in range(devices)]
    down_pairs = [(i, (i - PLANE) % devices) for i in range(devices)]

    core = place % 2
    both = jnp.concatenate([prefix_key, prefix_value], axis=0)
    mine = lax.dynamic_slice_in_dim(both, core * part, part, 1)
    theirs = lax.dynamic_slice_in_dim(both, (1 - core) * part, part, 1)
    lanes = [mine, lax.ppermute(theirs, "req", beside(1))]
    queries = []
    for k in range(1, PLANE):
        queries.append(lax.ppermute(suffix_query, "req", beside(k)))

    entries = {(0, 0): lanes[0], (0, 1): lanes[1]}
    half_way = planes // 2
    for lane in range(2):
        moving_up = lanes[lane]
        moving_down = lanes[lane]
        for step in range(1, half_way):
            moving_up = lax.ppermute(moving_up, "req", up_pairs)
            moving_down = lax.ppermute(moving_down, "req", down_pairs)
            entries[(-step, lane)] = moving_up
            entries[(step, lane)] = moving_down
        if lane == 0:
            entries[(-half_way, 0)] = lax.ppermute(moving_up, "req", up_pairs)
        else:
            entries[(half_way, 1)] = lax.ppermute(moving_down, "req", down_pairs)

    batches = [
        [(0, 0), (0, 1), (-1, 0), (1, 0), (-1, 1), (1, 1)],
        [(-2, 0), (2, 0), (-2, 1), (2, 1)],
        [(-3, 0), (3, 0), (-3, 1), (3, 1)],
        [(-half_way, 0), (half_way, 1)],
    ]
    order = [key for batch in batches for key in batch]

    numbers = jnp.arange(devices, dtype=jnp.int32)
    owner_match = prefix_owner[None, :] == numbers[:, None]
    holder_group = jnp.sum(jnp.where(owner_match, numbers[None, :], 0), axis=1) // per_group
    slot_match = request_slot[:, None] == numbers[None, :]
    asker_group = jnp.sum(jnp.where(slot_match, request_group[:, 0][None, :], 0), axis=1)
    asker_length = jnp.sum(jnp.where(slot_match, lengths[None, :], 0), axis=1)
    nearby = place ^ jnp.arange(PLANE, dtype=jnp.int32)
    near = nearby[:, None] == numbers[None, :]
    near_group = jnp.sum(jnp.where(near, asker_group[None, :], 0), axis=1)
    near_length = jnp.sum(jnp.where(near, asker_length[None, :], 0), axis=1)
    shift = jnp.array([key[0] for key in order], jnp.int32)
    twist = jnp.array([key[1] for key in order], jnp.int32)
    source = ((place // PLANE + shift) % planes) * PLANE + ((place % PLANE) ^ twist)
    from_there = source[:, None] == numbers[None, :]
    source_group = jnp.sum(jnp.where(from_there, holder_group[None, :], 0), axis=1)
    match = (source_group[:, None] == near_group[None, :]).astype(jnp.int32)
    tiles = (near_length + TILE - 1) // TILE
    meta = jnp.concatenate([near_length, tiles, match.reshape(-1)])

    half_dim = HD // 2
    positions = (prefix_length + jnp.arange(slots)).astype(f32)
    frequency = THETA ** (-(jnp.arange(half_dim).astype(f32) * 2.0 / HD))
    angles = positions[:, None] * frequency[None, :]
    cosines = jnp.cos(angles)
    sines = jnp.sin(angles)
    cosines = jnp.concatenate([cosines, cosines], axis=1)
    sines = jnp.concatenate([-sines, sines], axis=1)

    tiles_each = slots // TILE
    shape = jax.ShapeDtypeStruct
    q_own, cache_key, acc_own, max_own, sum_own = pl.pallas_call(
        own_kernel,
        out_shape=(
            shape((tiles_each, heads, TILE, HD), bf16),
            shape((slots, HD), bf16),
            shape((tiles_each, heads, HD, TILE), f32),
            shape((tiles_each, 8, TILE), f32),
            shape((tiles_each, 8, TILE), f32),
        ),
        in_specs=[full(SMEM)] + [full()] * 5,
        out_specs=(full(),) * 5,
        cost_estimate=cost(1, 3 << 20),
        compiler_params=params(),
        name="own",
    )(meta, suffix_query, suffix_key, suffix_value, cosines, sines)

    every = PLANE * tiles_each + 1
    state_shapes = (
        shape((every, heads, HD, TILE), f32),
        shape((every, 8, TILE), f32),
        shape((every, 8, TILE), f32),
    )

    def work(count):
        return [
            pltpu.SemaphoreType.DMA((count + 1,)),
            pltpu.VMEM((count, 2, part, HD), bf16),
            pltpu.VMEM((count, HD + 16, part), bf16),
            pltpu.VMEM((2, heads, part, TILE), f32),
            pltpu.VMEM((2, heads, part, TILE), bf16),
            pltpu.VMEM((2, 8, TILE), f32),
            pltpu.VMEM((2, 8, TILE), f32),
            pltpu.SMEM((count * PLANE * tiles_each + 4, 2), jnp.int32),
        ]

    base = 0
    parts = [entries[key] for key in batches[0]]
    q_all, *state = pl.pallas_call(
        make_first(base, len(parts)),
        out_shape=(shape((every, heads, TILE, HD), bf16),) + state_shapes,
        in_specs=[full(SMEM)] + [full()] * 9 + [full(pl.ANY)] * len(parts),
        out_specs=(full(),) * 4,
        scratch_shapes=work(len(parts)),
        cost_estimate=cost(len(parts), 8 << 20),
        compiler_params=params(),
        name="first",
    )(meta, q_own, acc_own, max_own, sum_own, *queries, cosines, sines, *parts)
    base += len(parts)
    for batch in batches[1:-1]:
        parts = [entries[key] for key in batch]
        state = pl.pallas_call(
            make_middle(base, len(parts)),
            out_shape=state_shapes,
            in_specs=[full(SMEM), full(), full(pl.ANY), full(), full()] + [full(pl.ANY)] * len(parts),
            out_specs=(full(),) * 3,
            scratch_shapes=work(len(parts)),
            cost_estimate=cost(len(parts), 8 << 20),
            compiler_params=params(),
            name="middle",
        )(meta, q_all, *state, *parts)
        base += len(parts)
    parts = [entries[key] for key in batches[-1]]
    packed = heads * slots + 2 * 3 * 8 * tiles_each
    last = pl.pallas_call(
        make_last(base, len(parts)),
        out_shape=(
            shape((tiles_each, heads, HD, TILE), f32),
            shape((tiles_each, 8, TILE), f32),
            shape((tiles_each, 8, TILE), f32),
        )
        + (shape((packed, HD), bf16),) * (PLANE - 1),
        in_specs=[full(SMEM), full(), full(pl.ANY), full(), full()] + [full(pl.ANY)] * len(parts),
        out_specs=(full(),) * (PLANE + 2),
        scratch_shapes=[
            pltpu.VMEM((every, heads, HD, TILE), f32),
            pltpu.VMEM((every, 8, TILE), f32),
            pltpu.VMEM((every, 8, TILE), f32),
        ]
        + work(len(parts)),
        cost_estimate=cost(len(parts), 8 << 20),
        compiler_params=params(),
        name="last",
    )(meta, q_all, *state, *parts)
    returned = [
        lax.ppermute(out, "req", beside(k)) for k, out in zip(range(1, PLANE), last[3:])
    ]
    width = residual.shape[1]
    columns = width // ways
    where = tensor.astype(jnp.int32).reshape(1)
    pieces = pl.pallas_call(
        combine_kernel,
        out_shape=tuple(shape((slots, columns), bf16 if k else f32) for k in range(ways)),
        in_specs=[full(SMEM)] * 2 + [full(pl.ANY)] * 6 + [full(pltpu.HBM)],
        out_specs=(full(),) * ways,
        scratch_shapes=[
            pltpu.VMEM((slots, heads * HD), bf16),
            pltpu.VMEM((ways, heads * HD, columns), bf16),
            pltpu.SemaphoreType.DMA((ways,)),
            pltpu.SemaphoreType.DMA((6,)),
            pltpu.VMEM((tiles_each, heads, HD, TILE), f32),
            pltpu.VMEM((tiles_each, 8, TILE), f32),
            pltpu.VMEM((tiles_each, 8, TILE), f32),
        ]
        + [pltpu.VMEM((packed, HD), bf16)] * 3,
        cost_estimate=pl.CostEstimate(
            flops=2 * slots * heads * HD * width, bytes_accessed=12 << 20, transcendentals=0
        ),
        compiler_params=params(26),
        name="combine",
    )(meta, where, *last[:3], *returned, out_weight)
    sent = []
    for k in range(1, ways):
        sent.append(lax.ppermute(pieces[k], "tp", [(i, i ^ k) for i in range(ways)]))
    shared = pieces[0]
    for piece in sent:
        shared = shared + piece.astype(f32)
    own_residual = lax.dynamic_slice_in_dim(residual, tensor * columns, columns, 1)
    hidden = (own_residual.astype(f32) + shared).astype(bf16)
    widened = hidden.astype(f32)
    squares = jnp.sum(widened * widened, axis=1).reshape(slots // HD, HD)
    squares = jnp.pad(squares, ((0, 8 - slots // HD), (0, 0)))
    spread = lax.all_to_all(jnp.broadcast_to(squares[None], (ways, 8, HD)), "tp", 0, 0)
    row_squares = jnp.sum(spread, axis=0)[: slots // HD].reshape(slots)
    scale_rows = lax.rsqrt(row_squares / width + EPSILON)
    normed = (widened * scale_rows[:, None] * norm_gain.astype(f32)[None, :]).astype(bf16)
    return (hidden, normed, cache_key)


def solution(mesh):
    return jax.shard_map(
        shards,
        mesh=mesh,
        in_specs=(
            P("req", "tp"),
            P("req", "tp"),
            P("req", "tp"),
            P("req", None, "tp"),
            P("req", None, "tp"),
            P("req", None),
            P("tp", None),
            P("tp"),
            P(),
            P(),
            P(),
            P(),
        ),
        out_specs=(P("req", "tp"), P("req", "tp"), P("req", "tp")),
        check_vma=False,
    )
```

```python
import jax
import jax.numpy as jnp
from jax import lax
from jax.experimental import pallas as pl
from jax.experimental.pallas import tpu as pltpu
from jax.sharding import PartitionSpec as P


HD = 128
GROUPS = 4
PLANE = 4
TILE = 128
THETA = 1000000.0
NEGATIVE = -1e30
EPSILON = 1e-06
LOG2E = 1.4426950408889634
PATHS = (6, 2, 4, 7, 5, 3, 1, 0)


SMEM = pltpu.SMEM
VMEM = pltpu.VMEM


def full(space=VMEM):
    return pl.BlockSpec(memory_space=space)


def params(limit=26):
    return pltpu.CompilerParams(vmem_limit_bytes=limit * 1024 * 1024)


RATE = HD ** (-0.5) * LOG2E
NT = (((1,), (1,)), ((), ()))


def turn(x, cosines, sines):
    return x * cosines + pltpu.roll(x, HD // 2, 1) * sines


def turn_tiles(q_in, q_ref, at, cosines, sines):
    for j in range(q_in.shape[0] // TILE):
        rows = slice(j * TILE, (j + 1) * TILE)
        for h in range(q_ref.shape[1] // TILE):
            x = q_in[rows, h * HD : (h + 1) * HD].astype(jnp.float32)
            q_ref[at + j, h * TILE : (h + 1) * TILE] = turn(x, cosines[rows], sines[rows]).astype(
                jnp.bfloat16
            )


def spans(width):
    return [(low, min(low + 2 * TILE, width)) for low in range(0, width, 2 * TILE)]


def own_kernel(meta, q_in, k_in, v_in, cos_in, sin_in, q_out, key_out, acc_ref, max_ref, sum_ref):
    tiles, lines = q_out.shape[:2]
    slots = k_in.shape[0]
    length = meta[0]
    cosines = cos_in[...]
    sines = sin_in[...]
    turn_tiles(q_in, q_out, 0, cosines, sines)
    turned = turn(k_in[...].astype(jnp.float32), cosines, sines)
    place = lax.broadcasted_iota(jnp.int32, turned.shape, 0)
    key_out[...] = jnp.where(place < length, turned, 0.0).astype(jnp.bfloat16)
    k = key_out[...]
    v = v_in[...].T
    u = lax.broadcasted_iota(jnp.int32, (slots, TILE), 0)
    t = lax.broadcasted_iota(jnp.int32, (slots, TILE), 1)
    for j in range(tiles):
        visible = (u <= t + j * TILE) & (u < length)
        for low in range(0, lines, TILE):
            high = low + TILE
            scores = lax.dot_general(
                k, q_out[j, low:high], NT, preferred_element_type=jnp.float32
            )
            scores = jnp.where(visible, scores, NEGATIVE)
            top = jnp.max(scores, axis=0, keepdims=True)
            weights = jnp.exp2((scores - top) * RATE)
            max_ref[j, :, low:high] = top
            sum_ref[j, :, low:high] = jnp.sum(weights, axis=0, keepdims=True)
            acc_ref[j, :, low:high] = jnp.dot(
                v, weights.astype(jnp.bfloat16), preferred_element_type=jnp.float32
            )


def visit(meta, base, count, q_ref, kv_ref, vt_ref, s_ref, p_ref, top_ref, keep_ref, acc_ref, max_ref, sum_ref, items):
    spare = q_ref.shape[0] - 1
    tiles = spare // PLANE
    part = kv_ref.shape[2]
    cuts = spans(q_ref.shape[1])
    for e in range(count):
        vt_ref[e, :HD] = kv_ref[e, 1].T
        vt_ref[e, HD:] = jnp.ones((16, part), jnp.bfloat16)
    for x in range(2):
        items[x, 0] = 0
        items[x, 1] = spare
    n = jnp.int32(2)
    for e in range(count):
        for i in range(PLANE):
            for j in range(tiles):
                live = (meta[2 * PLANE + (base + e) * PLANE + i] == 1) & (j < meta[PLANE + i])

                @pl.when(live)
                def _(n=n, e=e, i=i, j=j):
                    items[n, 0] = e
                    items[n, 1] = i * tiles + j

                n = n + live.astype(jnp.int32)
    for x in range(4):
        items[n + x, 0] = 0
        items[n + x, 1] = spare

    def score(step, slot):
        k = kv_ref[items[step, 0], 0]
        at = items[step, 1]
        for low, high in cuts:
            scores = lax.dot_general(
                k, q_ref[at, low:high], NT, preferred_element_type=jnp.float32
            )
            s_ref[slot, :, low:high] = scores
            top_ref[slot, :, low:high] = jnp.max(scores, axis=0, keepdims=True)

    def weigh(step, slot):
        at = items[step, 1]
        old = max_ref[at]
        new = jnp.maximum(old, top_ref[slot])
        max_ref[at] = new
        keep_ref[slot] = jnp.exp2((old - new) * RATE)
        for low, high in cuts:
            p_ref[slot, :, low:high] = jnp.exp2(
                (s_ref[slot, :, low:high] - new[:, low:high]) * RATE
            ).astype(jnp.bfloat16)

    def gather(step, slot):
        v = vt_ref[items[step, 0]]
        at = items[step, 1]
        for low, high in cuts:
            keep = keep_ref[slot, :, low:high]
            mixed = jnp.dot(v, p_ref[slot, :, low:high], preferred_element_type=jnp.float32)
            acc_ref[at, :, low:high] = acc_ref[at, :, low:high] * keep + mixed[:HD]
            sum_ref[at, :, low:high] = sum_ref[at, :, low:high] * keep + mixed[HD : HD + 1]

    @pl.when(n > 2)
    def _():
        def body(t, carry):
            for x in range(2):
                step = 2 * t + x
                gather(step, x)
                weigh(step + 1, 1 - x)
                score(step + 2, x)
            return carry

        lax.fori_loop(0, (n + 1) // 2, body, 0)


def fetch(pairs, sems):
    copies = [
        pltpu.make_async_copy(source, target, sems.at[n])
        for n, (source, target) in enumerate(pairs)
    ]
    for copy in copies:
        copy.start()
    return copies


def make_first(base, count):
    def kernel(meta, q_own, acc_own, max_own, sum_own, q1, q2, q3, cos_in, sin_in, *rest):
        kv_in = rest[:count]
        q_ref, acc_ref, max_ref, sum_ref, sems, kv_ref, vt_ref, s_ref, p_ref, top_ref, keep_ref, items = rest[count:]
        copies = fetch([(kv, kv_ref.at[e]) for e, kv in enumerate(kv_in)], sems)
        tiles = q_own.shape[0]
        acc_ref[tiles:] = jnp.zeros_like(acc_ref[tiles:])
        max_ref[tiles:] = jnp.full_like(max_ref[tiles:], NEGATIVE)
        sum_ref[tiles:] = jnp.zeros_like(sum_ref[tiles:])
        q_ref[:tiles] = q_own[...]
        q_ref[PLANE * tiles] = q_own[0]
        acc_ref[:tiles] = acc_own[...]
        max_ref[:tiles] = max_own[...]
        sum_ref[:tiles] = sum_own[...]
        cosines = cos_in[...]
        sines = sin_in[...]
        for i, q_in in enumerate((q1, q2, q3)):
            turn_tiles(q_in, q_ref, (i + 1) * tiles, cosines, sines)
        for copy in copies:
            copy.wait()
        visit(meta, base, count, q_ref, kv_ref, vt_ref, s_ref, p_ref, top_ref, keep_ref, acc_ref, max_ref, sum_ref, items)

    return kernel


def make_middle(base, count):
    def kernel(meta, q_ref, acc_in, max_in, sum_in, *rest):
        kv_in = rest[:count]
        acc_ref, max_ref, sum_ref, sems, kv_ref, vt_ref, s_ref, p_ref, top_ref, keep_ref, items = rest[count:]
        pairs = [(kv, kv_ref.at[e]) for e, kv in enumerate(kv_in)]
        copies = fetch(pairs + [(acc_in, acc_ref)], sems)
        max_ref[...] = max_in[...]
        sum_ref[...] = sum_in[...]
        for copy in copies:
            copy.wait()
        visit(meta, base, count, q_ref, kv_ref, vt_ref, s_ref, p_ref, top_ref, keep_ref, acc_ref, max_ref, sum_ref, items)

    return kernel


def stack(maxima, sums):
    rows = []
    for line in (maxima, sums):
        heads = line.shape[1] // TILE
        rows += [line[:, h * TILE : (h + 1) * TILE] for h in range(heads)]
        rows.append(jnp.zeros((8 - heads, TILE), jnp.float32))
    return jnp.concatenate(rows, axis=0)


def pack(out, at, stats):
    high = stats.astype(jnp.bfloat16)
    left = stats - high.astype(jnp.float32)
    middle = left.astype(jnp.bfloat16)
    low = (left - middle.astype(jnp.float32)).astype(jnp.bfloat16)
    for n, piece in enumerate((high, middle, low)):
        out[at + 16 * n : at + 16 * (n + 1)] = piece


def unpack(part, at):
    pieces = [part[at + 16 * n : at + 16 * (n + 1)].astype(jnp.float32) for n in range(3)]
    stats = pieces[0] + pieces[1] + pieces[2]
    return stats[:8], stats[8:]


def safe(total):
    return jnp.where(total > 0, 1.0 / jnp.where(total > 0, total, 1.0), 0.0)


def make_last(base, count):
    def kernel(meta, q_ref, acc_in, max_in, sum_in, *rest):
        kv_in = rest[:count]
        tiles = (q_ref.shape[0] - 1) // PLANE
        outs = rest[count : count + 5 * tiles]
        acc_ref, max_ref, sum_ref, sems, kv_ref, vt_ref, s_ref, p_ref, top_ref, keep_ref, items = rest[count + 5 * tiles :]
        pairs = [(kv, kv_ref.at[e]) for e, kv in enumerate(kv_in)]
        copies = fetch(pairs + [(acc_in, acc_ref)], sems)
        max_ref[...] = max_in[...]
        sum_ref[...] = sum_in[...]
        for copy in copies:
            copy.wait()
        visit(meta, base, count, q_ref, kv_ref, vt_ref, s_ref, p_ref, top_ref, keep_ref, acc_ref, max_ref, sum_ref, items)
        heads = q_ref.shape[1] // TILE
        for j in range(tiles):
            acc_own, stats_own, acc_two, stats_two, swap = outs[5 * j : 5 * j + 5]
            acc_own[...] = acc_ref[j]
            stats_own[...] = stack(max_ref[j], sum_ref[j])
            two = 2 * tiles + j
            acc_two[...] = acc_ref[two]
            stats_two[...] = stack(max_ref[two], sum_ref[two])
            for slot, i in enumerate((1, 3)):
                at = i * tiles + j
                inverse = safe(sum_ref[at])
                for h in range(heads):
                    lanes = slice(h * TILE, (h + 1) * TILE)
                    swap[slot, h * HD : (h + 1) * HD] = (
                        acc_ref[at, :, lanes] * inverse[:, lanes]
                    ).astype(jnp.bfloat16)
                pack(swap.at[slot], heads * HD, stack(max_ref[at], sum_ref[at]))

    return kernel


def merge_kernel(acc_two, stats_two, swapped, out):
    heads = acc_two.shape[1] // TILE
    other = swapped.at[1]
    max_a, sum_a = stats_two[:8], stats_two[8:]
    max_b, sum_b = unpack(other, heads * HD)
    top = jnp.maximum(max_a, max_b)
    scale_a = jnp.exp2((max_a - top) * RATE)
    mass_b = sum_b * jnp.exp2((max_b - top) * RATE)
    total = sum_a * scale_a + mass_b
    inverse = safe(total)
    share_a = scale_a * inverse
    share_b = mass_b * inverse
    for h in range(heads):
        lanes = slice(h * TILE, (h + 1) * TILE)
        rows = slice(h * HD, (h + 1) * HD)
        value = acc_two[:, lanes] * share_a[h : h + 1]
        value = value + other[rows].astype(jnp.float32) * share_b[h : h + 1]
        out[rows] = value.astype(jnp.bfloat16)
    pack(out, heads * HD, jnp.concatenate([top, total], axis=0))


def make_combine(j):
    def kernel(meta, where, acc_own, stats_own, swapped, crossed, weight_in, *rest):
        ways = len(rest) - 3
        outs = rest[:ways]
        attn_ref, weight_ref, sems = rest[ways:]
        columns = weight_ref.shape[2]
        copies = []
        for k in range(ways):
            at = pl.multiple_of((where[0] ^ k) * columns, HD)
            copies.append(
                pltpu.make_async_copy(
                    weight_in.at[:, pl.ds(at, columns)], weight_ref.at[k], sems.at[k]
                )
            )
        for k in PATHS:
            copies[k].start()
        heads = acc_own.shape[1] // TILE
        parts = (swapped.at[0], crossed)
        maxima = [stats_own[:8]]
        sums = [stats_own[8:]]
        for part in parts:
            found = unpack(part, heads * HD)
            maxima.append(found[0])
            sums.append(found[1])
        top = jnp.maximum(jnp.maximum(maxima[0], maxima[1]), maxima[2])
        factor = [jnp.exp2((m - top) * RATE) for m in maxima]
        mass = [f * s for f, s in zip(factor, sums)]
        inverse = safe(mass[0] + mass[1] + mass[2])
        shares = [factor[0] * inverse] + [m * inverse for m in mass[1:]]
        live = lax.broadcasted_iota(jnp.int32, (HD, TILE), 1) + j * TILE < meta[0]
        for h in range(heads):
            lanes = slice(h * TILE, (h + 1) * TILE)
            value = acc_own[:, lanes] * shares[0][h : h + 1]
            for w, part in zip(shares[1:], parts):
                value = value + w[h : h + 1] * part[h * HD : (h + 1) * HD].astype(jnp.float32)
            value = jnp.transpose(jnp.where(live, value, 0.0))
            attn_ref[:, h * HD : (h + 1) * HD] = value.astype(jnp.bfloat16)
        for k in PATHS:
            copies[k].wait()
            outs[k][...] = jnp.dot(
                attn_ref[...], weight_ref[k], preferred_element_type=jnp.float32
            ).astype(outs[k].dtype)

    return kernel


def cost(blocks, bytes_accessed):
    pairs = blocks * 1280 * 512
    return pl.CostEstimate(
        flops=4 * pairs * HD, bytes_accessed=bytes_accessed, transcendentals=pairs
    )


def shards(
    suffix_query,
    suffix_key,
    suffix_value,
    prefix_key,
    prefix_value,
    residual,
    out_weight,
    norm_gain,
    lengths,
    request_slot,
    prefix_owner,
    request_group,
):
    slots = suffix_query.shape[0]
    heads = suffix_query.shape[1] // HD
    devices = lax.axis_size("req")
    planes = devices // PLANE
    place = lax.axis_index("req")
    tensor = lax.axis_index("tp")
    ways = lax.axis_size("tp")
    per_group = devices // GROUPS
    block = prefix_key.shape[1]
    part = block // 2
    prefix_length = block * per_group
    bf16 = jnp.bfloat16
    f32 = jnp.float32

    def beside(k):
        return [(i, i ^ k) for i in range(devices)]

    up_pairs = [(i, (i + PLANE) % devices) for i in range(devices)]
    down_pairs = [(i, (i - PLANE) % devices) for i in range(devices)]

    core = place % 2
    both = jnp.concatenate([prefix_key, prefix_value], axis=0)
    mine = lax.dynamic_slice_in_dim(both, core * part, part, 1)
    theirs = lax.dynamic_slice_in_dim(both, (1 - core) * part, part, 1)
    lanes = [mine, lax.ppermute(theirs, "req", beside(1))]
    queries = []
    for k in range(1, PLANE):
        queries.append(lax.ppermute(suffix_query, "req", beside(k)))

    entries = {(0, 0): lanes[0], (0, 1): lanes[1]}
    half_way = planes // 2
    for lane in range(2):
        moving_up = lanes[lane]
        moving_down = lanes[lane]
        for step in range(1, half_way):
            moving_up = lax.ppermute(moving_up, "req", up_pairs)
            moving_down = lax.ppermute(moving_down, "req", down_pairs)
            entries[(-step, lane)] = moving_up
            entries[(step, lane)] = moving_down
        if lane == 0:
            entries[(-half_way, 0)] = lax.ppermute(moving_up, "req", up_pairs)
        else:
            entries[(half_way, 1)] = lax.ppermute(moving_down, "req", down_pairs)

    batches = [
        [(0, 0), (0, 1), (-1, 0), (1, 0), (-1, 1), (1, 1)],
        [(-2, 0), (2, 0), (-2, 1), (2, 1)],
        [(-3, 0), (3, 0), (-3, 1), (3, 1)],
        [(-half_way, 0), (half_way, 1)],
    ]
    order = [key for batch in batches for key in batch]

    numbers = jnp.arange(devices, dtype=jnp.int32)
    owner_match = prefix_owner[None, :] == numbers[:, None]
    holder_group = jnp.sum(jnp.where(owner_match, numbers[None, :], 0), axis=1) // per_group
    slot_match = request_slot[:, None] == numbers[None, :]
    asker_group = jnp.sum(jnp.where(slot_match, request_group[:, 0][None, :], 0), axis=1)
    asker_length = jnp.sum(jnp.where(slot_match, lengths[None, :], 0), axis=1)
    nearby = place ^ jnp.arange(PLANE, dtype=jnp.int32)
    near = nearby[:, None] == numbers[None, :]
    near_group = jnp.sum(jnp.where(near, asker_group[None, :], 0), axis=1)
    near_length = jnp.sum(jnp.where(near, asker_length[None, :], 0), axis=1)
    shift = jnp.array([key[0] for key in order], jnp.int32)
    twist = jnp.array([key[1] for key in order], jnp.int32)
    source = ((place // PLANE + shift) % planes) * PLANE + ((place % PLANE) ^ twist)
    from_there = source[:, None] == numbers[None, :]
    source_group = jnp.sum(jnp.where(from_there, holder_group[None, :], 0), axis=1)
    match = (source_group[:, None] == near_group[None, :]).astype(jnp.int32)
    tiles = (near_length + TILE - 1) // TILE
    meta = jnp.concatenate([near_length, tiles, match.reshape(-1)])

    half_dim = HD // 2
    positions = (prefix_length + jnp.arange(slots)).astype(f32)
    frequency = THETA ** (-(jnp.arange(half_dim).astype(f32) * 2.0 / HD))
    angles = positions[:, None] * frequency[None, :]
    cosines = jnp.cos(angles)
    sines = jnp.sin(angles)
    cosines = jnp.concatenate([cosines, cosines], axis=1)
    sines = jnp.concatenate([-sines, sines], axis=1)

    tiles_each = slots // TILE
    shape = jax.ShapeDtypeStruct
    q_own, cache_key, acc_own, max_own, sum_own = pl.pallas_call(
        own_kernel,
        out_shape=(
            shape((tiles_each, heads * TILE, HD), bf16),
            shape((slots, HD), bf16),
            shape((tiles_each, HD, heads * TILE), f32),
        shape((tiles_each, 1, heads * TILE), f32),
        shape((tiles_each, 1, heads * TILE), f32),
    ),
        in_specs=[full(SMEM)] + [full()] * 5,
        out_specs=(full(),) * 5,
        cost_estimate=cost(1, 3 << 20),
        compiler_params=params(),
        name="own",
    )(meta, suffix_query, suffix_key, suffix_value, cosines, sines)

    every = PLANE * tiles_each + 1
    lines = heads * TILE
    state_shapes = (
        shape((every, HD, lines), f32),
        shape((every, 1, lines), f32),
        shape((every, 1, lines), f32),
    )

    def work(count):
        return [
            pltpu.SemaphoreType.DMA((count + 1,)),
            pltpu.VMEM((count, 2, part, HD), bf16),
            pltpu.VMEM((count, HD + 16, part), bf16),
            pltpu.VMEM((2, part, lines), f32),
            pltpu.VMEM((2, part, lines), bf16),
            pltpu.VMEM((2, 1, lines), f32),
            pltpu.VMEM((2, 1, lines), f32),
            pltpu.SMEM((count * PLANE * tiles_each + 6, 2), jnp.int32),
        ]

    base = 0
    parts = [entries[key] for key in batches[0]]
    q_all, *state = pl.pallas_call(
        make_first(base, len(parts)),
        out_shape=(shape((every, lines, HD), bf16),) + state_shapes,
        in_specs=[full(SMEM)] + [full()] * 9 + [full(pl.ANY)] * len(parts),
        out_specs=(full(),) * 4,
        scratch_shapes=work(len(parts)),
        cost_estimate=cost(len(parts), 8 << 20),
        compiler_params=params(),
        name="first",
    )(meta, q_own, acc_own, max_own, sum_own, *queries, cosines, sines, *parts)
    base += len(parts)
    for batch in batches[1:-1]:
        parts = [entries[key] for key in batch]
        state = pl.pallas_call(
            make_middle(base, len(parts)),
            out_shape=state_shapes,
            in_specs=[full(SMEM), full(), full(pl.ANY), full(), full()] + [full(pl.ANY)] * len(parts),
            out_specs=(full(),) * 3,
            scratch_shapes=work(len(parts)),
            cost_estimate=cost(len(parts), 8 << 20),
            compiler_params=params(),
            name="middle",
        )(meta, q_all, *state, *parts)
        base += len(parts)
    parts = [entries[key] for key in batches[-1]]
    packed = heads * HD + 3 * 16
    last = pl.pallas_call(
        make_last(base, len(parts)),
        out_shape=(
            shape((HD, lines), f32),
            shape((16, TILE), f32),
            shape((HD, lines), f32),
            shape((16, TILE), f32),
            shape((2, packed, TILE), bf16),
        )
        * tiles_each,
        in_specs=[full(SMEM), full(), full(pl.ANY), full(), full()] + [full(pl.ANY)] * len(parts),
        out_specs=(full(),) * (5 * tiles_each),
        scratch_shapes=[
            pltpu.VMEM((every, HD, lines), f32),
            pltpu.VMEM((every, 1, lines), f32),
            pltpu.VMEM((every, 1, lines), f32),
        ]
        + work(len(parts)),
        cost_estimate=cost(len(parts), 8 << 20),
        compiler_params=params(),
        name="last",
    )(meta, q_all, *state, *parts)

    width = residual.shape[1]
    columns = width // ways
    where = tensor.astype(jnp.int32).reshape(1)
    swapped = []
    for j in range(tiles_each):
        swapped.append(lax.ppermute(last[5 * j + 4], "req", beside(1)))
    crossed = []
    for j in range(tiles_each):
        merged = pl.pallas_call(
            merge_kernel,
            out_shape=shape((packed, TILE), bf16),
            in_specs=[full()] * 3,
            out_specs=full(),
            cost_estimate=pl.CostEstimate(flops=1 << 20, bytes_accessed=1 << 20, transcendentals=0),
            compiler_params=params(),
            name="merge",
        )(last[5 * j + 2], last[5 * j + 3], swapped[j])
        crossed.append(lax.ppermute(merged, "req", beside(2)))
    shared = []
    for j in range(tiles_each):
        pieces = pl.pallas_call(
            make_combine(j),
            out_shape=tuple(
                shape((TILE, columns), bf16 if k else f32) for k in range(ways)
            ),
            in_specs=[full(SMEM)] * 2 + [full()] * 4 + [full(pl.ANY)],
            out_specs=(full(),) * ways,
            scratch_shapes=[
                pltpu.VMEM((TILE, heads * HD), bf16),
                pltpu.VMEM((ways, heads * HD, columns), bf16),
                pltpu.SemaphoreType.DMA((ways,)),
            ],
            cost_estimate=pl.CostEstimate(
                flops=2 * TILE * heads * HD * width,
                bytes_accessed=8 << 20,
                transcendentals=0,
            ),
            compiler_params=params(50),
            name="combine",
        )(meta, where, last[5 * j], last[5 * j + 1], swapped[j], crossed[j], out_weight)
        total = pieces[0]
        for k in range(1, ways):
            piece = lax.ppermute(pieces[k], "tp", [(i, i ^ k) for i in range(ways)])
            total = total + piece.astype(f32)
        shared.append(total)
    shared = jnp.concatenate(shared, axis=0)
    own_residual = lax.dynamic_slice_in_dim(residual, tensor * columns, columns, 1)
    hidden = (own_residual.astype(f32) + shared).astype(bf16)
    widened = hidden.astype(f32)
    squares = jnp.sum(widened * widened, axis=1).reshape(slots // HD, HD)
    squares = jnp.pad(squares, ((0, 8 - slots // HD), (0, 0)))
    spread = lax.all_to_all(jnp.broadcast_to(squares[None], (ways, 8, HD)), "tp", 0, 0)
    row_squares = jnp.sum(spread, axis=0)[: slots // HD].reshape(slots)
    scale_rows = lax.rsqrt(row_squares / width + EPSILON)
    normed = (widened * scale_rows[:, None] * norm_gain.astype(f32)[None, :]).astype(bf16)
    return (hidden, normed, cache_key)


def solution(mesh):
    return jax.shard_map(
        shards,
        mesh=mesh,
        in_specs=(
            P("req", "tp"),
            P("req", "tp"),
            P("req", "tp"),
            P("req", None, "tp"),
            P("req", None, "tp"),
            P("req", None),
            P("tp", None),
            P("tp"),
            P(),
            P(),
            P(),
            P(),
        ),
        out_specs=(P("req", "tp"), P("req", "tp"), P("req", "tp")),
        check_vma=False,
    )
```

```python
import jax
import jax.numpy as jnp
from jax import lax
from jax.experimental import pallas as pl
from jax.experimental.pallas import tpu as pltpu
from jax.sharding import PartitionSpec as P


HD = 128
GROUPS = 4
PLANE = 4
TILE = 128
THETA = 1000000.0
NEGATIVE = -1e30
EPSILON = 1e-06
LOG2E = 1.4426950408889634
PATHS = (2, 3, 1, 0)
FAR = 4


SMEM = pltpu.SMEM
VMEM = pltpu.VMEM


def full(space=VMEM):
    return pl.BlockSpec(memory_space=space)


def params(limit=26):
    return pltpu.CompilerParams(vmem_limit_bytes=limit * 1024 * 1024)


RATE = HD ** (-0.5) * LOG2E
NT = (((1,), (1,)), ((), ()))


def turn(x, cosines, sines):
    return x * cosines + pltpu.roll(x, HD // 2, 1) * sines


def turn_tiles(q_in, q_ref, at, cosines, sines):
    for j in range(q_in.shape[0] // TILE):
        rows = slice(j * TILE, (j + 1) * TILE)
        for h in range(q_ref.shape[1] // TILE):
            x = q_in[rows, h * HD : (h + 1) * HD].astype(jnp.float32)
            q_ref[at + j, h * TILE : (h + 1) * TILE] = turn(x, cosines[rows], sines[rows]).astype(
                jnp.bfloat16
            )


def spans(width):
    return [(low, min(low + 2 * TILE, width)) for low in range(0, width, 2 * TILE)]


def own_kernel(meta, q_in, k_in, v_in, cos_in, sin_in, q_out, key_out, acc_ref, max_ref, sum_ref):
    tiles, lines = q_out.shape[:2]
    slots = k_in.shape[0]
    length = meta[0]
    cosines = cos_in[...]
    sines = sin_in[...]
    turn_tiles(q_in, q_out, 0, cosines, sines)
    turned = turn(k_in[...].astype(jnp.float32), cosines, sines)
    place = lax.broadcasted_iota(jnp.int32, turned.shape, 0)
    key_out[...] = jnp.where(place < length, turned, 0.0).astype(jnp.bfloat16)
    k = key_out[...]
    v = v_in[...].T
    u = lax.broadcasted_iota(jnp.int32, (slots, TILE), 0)
    t = lax.broadcasted_iota(jnp.int32, (slots, TILE), 1)
    for j in range(tiles):
        visible = (u <= t + j * TILE) & (u < length)
        for low in range(0, lines, TILE):
            high = low + TILE
            scores = lax.dot_general(
                k, q_out[j, low:high], NT, preferred_element_type=jnp.float32
            )
            scores = jnp.where(visible, scores, NEGATIVE)
            top = jnp.max(scores, axis=0, keepdims=True)
            weights = jnp.exp2((scores - top) * RATE)
            max_ref[j, :, low:high] = top
            sum_ref[j, :, low:high] = jnp.sum(weights, axis=0, keepdims=True)
            acc_ref[j, :, low:high] = jnp.dot(
                v, weights.astype(jnp.bfloat16), preferred_element_type=jnp.float32
            )


def visit(meta, base, count, q_ref, kv_ref, vt_ref, s_ref, p_ref, top_ref, keep_ref, acc_ref, max_ref, sum_ref, items):
    spare = q_ref.shape[0] - 1
    tiles = spare // PLANE
    part = kv_ref.shape[2]
    cuts = spans(q_ref.shape[1])
    for e in range(count):
        vt_ref[e, :HD] = kv_ref[e, 1].T
        vt_ref[e, HD:] = jnp.ones((16, part), jnp.bfloat16)
    for x in range(2):
        items[x, 0] = 0
        items[x, 1] = spare
    n = jnp.int32(2)
    for e in range(count):
        for i in range(PLANE):
            for j in range(tiles):
                live = (meta[2 * PLANE + (base + e) * PLANE + i] == 1) & (j < meta[PLANE + i])

                @pl.when(live)
                def _(n=n, e=e, i=i, j=j):
                    items[n, 0] = e
                    items[n, 1] = i * tiles + j

                n = n + live.astype(jnp.int32)
    for x in range(4):
        items[n + x, 0] = 0
        items[n + x, 1] = spare

    def score(step, slot):
        k = kv_ref[items[step, 0], 0]
        at = items[step, 1]
        for low, high in cuts:
            scores = lax.dot_general(
                k, q_ref[at, low:high], NT, preferred_element_type=jnp.float32
            )
            s_ref[slot, :, low:high] = scores
            top_ref[slot, :, low:high] = jnp.max(scores, axis=0, keepdims=True)

    def weigh(step, slot):
        at = items[step, 1]
        old = max_ref[at]
        new = jnp.maximum(old, top_ref[slot])
        max_ref[at] = new
        keep_ref[slot] = jnp.exp2((old - new) * RATE)
        for low, high in cuts:
            p_ref[slot, :, low:high] = jnp.exp2(
                (s_ref[slot, :, low:high] - new[:, low:high]) * RATE
            ).astype(jnp.bfloat16)

    def gather(step, slot):
        v = vt_ref[items[step, 0]]
        at = items[step, 1]
        for low, high in cuts:
            keep = keep_ref[slot, :, low:high]
            mixed = jnp.dot(v, p_ref[slot, :, low:high], preferred_element_type=jnp.float32)
            acc_ref[at, :, low:high] = acc_ref[at, :, low:high] * keep + mixed[:HD]
            sum_ref[at, :, low:high] = sum_ref[at, :, low:high] * keep + mixed[HD : HD + 1]

    @pl.when(n > 2)
    def _():
        def body(t, carry):
            for x in range(2):
                step = 2 * t + x
                gather(step, x)
                weigh(step + 1, 1 - x)
                score(step + 2, x)
            return carry

        lax.fori_loop(0, (n + 1) // 2, body, 0)


def fetch(pairs, sems):
    copies = [
        pltpu.make_async_copy(source, target, sems.at[n])
        for n, (source, target) in enumerate(pairs)
    ]
    for copy in copies:
        copy.start()
    return copies


def make_first(base, count):
    def kernel(meta, q_own, acc_own, max_own, sum_own, q1, q2, q3, cos_in, sin_in, *rest):
        kv_in = rest[:count]
        q_ref, acc_ref, max_ref, sum_ref, sems, kv_ref, vt_ref, s_ref, p_ref, top_ref, keep_ref, items = rest[count:]
        copies = fetch([(kv, kv_ref.at[e]) for e, kv in enumerate(kv_in)], sems)
        tiles = q_own.shape[0]
        acc_ref[tiles:] = jnp.zeros_like(acc_ref[tiles:])
        max_ref[tiles:] = jnp.full_like(max_ref[tiles:], NEGATIVE)
        sum_ref[tiles:] = jnp.zeros_like(sum_ref[tiles:])
        q_ref[:tiles] = q_own[...]
        q_ref[PLANE * tiles] = q_own[0]
        acc_ref[:tiles] = acc_own[...]
        max_ref[:tiles] = max_own[...]
        sum_ref[:tiles] = sum_own[...]
        cosines = cos_in[...]
        sines = sin_in[...]
        for i, q_in in enumerate((q1, q2, q3)):
            turn_tiles(q_in, q_ref, (i + 1) * tiles, cosines, sines)
        for copy in copies:
            copy.wait()
        visit(meta, base, count, q_ref, kv_ref, vt_ref, s_ref, p_ref, top_ref, keep_ref, acc_ref, max_ref, sum_ref, items)

    return kernel


def make_middle(base, count):
    def kernel(meta, q_ref, acc_in, max_in, sum_in, *rest):
        kv_in = rest[:count]
        acc_ref, max_ref, sum_ref, sems, kv_ref, vt_ref, s_ref, p_ref, top_ref, keep_ref, items = rest[count:]
        pairs = [(kv, kv_ref.at[e]) for e, kv in enumerate(kv_in)]
        copies = fetch(pairs + [(acc_in, acc_ref)], sems)
        max_ref[...] = max_in[...]
        sum_ref[...] = sum_in[...]
        for copy in copies:
            copy.wait()
        visit(meta, base, count, q_ref, kv_ref, vt_ref, s_ref, p_ref, top_ref, keep_ref, acc_ref, max_ref, sum_ref, items)

    return kernel


def stack(maxima, sums):
    rows = []
    for line in (maxima, sums):
        heads = line.shape[1] // TILE
        rows += [line[:, h * TILE : (h + 1) * TILE] for h in range(heads)]
        rows.append(jnp.zeros((8 - heads, TILE), jnp.float32))
    return jnp.concatenate(rows, axis=0)


def pack(out, at, stats):
    high = stats.astype(jnp.bfloat16)
    left = stats - high.astype(jnp.float32)
    middle = left.astype(jnp.bfloat16)
    low = (left - middle.astype(jnp.float32)).astype(jnp.bfloat16)
    for n, piece in enumerate((high, middle, low)):
        out[at + 16 * n : at + 16 * (n + 1)] = piece


def unpack(part, at):
    pieces = [part[at + 16 * n : at + 16 * (n + 1)].astype(jnp.float32) for n in range(3)]
    stats = pieces[0] + pieces[1] + pieces[2]
    return stats[:8], stats[8:]


def safe(total):
    return jnp.where(total > 0, 1.0 / jnp.where(total > 0, total, 1.0), 0.0)


def make_last(base, count):
    def kernel(meta, q_ref, acc_in, max_in, sum_in, *rest):
        kv_in = rest[:count]
        tiles = (q_ref.shape[0] - 1) // PLANE
        outs = rest[count : count + 5 * tiles]
        acc_ref, max_ref, sum_ref, sems, kv_ref, vt_ref, s_ref, p_ref, top_ref, keep_ref, items = rest[count + 5 * tiles :]
        pairs = [(kv, kv_ref.at[e]) for e, kv in enumerate(kv_in)]
        copies = fetch(pairs + [(acc_in, acc_ref)], sems)
        max_ref[...] = max_in[...]
        sum_ref[...] = sum_in[...]
        for copy in copies:
            copy.wait()
        visit(meta, base, count, q_ref, kv_ref, vt_ref, s_ref, p_ref, top_ref, keep_ref, acc_ref, max_ref, sum_ref, items)
        heads = q_ref.shape[1] // TILE
        for j in range(tiles):
            acc_own, stats_own, acc_two, stats_two, swap = outs[5 * j : 5 * j + 5]
            acc_own[...] = acc_ref[j]
            stats_own[...] = stack(max_ref[j], sum_ref[j])
            two = 2 * tiles + j
            acc_two[...] = acc_ref[two]
            stats_two[...] = stack(max_ref[two], sum_ref[two])
            for slot, i in enumerate((1, 3)):
                at = i * tiles + j
                inverse = safe(sum_ref[at])
                for h in range(heads):
                    lanes = slice(h * TILE, (h + 1) * TILE)
                    swap[slot, h * HD : (h + 1) * HD] = (
                        acc_ref[at, :, lanes] * inverse[:, lanes]
                    ).astype(jnp.bfloat16)
                pack(swap.at[slot], heads * HD, stack(max_ref[at], sum_ref[at]))

    return kernel


def merge_kernel(acc_two, stats_two, swapped, out):
    heads = acc_two.shape[1] // TILE
    other = swapped.at[1]
    max_a, sum_a = stats_two[:8], stats_two[8:]
    max_b, sum_b = unpack(other, heads * HD)
    top = jnp.maximum(max_a, max_b)
    scale_a = jnp.exp2((max_a - top) * RATE)
    mass_b = sum_b * jnp.exp2((max_b - top) * RATE)
    total = sum_a * scale_a + mass_b
    inverse = safe(total)
    share_a = scale_a * inverse
    share_b = mass_b * inverse
    for h in range(heads):
        lanes = slice(h * TILE, (h + 1) * TILE)
        rows = slice(h * HD, (h + 1) * HD)
        value = acc_two[:, lanes] * share_a[h : h + 1]
        value = value + other[rows].astype(jnp.float32) * share_b[h : h + 1]
        out[rows] = value.astype(jnp.bfloat16)
    pack(out, heads * HD, jnp.concatenate([top, total], axis=0))


def make_combine(j):
    def kernel(meta, acc_own, stats_own, swapped, crossed, attn_ref):
        heads = acc_own.shape[1] // TILE
        parts = (swapped.at[0], crossed)
        maxima = [stats_own[:8]]
        sums = [stats_own[8:]]
        for part in parts:
            found = unpack(part, heads * HD)
            maxima.append(found[0])
            sums.append(found[1])
        top = jnp.maximum(jnp.maximum(maxima[0], maxima[1]), maxima[2])
        factor = [jnp.exp2((m - top) * RATE) for m in maxima]
        mass = [f * s for f, s in zip(factor, sums)]
        inverse = safe(mass[0] + mass[1] + mass[2])
        shares = [factor[0] * inverse] + [m * inverse for m in mass[1:]]
        live = lax.broadcasted_iota(jnp.int32, (HD, TILE), 1) + j * TILE < meta[0]
        for h in range(heads):
            lanes = slice(h * TILE, (h + 1) * TILE)
            value = acc_own[:, lanes] * shares[0][h : h + 1]
            for w, part in zip(shares[1:], parts):
                value = value + w[h : h + 1] * part[h * HD : (h + 1) * HD].astype(jnp.float32)
            value = jnp.transpose(jnp.where(live, value, 0.0))
            attn_ref[:, h * HD : (h + 1) * HD] = value.astype(jnp.bfloat16)

    return kernel


def project_kernel(where, attn_near, attn_far, weight_in, mine_in, theirs_in, *rest):
    paths = len(PATHS)
    outs = rest[:paths]
    near_ref, far_ref, sems = rest[paths:]
    columns = near_ref.shape[2]
    tensor, core = where[0], where[1]

    def copy_near(k):
        at = pl.multiple_of((tensor ^ k) * columns, HD)
        return pltpu.make_async_copy(weight_in.at[:, pl.ds(at, columns)], near_ref.at[k], sems.at[0, k])

    def copy_far(k, source):
        at = pl.multiple_of(((tensor ^ k) % 2) * columns, HD)
        return pltpu.make_async_copy(source.at[:, pl.ds(at, columns)], far_ref.at[k], sems.at[1, k])

    for k in PATHS:
        copy_near(k).start()
        same = ((tensor ^ k) % FAR) // 2 == core

        @pl.when(same)
        def _(k=k):
            copy_far(k, mine_in).start()

        @pl.when(jnp.logical_not(same))
        def _(k=k):
            copy_far(k, theirs_in).start()

    for k in PATHS:
        copy_near(k).wait()
        copy_far(k, mine_in).wait()
        total = jnp.dot(attn_near[...], near_ref[k], preferred_element_type=jnp.float32)
        total = total + jnp.dot(attn_far[...], far_ref[k], preferred_element_type=jnp.float32)
        outs[k][...] = total.astype(outs[k].dtype)


def cost(blocks, bytes_accessed):
    pairs = blocks * 1280 * 512
    return pl.CostEstimate(
        flops=4 * pairs * HD, bytes_accessed=bytes_accessed, transcendentals=pairs
    )


def shards(
    suffix_query,
    suffix_key,
    suffix_value,
    prefix_key,
    prefix_value,
    residual,
    out_weight,
    norm_gain,
    lengths,
    request_slot,
    prefix_owner,
    request_group,
):
    slots = suffix_query.shape[0]
    heads = suffix_query.shape[1] // HD
    devices = lax.axis_size("req")
    planes = devices // PLANE
    place = lax.axis_index("req")
    tensor = lax.axis_index("tp")
    ways = lax.axis_size("tp")
    per_group = devices // GROUPS
    block = prefix_key.shape[1]
    part = block // 2
    prefix_length = block * per_group
    bf16 = jnp.bfloat16
    f32 = jnp.float32

    def beside(k):
        return [(i, i ^ k) for i in range(devices)]

    up_pairs = [(i, (i + PLANE) % devices) for i in range(devices)]
    down_pairs = [(i, (i - PLANE) % devices) for i in range(devices)]

    core = place % 2
    width = residual.shape[1]
    columns = width // ways
    where = jnp.stack([tensor, core]).astype(jnp.int32)
    far_side = (tensor // FAR) ^ 1
    outgoing = lax.dynamic_slice_in_dim(
        out_weight, (far_side * FAR + 2 * core) * columns, 2 * columns, 1
    )
    weight_mine = lax.ppermute(outgoing, "tp", [(i, i ^ FAR) for i in range(ways)])
    both = jnp.concatenate([prefix_key, prefix_value], axis=0)
    mine = lax.dynamic_slice_in_dim(both, core * part, part, 1)
    theirs = lax.dynamic_slice_in_dim(both, (1 - core) * part, part, 1)
    lanes = [mine, lax.ppermute(theirs, "req", beside(1))]
    queries = []
    for k in range(1, PLANE):
        queries.append(lax.ppermute(suffix_query, "req", beside(k)))

    entries = {(0, 0): lanes[0], (0, 1): lanes[1]}
    half_way = planes // 2
    for lane in range(2):
        moving_up = lanes[lane]
        moving_down = lanes[lane]
        for step in range(1, half_way):
            moving_up = lax.ppermute(moving_up, "req", up_pairs)
            moving_down = lax.ppermute(moving_down, "req", down_pairs)
            entries[(-step, lane)] = moving_up
            entries[(step, lane)] = moving_down
        if lane == 0:
            entries[(-half_way, 0)] = lax.ppermute(moving_up, "req", up_pairs)
        else:
            entries[(half_way, 1)] = lax.ppermute(moving_down, "req", down_pairs)

    batches = [
        [(0, 0), (0, 1), (-1, 0), (1, 0), (-1, 1), (1, 1)],
        [(-2, 0), (2, 0), (-2, 1), (2, 1)],
        [(-3, 0), (3, 0), (-3, 1), (3, 1)],
        [(-half_way, 0), (half_way, 1)],
    ]
    order = [key for batch in batches for key in batch]

    numbers = jnp.arange(devices, dtype=jnp.int32)
    owner_match = prefix_owner[None, :] == numbers[:, None]
    holder_group = jnp.sum(jnp.where(owner_match, numbers[None, :], 0), axis=1) // per_group
    slot_match = request_slot[:, None] == numbers[None, :]
    asker_group = jnp.sum(jnp.where(slot_match, request_group[:, 0][None, :], 0), axis=1)
    asker_length = jnp.sum(jnp.where(slot_match, lengths[None, :], 0), axis=1)
    nearby = place ^ jnp.arange(PLANE, dtype=jnp.int32)
    near = nearby[:, None] == numbers[None, :]
    near_group = jnp.sum(jnp.where(near, asker_group[None, :], 0), axis=1)
    near_length = jnp.sum(jnp.where(near, asker_length[None, :], 0), axis=1)
    shift = jnp.array([key[0] for key in order], jnp.int32)
    twist = jnp.array([key[1] for key in order], jnp.int32)
    source = ((place // PLANE + shift) % planes) * PLANE + ((place % PLANE) ^ twist)
    from_there = source[:, None] == numbers[None, :]
    source_group = jnp.sum(jnp.where(from_there, holder_group[None, :], 0), axis=1)
    match = (source_group[:, None] == near_group[None, :]).astype(jnp.int32)
    tiles = (near_length + TILE - 1) // TILE
    meta = jnp.concatenate([near_length, tiles, match.reshape(-1)])

    half_dim = HD // 2
    positions = (prefix_length + jnp.arange(slots)).astype(f32)
    frequency = THETA ** (-(jnp.arange(half_dim).astype(f32) * 2.0 / HD))
    angles = positions[:, None] * frequency[None, :]
    cosines = jnp.cos(angles)
    sines = jnp.sin(angles)
    cosines = jnp.concatenate([cosines, cosines], axis=1)
    sines = jnp.concatenate([-sines, sines], axis=1)

    tiles_each = slots // TILE
    shape = jax.ShapeDtypeStruct
    q_own, cache_key, acc_own, max_own, sum_own = pl.pallas_call(
        own_kernel,
        out_shape=(
            shape((tiles_each, heads * TILE, HD), bf16),
            shape((slots, HD), bf16),
            shape((tiles_each, HD, heads * TILE), f32),
        shape((tiles_each, 1, heads * TILE), f32),
        shape((tiles_each, 1, heads * TILE), f32),
    ),
        in_specs=[full(SMEM)] + [full()] * 5,
        out_specs=(full(),) * 5,
        cost_estimate=cost(1, 3 << 20),
        compiler_params=params(),
        name="own",
    )(meta, suffix_query, suffix_key, suffix_value, cosines, sines)

    every = PLANE * tiles_each + 1
    lines = heads * TILE
    state_shapes = (
        shape((every, HD, lines), f32),
        shape((every, 1, lines), f32),
        shape((every, 1, lines), f32),
    )

    def work(count):
        return [
            pltpu.SemaphoreType.DMA((count + 1,)),
            pltpu.VMEM((count, 2, part, HD), bf16),
            pltpu.VMEM((count, HD + 16, part), bf16),
            pltpu.VMEM((2, part, lines), f32),
            pltpu.VMEM((2, part, lines), bf16),
            pltpu.VMEM((2, 1, lines), f32),
            pltpu.VMEM((2, 1, lines), f32),
            pltpu.SMEM((count * PLANE * tiles_each + 6, 2), jnp.int32),
        ]

    base = 0
    parts = [entries[key] for key in batches[0]]
    q_all, *state = pl.pallas_call(
        make_first(base, len(parts)),
        out_shape=(shape((every, lines, HD), bf16),) + state_shapes,
        in_specs=[full(SMEM)] + [full()] * 9 + [full(pl.ANY)] * len(parts),
        out_specs=(full(),) * 4,
        scratch_shapes=work(len(parts)),
        cost_estimate=cost(len(parts), 8 << 20),
        compiler_params=params(),
        name="first",
    )(meta, q_own, acc_own, max_own, sum_own, *queries, cosines, sines, *parts)
    base += len(parts)
    for batch in batches[1:-1]:
        parts = [entries[key] for key in batch]
        state = pl.pallas_call(
            make_middle(base, len(parts)),
            out_shape=state_shapes,
            in_specs=[full(SMEM), full(), full(pl.ANY), full(), full()] + [full(pl.ANY)] * len(parts),
            out_specs=(full(),) * 3,
            scratch_shapes=work(len(parts)),
            cost_estimate=cost(len(parts), 8 << 20),
            compiler_params=params(),
            name="middle",
        )(meta, q_all, *state, *parts)
        base += len(parts)
    parts = [entries[key] for key in batches[-1]]
    packed = heads * HD + 3 * 16
    last = pl.pallas_call(
        make_last(base, len(parts)),
        out_shape=(
            shape((HD, lines), f32),
            shape((16, TILE), f32),
            shape((HD, lines), f32),
            shape((16, TILE), f32),
            shape((2, packed, TILE), bf16),
        )
        * tiles_each,
        in_specs=[full(SMEM), full(), full(pl.ANY), full(), full()] + [full(pl.ANY)] * len(parts),
        out_specs=(full(),) * (5 * tiles_each),
        scratch_shapes=[
            pltpu.VMEM((every, HD, lines), f32),
            pltpu.VMEM((every, 1, lines), f32),
            pltpu.VMEM((every, 1, lines), f32),
        ]
        + work(len(parts)),
        cost_estimate=cost(len(parts), 8 << 20),
        compiler_params=params(),
        name="last",
    )(meta, q_all, *state, *parts)

    swapped = []
    for j in range(tiles_each):
        swapped.append(lax.ppermute(last[5 * j + 4], "req", beside(1)))
    crossed = []
    for j in range(tiles_each):
        merged = pl.pallas_call(
            merge_kernel,
            out_shape=shape((packed, TILE), bf16),
            in_specs=[full()] * 3,
            out_specs=full(),
            cost_estimate=pl.CostEstimate(flops=1 << 20, bytes_accessed=1 << 20, transcendentals=0),
            compiler_params=params(),
            name="merge",
        )(last[5 * j + 2], last[5 * j + 3], swapped[j])
        crossed.append(lax.ppermute(merged, "req", beside(2)))
    near = []
    far = []
    for j in range(tiles_each):
        attn = pl.pallas_call(
            make_combine(j),
            out_shape=shape((TILE, heads * HD), bf16),
            in_specs=[full(SMEM)] + [full()] * 4,
            out_specs=full(),
            cost_estimate=pl.CostEstimate(flops=1 << 20, bytes_accessed=1 << 20, transcendentals=0),
            compiler_params=params(),
            name="combine",
        )(meta, last[5 * j], last[5 * j + 1], swapped[j], crossed[j])
        near.append(attn)
        far.append(lax.ppermute(attn, "tp", [(i, i ^ FAR) for i in range(ways)]))
    weight_theirs = lax.ppermute(weight_mine, "req", beside(1))
    shared = []
    paths = len(PATHS)
    for j in range(tiles_each):
        pieces = pl.pallas_call(
            project_kernel,
            out_shape=tuple(
                shape((TILE, columns), bf16 if k else f32) for k in range(paths)
            ),
            in_specs=[full(SMEM), full(), full()] + [full(pl.ANY)] * 3,
            out_specs=(full(),) * paths,
            scratch_shapes=[
                pltpu.VMEM((paths, heads * HD, columns), bf16),
                pltpu.VMEM((paths, heads * HD, columns), bf16),
                pltpu.SemaphoreType.DMA((2, paths)),
            ],
            cost_estimate=pl.CostEstimate(
                flops=2 * TILE * heads * HD * width,
                bytes_accessed=8 << 20,
                transcendentals=0,
            ),
            compiler_params=params(50),
            name="project",
        )(where, near[j], far[j], out_weight, weight_mine, weight_theirs)
        total = pieces[0]
        for k in range(1, paths):
            piece = lax.ppermute(pieces[k], "tp", [(i, i ^ k) for i in range(ways)])
            total = total + piece.astype(f32)
        shared.append(total)
    shared = jnp.concatenate(shared, axis=0)
    own_residual = lax.dynamic_slice_in_dim(residual, tensor * columns, columns, 1)
    hidden = (own_residual.astype(f32) + shared).astype(bf16)
    widened = hidden.astype(f32)
    squares = jnp.sum(widened * widened, axis=1).reshape(slots // HD, HD)
    squares = jnp.pad(squares, ((0, 8 - slots // HD), (0, 0)))
    spread = lax.all_to_all(jnp.broadcast_to(squares[None], (ways, 8, HD)), "tp", 0, 0)
    row_squares = jnp.sum(spread, axis=0)[: slots // HD].reshape(slots)
    scale_rows = lax.rsqrt(row_squares / width + EPSILON)
    normed = (widened * scale_rows[:, None] * norm_gain.astype(f32)[None, :]).astype(bf16)
    return (hidden, normed, cache_key)


def solution(mesh):
    return jax.shard_map(
        shards,
        mesh=mesh,
        in_specs=(
            P("req", "tp"),
            P("req", "tp"),
            P("req", "tp"),
            P("req", None, "tp"),
            P("req", None, "tp"),
            P("req", None),
            P("tp", None),
            P("tp"),
            P(),
            P(),
            P(),
            P(),
        ),
        out_specs=(P("req", "tp"), P("req", "tp"), P("req", "tp")),
        check_vma=False,
    )
```

```python
import jax
import jax.numpy as jnp
from jax import lax
from jax.experimental import pallas as pl
from jax.experimental.pallas import tpu as pltpu
from jax.sharding import PartitionSpec as P


HD = 128
GROUPS = 4
PLANE = 4
TILE = 128
THETA = 1000000.0
NEGATIVE = -1e30
EPSILON = 1e-06
LOG2E = 1.4426950408889634
PATHS = (2, 3, 1, 0)
FAR = 4
LIMIT = 50


SMEM = pltpu.SMEM
VMEM = pltpu.VMEM


def full(space=VMEM):
    return pl.BlockSpec(memory_space=space)


def params(limit=18):
    return pltpu.CompilerParams(vmem_limit_bytes=limit * 1024 * 1024)


RATE = HD ** (-0.5) * LOG2E
NT = (((1,), (1,)), ((), ()))


def turn(x, cosines, sines):
    return x * cosines + pltpu.roll(x, HD // 2, 1) * sines


def turn_tiles(q_in, q_ref, at, cosines, sines):
    for j in range(q_in.shape[0] // TILE):
        rows = slice(j * TILE, (j + 1) * TILE)
        for h in range(q_ref.shape[1] // TILE):
            x = q_in[rows, h * HD : (h + 1) * HD].astype(jnp.float32)
            q_ref[at + j, h * TILE : (h + 1) * TILE] = turn(x, cosines[rows], sines[rows]).astype(
                jnp.bfloat16
            )


def spans(width):
    return [(low, min(low + 2 * TILE, width)) for low in range(0, width, 2 * TILE)]


def own_kernel(meta, q_in, k_in, v_in, cos_in, sin_in, q_out, key_out, acc_ref, max_ref, sum_ref):
    tiles, lines = q_out.shape[:2]
    slots = k_in.shape[0]
    length = meta[0]
    cosines = cos_in[...]
    sines = sin_in[...]
    turn_tiles(q_in, q_out, 0, cosines, sines)
    turned = turn(k_in[...].astype(jnp.float32), cosines, sines)
    place = lax.broadcasted_iota(jnp.int32, turned.shape, 0)
    key_out[...] = jnp.where(place < length, turned, 0.0).astype(jnp.bfloat16)
    k = key_out[...]
    v = v_in[...].T
    u = lax.broadcasted_iota(jnp.int32, (slots, TILE), 0)
    t = lax.broadcasted_iota(jnp.int32, (slots, TILE), 1)
    for j in range(tiles):
        visible = (u <= t + j * TILE) & (u < length)
        for low in range(0, lines, TILE):
            high = low + TILE
            scores = lax.dot_general(
                k, q_out[j, low:high], NT, preferred_element_type=jnp.float32
            )
            scores = jnp.where(visible, scores, NEGATIVE)
            top = jnp.max(scores, axis=0, keepdims=True)
            weights = jnp.exp2((scores - top) * RATE)
            max_ref[j, :, low:high] = top
            sum_ref[j, :, low:high] = jnp.sum(weights, axis=0, keepdims=True)
            acc_ref[j, :, low:high] = jnp.dot(
                v, weights.astype(jnp.bfloat16), preferred_element_type=jnp.float32
            )


def visit(meta, base, count, q_ref, kv_ref, vt_ref, s_ref, p_ref, top_ref, keep_ref, acc_ref, max_ref, sum_ref, items):
    spare = q_ref.shape[0] - 1
    tiles = spare // PLANE
    part = kv_ref.shape[2]
    cuts = spans(q_ref.shape[1])
    for e in range(count):
        vt_ref[e, :HD] = kv_ref[e, 1].T
        vt_ref[e, HD:] = jnp.ones((16, part), jnp.bfloat16)
    for x in range(2):
        items[x, 0] = 0
        items[x, 1] = spare
    n = jnp.int32(2)
    for e in range(count):
        for i in range(PLANE):
            for j in range(tiles):
                live = (meta[2 * PLANE + (base + e) * PLANE + i] == 1) & (j < meta[PLANE + i])

                @pl.when(live)
                def _(n=n, e=e, i=i, j=j):
                    items[n, 0] = e
                    items[n, 1] = i * tiles + j

                n = n + live.astype(jnp.int32)
    for x in range(4):
        items[n + x, 0] = 0
        items[n + x, 1] = spare

    def score(step, slot):
        k = kv_ref[items[step, 0], 0]
        at = items[step, 1]
        for low, high in cuts:
            scores = lax.dot_general(
                k, q_ref[at, low:high], NT, preferred_element_type=jnp.float32
            )
            s_ref[slot, :, low:high] = scores
            top_ref[slot, :, low:high] = jnp.max(scores, axis=0, keepdims=True)

    def weigh(step, slot):
        at = items[step, 1]
        old = max_ref[at]
        new = jnp.maximum(old, top_ref[slot])
        max_ref[at] = new
        keep_ref[slot] = jnp.exp2((old - new) * RATE)
        for low, high in cuts:
            p_ref[slot, :, low:high] = jnp.exp2(
                (s_ref[slot, :, low:high] - new[:, low:high]) * RATE
            ).astype(jnp.bfloat16)

    def gather(step, slot):
        v = vt_ref[items[step, 0]]
        at = items[step, 1]
        for low, high in cuts:
            keep = keep_ref[slot, :, low:high]
            mixed = jnp.dot(v, p_ref[slot, :, low:high], preferred_element_type=jnp.float32)
            acc_ref[at, :, low:high] = acc_ref[at, :, low:high] * keep + mixed[:HD]
            sum_ref[at, :, low:high] = sum_ref[at, :, low:high] * keep + mixed[HD : HD + 1]

    @pl.when(n > 2)
    def _():
        def body(t, carry):
            for x in range(2):
                step = 2 * t + x
                gather(step, x)
                weigh(step + 1, 1 - x)
                score(step + 2, x)
            return carry

        lax.fori_loop(0, (n + 1) // 2, body, 0)


def fetch(pairs, sems):
    copies = [
        pltpu.make_async_copy(source, target, sems.at[n])
        for n, (source, target) in enumerate(pairs)
    ]
    for copy in copies:
        copy.start()
    return copies


def make_first(base, count):
    def kernel(meta, q_own, acc_own, max_own, sum_own, q1, q2, q3, cos_in, sin_in, *rest):
        kv_in = rest[:count]
        q_ref, acc_ref, max_ref, sum_ref, sems, kv_ref, vt_ref, s_ref, p_ref, top_ref, keep_ref, items = rest[count:]
        copies = fetch([(kv, kv_ref.at[e]) for e, kv in enumerate(kv_in)], sems)
        tiles = q_own.shape[0]
        acc_ref[tiles:] = jnp.zeros_like(acc_ref[tiles:])
        max_ref[tiles:] = jnp.full_like(max_ref[tiles:], NEGATIVE)
        sum_ref[tiles:] = jnp.zeros_like(sum_ref[tiles:])
        q_ref[:tiles] = q_own[...]
        q_ref[PLANE * tiles] = q_own[0]
        acc_ref[:tiles] = acc_own[...]
        max_ref[:tiles] = max_own[...]
        sum_ref[:tiles] = sum_own[...]
        cosines = cos_in[...]
        sines = sin_in[...]
        for i, q_in in enumerate((q1, q2, q3)):
            turn_tiles(q_in, q_ref, (i + 1) * tiles, cosines, sines)
        for copy in copies:
            copy.wait()
        visit(meta, base, count, q_ref, kv_ref, vt_ref, s_ref, p_ref, top_ref, keep_ref, acc_ref, max_ref, sum_ref, items)

    return kernel


def make_middle(base, count):
    def kernel(meta, q_ref, acc_in, max_in, sum_in, *rest):
        kv_in = rest[:count]
        acc_ref, max_ref, sum_ref, sems, kv_ref, vt_ref, s_ref, p_ref, top_ref, keep_ref, items = rest[count:]
        pairs = [(kv, kv_ref.at[e]) for e, kv in enumerate(kv_in)]
        copies = fetch(pairs + [(acc_in, acc_ref)], sems)
        max_ref[...] = max_in[...]
        sum_ref[...] = sum_in[...]
        for copy in copies:
            copy.wait()
        visit(meta, base, count, q_ref, kv_ref, vt_ref, s_ref, p_ref, top_ref, keep_ref, acc_ref, max_ref, sum_ref, items)

    return kernel


def stack(maxima, sums):
    rows = []
    for line in (maxima, sums):
        heads = line.shape[1] // TILE
        rows += [line[:, h * TILE : (h + 1) * TILE] for h in range(heads)]
        rows.append(jnp.zeros((8 - heads, TILE), jnp.float32))
    return jnp.concatenate(rows, axis=0)


def pack(out, at, stats):
    high = stats.astype(jnp.bfloat16)
    left = stats - high.astype(jnp.float32)
    middle = left.astype(jnp.bfloat16)
    low = (left - middle.astype(jnp.float32)).astype(jnp.bfloat16)
    for n, piece in enumerate((high, middle, low)):
        out[at + 16 * n : at + 16 * (n + 1)] = piece


def unpack(part, at):
    pieces = [part[at + 16 * n : at + 16 * (n + 1)].astype(jnp.float32) for n in range(3)]
    stats = pieces[0] + pieces[1] + pieces[2]
    return stats[:8], stats[8:]


def safe(total):
    return jnp.where(total > 0, 1.0 / jnp.where(total > 0, total, 1.0), 0.0)


def make_last(base, count):
    def kernel(meta, q_ref, acc_in, max_in, sum_in, *rest):
        kv_in = rest[:count]
        tiles = (q_ref.shape[0] - 1) // PLANE
        outs = rest[count : count + 5 * tiles]
        acc_ref, max_ref, sum_ref, sems, kv_ref, vt_ref, s_ref, p_ref, top_ref, keep_ref, items = rest[count + 5 * tiles :]
        pairs = [(kv, kv_ref.at[e]) for e, kv in enumerate(kv_in)]
        copies = fetch(pairs + [(acc_in, acc_ref)], sems)
        max_ref[...] = max_in[...]
        sum_ref[...] = sum_in[...]
        for copy in copies:
            copy.wait()
        visit(meta, base, count, q_ref, kv_ref, vt_ref, s_ref, p_ref, top_ref, keep_ref, acc_ref, max_ref, sum_ref, items)
        heads = q_ref.shape[1] // TILE
        for j in range(tiles):
            acc_own, stats_own, acc_two, stats_two, swap = outs[5 * j : 5 * j + 5]
            acc_own[...] = acc_ref[j]
            stats_own[...] = stack(max_ref[j], sum_ref[j])
            two = 2 * tiles + j
            acc_two[...] = acc_ref[two]
            stats_two[...] = stack(max_ref[two], sum_ref[two])
            for slot, i in enumerate((1, 3)):
                at = i * tiles + j
                inverse = safe(sum_ref[at])
                for h in range(heads):
                    lanes = slice(h * TILE, (h + 1) * TILE)
                    swap[slot, h * HD : (h + 1) * HD] = (
                        acc_ref[at, :, lanes] * inverse[:, lanes]
                    ).astype(jnp.bfloat16)
                pack(swap.at[slot], heads * HD, stack(max_ref[at], sum_ref[at]))

    return kernel


def merge_kernel(acc_two, stats_two, swapped, out):
    heads = acc_two.shape[1] // TILE
    other = swapped.at[1]
    max_a, sum_a = stats_two[:8], stats_two[8:]
    max_b, sum_b = unpack(other, heads * HD)
    top = jnp.maximum(max_a, max_b)
    scale_a = jnp.exp2((max_a - top) * RATE)
    mass_b = sum_b * jnp.exp2((max_b - top) * RATE)
    total = sum_a * scale_a + mass_b
    inverse = safe(total)
    share_a = scale_a * inverse
    share_b = mass_b * inverse
    for h in range(heads):
        lanes = slice(h * TILE, (h + 1) * TILE)
        rows = slice(h * HD, (h + 1) * HD)
        value = acc_two[:, lanes] * share_a[h : h + 1]
        value = value + other[rows].astype(jnp.float32) * share_b[h : h + 1]
        out[rows] = value.astype(jnp.bfloat16)
    pack(out, heads * HD, jnp.concatenate([top, total], axis=0))


def make_combine(j):
    def kernel(meta, acc_own, stats_own, swapped, crossed, attn_ref):
        heads = acc_own.shape[1] // TILE
        parts = (swapped.at[0], crossed)
        maxima = [stats_own[:8]]
        sums = [stats_own[8:]]
        for part in parts:
            found = unpack(part, heads * HD)
            maxima.append(found[0])
            sums.append(found[1])
        top = jnp.maximum(jnp.maximum(maxima[0], maxima[1]), maxima[2])
        factor = [jnp.exp2((m - top) * RATE) for m in maxima]
        mass = [f * s for f, s in zip(factor, sums)]
        inverse = safe(mass[0] + mass[1] + mass[2])
        shares = [factor[0] * inverse] + [m * inverse for m in mass[1:]]
        live = lax.broadcasted_iota(jnp.int32, (HD, TILE), 1) + j * TILE < meta[0]
        for h in range(heads):
            lanes = slice(h * TILE, (h + 1) * TILE)
            value = acc_own[:, lanes] * shares[0][h : h + 1]
            for w, part in zip(shares[1:], parts):
                value = value + w[h : h + 1] * part[h * HD : (h + 1) * HD].astype(jnp.float32)
            value = jnp.transpose(jnp.where(live, value, 0.0))
            attn_ref[:, h * HD : (h + 1) * HD] = value.astype(jnp.bfloat16)

    return kernel


def near_kernel(where, attn_near, weight_in, *rest):
    paths = len(PATHS)
    outs = rest[:paths]
    near_ref, sems = rest[paths:]
    columns = near_ref.shape[2]
    copies = {}
    for k in PATHS:
        at = pl.multiple_of((where[0] ^ k) * columns, HD)
        copies[k] = pltpu.make_async_copy(
            weight_in.at[:, pl.ds(at, columns)], near_ref.at[k], sems.at[k]
        )
        copies[k].start()
    for k in PATHS:
        copies[k].wait()
        outs[k][...] = jnp.dot(attn_near[...], near_ref[k], preferred_element_type=jnp.float32)


def far_kernel(where, attn_far, mine_in, theirs_in, *rest):
    paths = len(PATHS)
    sums = rest[:paths]
    outs = rest[paths : 2 * paths]
    far_ref, sems = rest[2 * paths :]
    columns = far_ref.shape[2]
    tensor, core = where[0], where[1]

    def copy_far(k, source):
        at = pl.multiple_of(((tensor ^ k) % 2) * columns, HD)
        return pltpu.make_async_copy(source.at[:, pl.ds(at, columns)], far_ref.at[k], sems.at[k])

    for k in PATHS:
        same = ((tensor ^ k) % FAR) // 2 == core

        @pl.when(same)
        def _(k=k):
            copy_far(k, mine_in).start()

        @pl.when(jnp.logical_not(same))
        def _(k=k):
            copy_far(k, theirs_in).start()

    for k in PATHS:
        copy_far(k, mine_in).wait()
        total = sums[k][...] + jnp.dot(
            attn_far[...], far_ref[k], preferred_element_type=jnp.float32
        )
        outs[k][...] = total.astype(outs[k].dtype)


def cost(blocks, bytes_accessed):
    pairs = blocks * 1280 * 512
    return pl.CostEstimate(
        flops=4 * pairs * HD, bytes_accessed=bytes_accessed, transcendentals=pairs
    )


def shards(
    suffix_query,
    suffix_key,
    suffix_value,
    prefix_key,
    prefix_value,
    residual,
    out_weight,
    norm_gain,
    lengths,
    request_slot,
    prefix_owner,
    request_group,
):
    slots = suffix_query.shape[0]
    heads = suffix_query.shape[1] // HD
    devices = lax.axis_size("req")
    planes = devices // PLANE
    place = lax.axis_index("req")
    tensor = lax.axis_index("tp")
    ways = lax.axis_size("tp")
    per_group = devices // GROUPS
    block = prefix_key.shape[1]
    part = block // 2
    prefix_length = block * per_group
    bf16 = jnp.bfloat16
    f32 = jnp.float32

    def beside(k):
        return [(i, i ^ k) for i in range(devices)]

    up_pairs = [(i, (i + PLANE) % devices) for i in range(devices)]
    down_pairs = [(i, (i - PLANE) % devices) for i in range(devices)]

    core = place % 2
    width = residual.shape[1]
    columns = width // ways
    where = jnp.stack([tensor, core]).astype(jnp.int32)
    far_side = (tensor // FAR) ^ 1
    outgoing = lax.dynamic_slice_in_dim(
        out_weight, (far_side * FAR + 2 * core) * columns, 2 * columns, 1
    )
    weight_mine = lax.ppermute(outgoing, "tp", [(i, i ^ FAR) for i in range(ways)])

    def half(which):
        cut = [
            lax.dynamic_slice_in_dim(x, which * part, part, 1) for x in (prefix_key, prefix_value)
        ]
        return jnp.concatenate(cut, axis=0)

    theirs = half(1 - core)
    swapped_half = lax.ppermute(theirs, "req", beside(1))
    lanes = [half(core), swapped_half]
    queries = []
    for k in range(1, PLANE):
        queries.append(lax.ppermute(suffix_query, "req", beside(k)))

    entries = {(0, 0): lanes[0], (0, 1): lanes[1]}
    half_way = planes // 2
    for lane in range(2):
        moving_up = lanes[lane]
        moving_down = lanes[lane]
        for step in range(1, half_way):
            moving_up = lax.ppermute(moving_up, "req", up_pairs)
            moving_down = lax.ppermute(moving_down, "req", down_pairs)
            entries[(-step, lane)] = moving_up
            entries[(step, lane)] = moving_down
        if lane == 0:
            entries[(-half_way, 0)] = lax.ppermute(moving_up, "req", up_pairs)
        else:
            entries[(half_way, 1)] = lax.ppermute(moving_down, "req", down_pairs)

    batches = [
        [(0, 0), (0, 1), (-1, 0), (1, 0), (-1, 1), (1, 1)],
        [(-2, 0), (2, 0), (-2, 1), (2, 1)],
        [(-3, 0), (3, 0), (-3, 1), (3, 1)],
        [(-half_way, 0), (half_way, 1)],
    ]
    order = [key for batch in batches for key in batch]

    numbers = jnp.arange(devices, dtype=jnp.int32)
    owner_match = prefix_owner[None, :] == numbers[:, None]
    holder_group = jnp.sum(jnp.where(owner_match, numbers[None, :], 0), axis=1) // per_group
    slot_match = request_slot[:, None] == numbers[None, :]
    asker_group = jnp.sum(jnp.where(slot_match, request_group[:, 0][None, :], 0), axis=1)
    asker_length = jnp.sum(jnp.where(slot_match, lengths[None, :], 0), axis=1)
    nearby = place ^ jnp.arange(PLANE, dtype=jnp.int32)
    near = nearby[:, None] == numbers[None, :]
    near_group = jnp.sum(jnp.where(near, asker_group[None, :], 0), axis=1)
    near_length = jnp.sum(jnp.where(near, asker_length[None, :], 0), axis=1)
    shift = jnp.array([key[0] for key in order], jnp.int32)
    twist = jnp.array([key[1] for key in order], jnp.int32)
    source = ((place // PLANE + shift) % planes) * PLANE + ((place % PLANE) ^ twist)
    from_there = source[:, None] == numbers[None, :]
    source_group = jnp.sum(jnp.where(from_there, holder_group[None, :], 0), axis=1)
    match = (source_group[:, None] == near_group[None, :]).astype(jnp.int32)
    tiles = (near_length + TILE - 1) // TILE
    meta = jnp.concatenate([near_length, tiles, match.reshape(-1)])

    half_dim = HD // 2
    positions = (prefix_length + jnp.arange(slots)).astype(f32)
    frequency = THETA ** (-(jnp.arange(half_dim).astype(f32) * 2.0 / HD))
    angles = positions[:, None] * frequency[None, :]
    cosines = jnp.cos(angles)
    sines = jnp.sin(angles)
    cosines = jnp.concatenate([cosines, cosines], axis=1)
    sines = jnp.concatenate([-sines, sines], axis=1)

    tiles_each = slots // TILE
    shape = jax.ShapeDtypeStruct
    q_own, cache_key, acc_own, max_own, sum_own = pl.pallas_call(
        own_kernel,
        out_shape=(
            shape((tiles_each, heads * TILE, HD), bf16),
            shape((slots, HD), bf16),
            shape((tiles_each, HD, heads * TILE), f32),
        shape((tiles_each, 1, heads * TILE), f32),
        shape((tiles_each, 1, heads * TILE), f32),
    ),
        in_specs=[full(SMEM)] + [full()] * 5,
        out_specs=(full(),) * 5,
        cost_estimate=cost(1, 3 << 20),
        compiler_params=params(),
        name="own",
    )(meta, suffix_query, suffix_key, suffix_value, cosines, sines)

    every = PLANE * tiles_each + 1
    lines = heads * TILE
    state_shapes = (
        shape((every, HD, lines), f32),
        shape((every, 1, lines), f32),
        shape((every, 1, lines), f32),
    )

    def work(count):
        return [
            pltpu.SemaphoreType.DMA((count + 1,)),
            pltpu.VMEM((count, 2, part, HD), bf16),
            pltpu.VMEM((count, HD + 16, part), bf16),
            pltpu.VMEM((2, part, lines), f32),
            pltpu.VMEM((2, part, lines), bf16),
            pltpu.VMEM((2, 1, lines), f32),
            pltpu.VMEM((2, 1, lines), f32),
            pltpu.SMEM((count * PLANE * tiles_each + 6, 2), jnp.int32),
        ]

    base = 0
    parts = [entries[key] for key in batches[0]]
    q_all, *state = pl.pallas_call(
        make_first(base, len(parts)),
        out_shape=(shape((every, lines, HD), bf16),) + state_shapes,
        in_specs=[full(SMEM)] + [full()] * 9 + [full(pl.ANY)] * len(parts),
        out_specs=(full(),) * 4,
        scratch_shapes=work(len(parts)),
        cost_estimate=cost(len(parts), 8 << 20),
        compiler_params=params(),
        name="first",
    )(meta, q_own, acc_own, max_own, sum_own, *queries, cosines, sines, *parts)
    base += len(parts)
    for batch in batches[1:-1]:
        parts = [entries[key] for key in batch]
        state = pl.pallas_call(
            make_middle(base, len(parts)),
            out_shape=state_shapes,
            in_specs=[full(SMEM), full(), full(pl.ANY), full(), full()] + [full(pl.ANY)] * len(parts),
            out_specs=(full(),) * 3,
            scratch_shapes=work(len(parts)),
            cost_estimate=cost(len(parts), 8 << 20),
            compiler_params=params(),
            name="middle",
        )(meta, q_all, *state, *parts)
        base += len(parts)
    parts = [entries[key] for key in batches[-1]]
    packed = heads * HD + 3 * 16
    last = pl.pallas_call(
        make_last(base, len(parts)),
        out_shape=(
            shape((HD, lines), f32),
            shape((16, TILE), f32),
            shape((HD, lines), f32),
            shape((16, TILE), f32),
            shape((2, packed, TILE), bf16),
        )
        * tiles_each,
        in_specs=[full(SMEM), full(), full(pl.ANY), full(), full()] + [full(pl.ANY)] * len(parts),
        out_specs=(full(),) * (5 * tiles_each),
        scratch_shapes=[
            pltpu.VMEM((every, HD, lines), f32),
            pltpu.VMEM((every, 1, lines), f32),
            pltpu.VMEM((every, 1, lines), f32),
        ]
        + work(len(parts)),
        cost_estimate=cost(len(parts), 8 << 20),
        compiler_params=params(),
        name="last",
    )(meta, q_all, *state, *parts)

    swapped = []
    for j in range(tiles_each):
        swapped.append(lax.ppermute(last[5 * j + 4], "req", beside(1)))
    crossed = []
    for j in range(tiles_each):
        merged = pl.pallas_call(
            merge_kernel,
            out_shape=shape((packed, TILE), bf16),
            in_specs=[full()] * 3,
            out_specs=full(),
            cost_estimate=pl.CostEstimate(flops=1 << 20, bytes_accessed=1 << 20, transcendentals=0),
            compiler_params=params(),
            name="merge",
        )(last[5 * j + 2], last[5 * j + 3], swapped[j])
        crossed.append(lax.ppermute(merged, "req", beside(2)))
    near = []
    far = []
    for j in range(tiles_each):
        attn = pl.pallas_call(
            make_combine(j),
            out_shape=shape((TILE, heads * HD), bf16),
            in_specs=[full(SMEM)] + [full()] * 4,
            out_specs=full(),
            cost_estimate=pl.CostEstimate(flops=1 << 20, bytes_accessed=1 << 20, transcendentals=0),
            compiler_params=params(),
            name="combine",
        )(meta, last[5 * j], last[5 * j + 1], swapped[j], crossed[j])
        near.append(attn)
        far.append(lax.ppermute(attn, "tp", [(i, i ^ FAR) for i in range(ways)]))
    weight_theirs = lax.ppermute(weight_mine, "req", beside(1))
    shared = []
    paths = len(PATHS)
    estimate = pl.CostEstimate(
        flops=TILE * heads * HD * width, bytes_accessed=4 << 20, transcendentals=0
    )
    begun = []
    for j in range(tiles_each):
        begun.append(
            pl.pallas_call(
                near_kernel,
                out_shape=(shape((TILE, columns), f32),) * paths,
                in_specs=[full(SMEM), full(), full(pl.ANY)],
                out_specs=(full(),) * paths,
                scratch_shapes=[
                    pltpu.VMEM((paths, heads * HD, columns), bf16),
                    pltpu.SemaphoreType.DMA((paths,)),
                ],
                cost_estimate=estimate,
                compiler_params=params(LIMIT),
                name="near",
            )(where, near[j], out_weight)
        )
    for j in range(tiles_each):
        pieces = pl.pallas_call(
            far_kernel,
            out_shape=tuple(
                shape((TILE, columns), bf16 if k else f32) for k in range(paths)
            ),
            in_specs=[full(SMEM), full()] + [full(pl.ANY)] * 2 + [full()] * paths,
            out_specs=(full(),) * paths,
            scratch_shapes=[
                pltpu.VMEM((paths, heads * HD, columns), bf16),
                pltpu.SemaphoreType.DMA((paths,)),
            ],
            cost_estimate=estimate,
            compiler_params=params(16),
            name="project",
        )(where, far[j], weight_mine, weight_theirs, *begun[j])
        total = pieces[0]
        for k in range(1, paths):
            piece = lax.ppermute(pieces[k], "tp", [(i, i ^ k) for i in range(ways)])
            total = total + piece.astype(f32)
        shared.append(total)
    shared = jnp.concatenate(shared, axis=0)
    own_residual = lax.dynamic_slice_in_dim(residual, tensor * columns, columns, 1)
    hidden = (own_residual.astype(f32) + shared).astype(bf16)
    widened = hidden.astype(f32)
    squares = jnp.sum(widened * widened, axis=1).reshape(slots // HD, HD)
    squares = jnp.pad(squares, ((0, 8 - slots // HD), (0, 0)))
    spread = lax.all_to_all(jnp.broadcast_to(squares[None], (ways, 8, HD)), "tp", 0, 0)
    row_squares = jnp.sum(spread, axis=0)[: slots // HD].reshape(slots)
    scale_rows = lax.rsqrt(row_squares / width + EPSILON)
    normed = (widened * scale_rows[:, None] * norm_gain.astype(f32)[None, :]).astype(bf16)
    return (hidden, normed, cache_key)


def solution(mesh):
    return jax.shard_map(
        shards,
        mesh=mesh,
        in_specs=(
            P("req", "tp"),
            P("req", "tp"),
            P("req", "tp"),
            P("req", None, "tp"),
            P("req", None, "tp"),
            P("req", None),
            P("tp", None),
            P("tp"),
            P(),
            P(),
            P(),
            P(),
        ),
        out_specs=(P("req", "tp"), P("req", "tp"), P("req", "tp")),
        check_vma=False,
    )
```

```python
import jax
import jax.numpy as jnp
from jax import lax
from jax.experimental import pallas as pl
from jax.experimental.pallas import tpu as pltpu
from jax.sharding import PartitionSpec as P


HD = 128
GROUPS = 4
PLANE = 4
TILE = 128
THETA = 1000000.0
NEGATIVE = -1e30
EPSILON = 1e-06
LOG2E = 1.4426950408889634
PATHS = (2, 3, 1, 0)
FAR = 4


SMEM = pltpu.SMEM
VMEM = pltpu.VMEM


def full(space=VMEM):
    return pl.BlockSpec(memory_space=space)


def params(limit=26):
    return pltpu.CompilerParams(vmem_limit_bytes=limit * 1024 * 1024)


RATE = HD ** (-0.5) * LOG2E
NT = (((1,), (1,)), ((), ()))


def turn(x, cosines, sines):
    return x * cosines + pltpu.roll(x, HD // 2, 1) * sines


def turn_tiles(q_in, q_ref, at, cosines, sines):
    for j in range(q_in.shape[0] // TILE):
        rows = slice(j * TILE, (j + 1) * TILE)
        for h in range(q_ref.shape[1] // TILE):
            x = q_in[rows, h * HD : (h + 1) * HD].astype(jnp.float32)
            q_ref[at + j, h * TILE : (h + 1) * TILE] = turn(x, cosines[rows], sines[rows]).astype(
                jnp.bfloat16
            )


def spans(width):
    return [(low, min(low + 2 * TILE, width)) for low in range(0, width, 2 * TILE)]


def own_kernel(meta, q_in, k_in, v_in, cos_in, sin_in, q_out, key_out, acc_ref, max_ref, sum_ref):
    tiles, lines = q_out.shape[:2]
    slots = k_in.shape[0]
    length = meta[0]
    cosines = cos_in[...]
    sines = sin_in[...]
    turn_tiles(q_in, q_out, 0, cosines, sines)
    turned = turn(k_in[...].astype(jnp.float32), cosines, sines)
    place = lax.broadcasted_iota(jnp.int32, turned.shape, 0)
    key_out[...] = jnp.where(place < length, turned, 0.0).astype(jnp.bfloat16)
    k = key_out[...]
    v = v_in[...].T
    u = lax.broadcasted_iota(jnp.int32, (slots, TILE), 0)
    t = lax.broadcasted_iota(jnp.int32, (slots, TILE), 1)
    for j in range(tiles):
        visible = (u <= t + j * TILE) & (u < length)
        for low in range(0, lines, TILE):
            high = low + TILE
            scores = lax.dot_general(
                k, q_out[j, low:high], NT, preferred_element_type=jnp.float32
            )
            scores = jnp.where(visible, scores, NEGATIVE)
            top = jnp.max(scores, axis=0, keepdims=True)
            weights = jnp.exp2((scores - top) * RATE)
            max_ref[j, :, low:high] = top
            sum_ref[j, :, low:high] = jnp.sum(weights, axis=0, keepdims=True)
            acc_ref[j, :, low:high] = jnp.dot(
                v, weights.astype(jnp.bfloat16), preferred_element_type=jnp.float32
            )


def visit(meta, base, count, q_ref, kv_ref, vt_ref, s_ref, p_ref, top_ref, keep_ref, acc_ref, max_ref, sum_ref, items):
    spare = q_ref.shape[0] - 1
    tiles = spare // PLANE
    part = kv_ref.shape[2]
    cuts = spans(q_ref.shape[1])
    for e in range(count):
        vt_ref[e, :HD] = kv_ref[e, 1].T
        vt_ref[e, HD:] = jnp.ones((16, part), jnp.bfloat16)
    for x in range(2):
        items[x, 0] = 0
        items[x, 1] = spare
    n = jnp.int32(2)
    for e in range(count):
        for i in range(PLANE):
            for j in range(tiles):
                live = (meta[2 * PLANE + (base + e) * PLANE + i] == 1) & (j < meta[PLANE + i])

                @pl.when(live)
                def _(n=n, e=e, i=i, j=j):
                    items[n, 0] = e
                    items[n, 1] = i * tiles + j

                n = n + live.astype(jnp.int32)
    for x in range(4):
        items[n + x, 0] = 0
        items[n + x, 1] = spare

    def score(step, slot):
        k = kv_ref[items[step, 0], 0]
        at = items[step, 1]
        for low, high in cuts:
            scores = lax.dot_general(
                k, q_ref[at, low:high], NT, preferred_element_type=jnp.float32
            )
            s_ref[slot, :, low:high] = scores
            top_ref[slot, :, low:high] = jnp.max(scores, axis=0, keepdims=True)

    def weigh(step, slot):
        at = items[step, 1]
        old = max_ref[at]
        new = jnp.maximum(old, top_ref[slot])
        max_ref[at] = new
        keep_ref[slot] = jnp.exp2((old - new) * RATE)
        for low, high in cuts:
            p_ref[slot, :, low:high] = jnp.exp2(
                (s_ref[slot, :, low:high] - new[:, low:high]) * RATE
            ).astype(jnp.bfloat16)

    def gather(step, slot):
        v = vt_ref[items[step, 0]]
        at = items[step, 1]
        for low, high in cuts:
            keep = keep_ref[slot, :, low:high]
            mixed = jnp.dot(v, p_ref[slot, :, low:high], preferred_element_type=jnp.float32)
            acc_ref[at, :, low:high] = acc_ref[at, :, low:high] * keep + mixed[:HD]
            sum_ref[at, :, low:high] = sum_ref[at, :, low:high] * keep + mixed[HD : HD + 1]

    @pl.when(n > 2)
    def _():
        def body(t, carry):
            for x in range(2):
                step = 2 * t + x
                gather(step, x)
                weigh(step + 1, 1 - x)
                score(step + 2, x)
            return carry

        lax.fori_loop(0, (n + 1) // 2, body, 0)


def fetch(pairs, sems):
    copies = [
        pltpu.make_async_copy(source, target, sems.at[n])
        for n, (source, target) in enumerate(pairs)
    ]
    for copy in copies:
        copy.start()
    return copies


def make_first(base, count):
    def kernel(meta, q_own, acc_own, max_own, sum_own, q1, q2, q3, cos_in, sin_in, *rest):
        kv_in = rest[:count]
        q_ref, acc_ref, max_ref, sum_ref, sems, kv_ref, vt_ref, s_ref, p_ref, top_ref, keep_ref, items = rest[count:]
        copies = fetch([(kv, kv_ref.at[e]) for e, kv in enumerate(kv_in)], sems)
        tiles = q_own.shape[0]
        acc_ref[tiles:] = jnp.zeros_like(acc_ref[tiles:])
        max_ref[tiles:] = jnp.full_like(max_ref[tiles:], NEGATIVE)
        sum_ref[tiles:] = jnp.zeros_like(sum_ref[tiles:])
        q_ref[:tiles] = q_own[...]
        q_ref[PLANE * tiles] = q_own[0]
        acc_ref[:tiles] = acc_own[...]
        max_ref[:tiles] = max_own[...]
        sum_ref[:tiles] = sum_own[...]
        cosines = cos_in[...]
        sines = sin_in[...]
        for i, q_in in enumerate((q1, q2, q3)):
            turn_tiles(q_in, q_ref, (i + 1) * tiles, cosines, sines)
        for copy in copies:
            copy.wait()
        visit(meta, base, count, q_ref, kv_ref, vt_ref, s_ref, p_ref, top_ref, keep_ref, acc_ref, max_ref, sum_ref, items)

    return kernel


def make_middle(base, count):
    def kernel(meta, q_ref, acc_in, max_in, sum_in, *rest):
        kv_in = rest[:count]
        acc_ref, max_ref, sum_ref, sems, kv_ref, vt_ref, s_ref, p_ref, top_ref, keep_ref, items = rest[count:]
        pairs = [(kv, kv_ref.at[e]) for e, kv in enumerate(kv_in)]
        copies = fetch(pairs + [(acc_in, acc_ref)], sems)
        max_ref[...] = max_in[...]
        sum_ref[...] = sum_in[...]
        for copy in copies:
            copy.wait()
        visit(meta, base, count, q_ref, kv_ref, vt_ref, s_ref, p_ref, top_ref, keep_ref, acc_ref, max_ref, sum_ref, items)

    return kernel


def stack(maxima, sums):
    rows = []
    for line in (maxima, sums):
        heads = line.shape[1] // TILE
        rows += [line[:, h * TILE : (h + 1) * TILE] for h in range(heads)]
        rows.append(jnp.zeros((8 - heads, TILE), jnp.float32))
    return jnp.concatenate(rows, axis=0)


def pack(out, at, stats):
    high = stats.astype(jnp.bfloat16)
    left = stats - high.astype(jnp.float32)
    middle = left.astype(jnp.bfloat16)
    low = (left - middle.astype(jnp.float32)).astype(jnp.bfloat16)
    for n, piece in enumerate((high, middle, low)):
        out[at + 16 * n : at + 16 * (n + 1)] = piece


def unpack(part, at):
    pieces = [part[at + 16 * n : at + 16 * (n + 1)].astype(jnp.float32) for n in range(3)]
    stats = pieces[0] + pieces[1] + pieces[2]
    return stats[:8], stats[8:]


def safe(total):
    return jnp.where(total > 0, 1.0 / jnp.where(total > 0, total, 1.0), 0.0)


def make_last(base, count):
    def kernel(meta, q_ref, acc_in, max_in, sum_in, *rest):
        kv_in = rest[:count]
        tiles = (q_ref.shape[0] - 1) // PLANE
        outs = rest[count : count + 5 * tiles]
        acc_ref, max_ref, sum_ref, sems, kv_ref, vt_ref, s_ref, p_ref, top_ref, keep_ref, items = rest[count + 5 * tiles :]
        pairs = [(kv, kv_ref.at[e]) for e, kv in enumerate(kv_in)]
        copies = fetch(pairs + [(acc_in, acc_ref)], sems)
        max_ref[...] = max_in[...]
        sum_ref[...] = sum_in[...]
        for copy in copies:
            copy.wait()
        visit(meta, base, count, q_ref, kv_ref, vt_ref, s_ref, p_ref, top_ref, keep_ref, acc_ref, max_ref, sum_ref, items)
        heads = q_ref.shape[1] // TILE
        for j in range(tiles):
            acc_own, stats_own, acc_two, stats_two, swap = outs[5 * j : 5 * j + 5]
            acc_own[...] = acc_ref[j]
            stats_own[...] = stack(max_ref[j], sum_ref[j])
            two = 2 * tiles + j
            acc_two[...] = acc_ref[two]
            stats_two[...] = stack(max_ref[two], sum_ref[two])
            for slot, i in enumerate((1, 3)):
                at = i * tiles + j
                inverse = safe(sum_ref[at])
                for h in range(heads):
                    lanes = slice(h * TILE, (h + 1) * TILE)
                    swap[slot, h * HD : (h + 1) * HD] = (
                        acc_ref[at, :, lanes] * inverse[:, lanes]
                    ).astype(jnp.bfloat16)
                pack(swap.at[slot], heads * HD, stack(max_ref[at], sum_ref[at]))

    return kernel


def merge_kernel(acc_two, stats_two, swapped, out):
    heads = acc_two.shape[1] // TILE
    other = swapped.at[1]
    max_a, sum_a = stats_two[:8], stats_two[8:]
    max_b, sum_b = unpack(other, heads * HD)
    top = jnp.maximum(max_a, max_b)
    scale_a = jnp.exp2((max_a - top) * RATE)
    mass_b = sum_b * jnp.exp2((max_b - top) * RATE)
    total = sum_a * scale_a + mass_b
    inverse = safe(total)
    share_a = scale_a * inverse
    share_b = mass_b * inverse
    for h in range(heads):
        lanes = slice(h * TILE, (h + 1) * TILE)
        rows = slice(h * HD, (h + 1) * HD)
        value = acc_two[:, lanes] * share_a[h : h + 1]
        value = value + other[rows].astype(jnp.float32) * share_b[h : h + 1]
        out[rows] = value.astype(jnp.bfloat16)
    pack(out, heads * HD, jnp.concatenate([top, total], axis=0))


def make_combine(j):
    def kernel(meta, acc_own, stats_own, swapped, crossed, attn_ref):
        heads = acc_own.shape[1] // TILE
        parts = (swapped.at[0], crossed)
        maxima = [stats_own[:8]]
        sums = [stats_own[8:]]
        for part in parts:
            found = unpack(part, heads * HD)
            maxima.append(found[0])
            sums.append(found[1])
        top = jnp.maximum(jnp.maximum(maxima[0], maxima[1]), maxima[2])
        factor = [jnp.exp2((m - top) * RATE) for m in maxima]
        mass = [f * s for f, s in zip(factor, sums)]
        inverse = safe(mass[0] + mass[1] + mass[2])
        shares = [factor[0] * inverse] + [m * inverse for m in mass[1:]]
        live = lax.broadcasted_iota(jnp.int32, (HD, TILE), 1) + j * TILE < meta[0]
        for h in range(heads):
            lanes = slice(h * TILE, (h + 1) * TILE)
            value = acc_own[:, lanes] * shares[0][h : h + 1]
            for w, part in zip(shares[1:], parts):
                value = value + w[h : h + 1] * part[h * HD : (h + 1) * HD].astype(jnp.float32)
            value = jnp.transpose(jnp.where(live, value, 0.0))
            attn_ref[:, h * HD : (h + 1) * HD] = value.astype(jnp.bfloat16)

    return kernel


def project_kernel(where, attn_near, attn_far, weight_in, mine_in, theirs_in, *rest):
    paths = len(PATHS)
    outs = rest[:paths]
    near_ref, far_ref, sems = rest[paths:]
    columns = near_ref.shape[2]
    tensor, core = where[0], where[1]

    def copy_near(k):
        at = pl.multiple_of((tensor ^ k) * columns, HD)
        return pltpu.make_async_copy(weight_in.at[:, pl.ds(at, columns)], near_ref.at[k], sems.at[0, k])

    def copy_far(k, source):
        at = pl.multiple_of(((tensor ^ k) % 2) * columns, HD)
        return pltpu.make_async_copy(source.at[:, pl.ds(at, columns)], far_ref.at[k], sems.at[1, k])

    for k in PATHS:
        copy_near(k).start()
        same = ((tensor ^ k) % FAR) // 2 == core

        @pl.when(same)
        def _(k=k):
            copy_far(k, mine_in).start()

        @pl.when(jnp.logical_not(same))
        def _(k=k):
            copy_far(k, theirs_in).start()

    for k in PATHS:
        copy_near(k).wait()
        copy_far(k, mine_in).wait()
        total = jnp.dot(attn_near[...], near_ref[k], preferred_element_type=jnp.float32)
        total = total + jnp.dot(attn_far[...], far_ref[k], preferred_element_type=jnp.float32)
        outs[k][...] = total.astype(outs[k].dtype)


def cost(blocks, bytes_accessed):
    pairs = blocks * 1280 * 512
    return pl.CostEstimate(
        flops=4 * pairs * HD, bytes_accessed=bytes_accessed, transcendentals=pairs
    )


def shards(
    suffix_query,
    suffix_key,
    suffix_value,
    prefix_key,
    prefix_value,
    residual,
    out_weight,
    norm_gain,
    lengths,
    request_slot,
    prefix_owner,
    request_group,
):
    slots = suffix_query.shape[0]
    heads = suffix_query.shape[1] // HD
    devices = lax.axis_size("req")
    planes = devices // PLANE
    place = lax.axis_index("req")
    tensor = lax.axis_index("tp")
    ways = lax.axis_size("tp")
    per_group = devices // GROUPS
    block = prefix_key.shape[1]
    part = block // 2
    prefix_length = block * per_group
    bf16 = jnp.bfloat16
    f32 = jnp.float32

    def beside(k):
        return [(i, i ^ k) for i in range(devices)]

    up_pairs = [(i, (i + PLANE) % devices) for i in range(devices)]
    down_pairs = [(i, (i - PLANE) % devices) for i in range(devices)]

    core = place % 2
    width = residual.shape[1]
    columns = width // ways
    where = jnp.stack([tensor, core]).astype(jnp.int32)
    far_side = (tensor // FAR) ^ 1
    outgoing = lax.dynamic_slice_in_dim(
        out_weight, (far_side * FAR + 2 * core) * columns, 2 * columns, 1
    )
    weight_mine = lax.ppermute(outgoing, "tp", [(i, i ^ FAR) for i in range(ways)])

    def half(which):
        cut = [
            lax.dynamic_slice_in_dim(x, which * part, part, 1) for x in (prefix_key, prefix_value)
        ]
        return jnp.concatenate(cut, axis=0)

    theirs = half(1 - core)
    lanes = [half(core), lax.ppermute(theirs, "req", beside(1))]
    queries = []
    for k in range(1, PLANE):
        queries.append(lax.ppermute(suffix_query, "req", beside(k)))

    entries = {(0, 0): lanes[0], (0, 1): lanes[1]}
    half_way = planes // 2
    for lane in range(2):
        moving_up = lanes[lane]
        moving_down = lanes[lane]
        for step in range(1, half_way):
            moving_up = lax.ppermute(moving_up, "req", up_pairs)
            moving_down = lax.ppermute(moving_down, "req", down_pairs)
            entries[(-step, lane)] = moving_up
            entries[(step, lane)] = moving_down
        if lane == 0:
            entries[(-half_way, 0)] = lax.ppermute(moving_up, "req", up_pairs)
        else:
            entries[(half_way, 1)] = lax.ppermute(moving_down, "req", down_pairs)

    batches = [
        [(0, 0), (0, 1), (-1, 0), (1, 0), (-1, 1), (1, 1)],
        [(-2, 0), (2, 0), (-2, 1), (2, 1)],
        [(-3, 0), (3, 0), (-3, 1), (3, 1)],
        [(-half_way, 0), (half_way, 1)],
    ]
    order = [key for batch in batches for key in batch]

    numbers = jnp.arange(devices, dtype=jnp.int32)
    owner_match = prefix_owner[None, :] == numbers[:, None]
    holder_group = jnp.sum(jnp.where(owner_match, numbers[None, :], 0), axis=1) // per_group
    slot_match = request_slot[:, None] == numbers[None, :]
    asker_group = jnp.sum(jnp.where(slot_match, request_group[:, 0][None, :], 0), axis=1)
    asker_length = jnp.sum(jnp.where(slot_match, lengths[None, :], 0), axis=1)
    nearby = place ^ jnp.arange(PLANE, dtype=jnp.int32)
    near = nearby[:, None] == numbers[None, :]
    near_group = jnp.sum(jnp.where(near, asker_group[None, :], 0), axis=1)
    near_length = jnp.sum(jnp.where(near, asker_length[None, :], 0), axis=1)
    shift = jnp.array([key[0] for key in order], jnp.int32)
    twist = jnp.array([key[1] for key in order], jnp.int32)
    source = ((place // PLANE + shift) % planes) * PLANE + ((place % PLANE) ^ twist)
    from_there = source[:, None] == numbers[None, :]
    source_group = jnp.sum(jnp.where(from_there, holder_group[None, :], 0), axis=1)
    match = (source_group[:, None] == near_group[None, :]).astype(jnp.int32)
    tiles = (near_length + TILE - 1) // TILE
    meta = jnp.concatenate([near_length, tiles, match.reshape(-1)])

    half_dim = HD // 2
    positions = (prefix_length + jnp.arange(slots)).astype(f32)
    frequency = THETA ** (-(jnp.arange(half_dim).astype(f32) * 2.0 / HD))
    angles = positions[:, None] * frequency[None, :]
    cosines = jnp.cos(angles)
    sines = jnp.sin(angles)
    cosines = jnp.concatenate([cosines, cosines], axis=1)
    sines = jnp.concatenate([-sines, sines], axis=1)

    tiles_each = slots // TILE
    shape = jax.ShapeDtypeStruct
    q_own, cache_key, acc_own, max_own, sum_own = pl.pallas_call(
        own_kernel,
        out_shape=(
            shape((tiles_each, heads * TILE, HD), bf16),
            shape((slots, HD), bf16),
            shape((tiles_each, HD, heads * TILE), f32),
        shape((tiles_each, 1, heads * TILE), f32),
        shape((tiles_each, 1, heads * TILE), f32),
    ),
        in_specs=[full(SMEM)] + [full()] * 5,
        out_specs=(full(),) * 5,
        cost_estimate=cost(1, 3 << 20),
        compiler_params=params(),
        name="own",
    )(meta, suffix_query, suffix_key, suffix_value, cosines, sines)

    every = PLANE * tiles_each + 1
    lines = heads * TILE
    state_shapes = (
        shape((every, HD, lines), f32),
        shape((every, 1, lines), f32),
        shape((every, 1, lines), f32),
    )

    def work(count):
        return [
            pltpu.SemaphoreType.DMA((count + 1,)),
            pltpu.VMEM((count, 2, part, HD), bf16),
            pltpu.VMEM((count, HD + 16, part), bf16),
            pltpu.VMEM((2, part, lines), f32),
            pltpu.VMEM((2, part, lines), bf16),
            pltpu.VMEM((2, 1, lines), f32),
            pltpu.VMEM((2, 1, lines), f32),
            pltpu.SMEM((count * PLANE * tiles_each + 6, 2), jnp.int32),
        ]

    base = 0
    parts = [entries[key] for key in batches[0]]
    q_all, *state = pl.pallas_call(
        make_first(base, len(parts)),
        out_shape=(shape((every, lines, HD), bf16),) + state_shapes,
        in_specs=[full(SMEM)] + [full()] * 9 + [full(pl.ANY)] * len(parts),
        out_specs=(full(),) * 4,
        scratch_shapes=work(len(parts)),
        cost_estimate=cost(len(parts), 8 << 20),
        compiler_params=params(),
        name="first",
    )(meta, q_own, acc_own, max_own, sum_own, *queries, cosines, sines, *parts)
    base += len(parts)
    for batch in batches[1:-1]:
        parts = [entries[key] for key in batch]
        state = pl.pallas_call(
            make_middle(base, len(parts)),
            out_shape=state_shapes,
            in_specs=[full(SMEM), full(), full(pl.ANY), full(), full()] + [full(pl.ANY)] * len(parts),
            out_specs=(full(),) * 3,
            scratch_shapes=work(len(parts)),
            cost_estimate=cost(len(parts), 8 << 20),
            compiler_params=params(),
            name="middle",
        )(meta, q_all, *state, *parts)
        base += len(parts)
    parts = [entries[key] for key in batches[-1]]
    packed = heads * HD + 3 * 16
    last = pl.pallas_call(
        make_last(base, len(parts)),
        out_shape=(
            shape((HD, lines), f32),
            shape((16, TILE), f32),
            shape((HD, lines), f32),
            shape((16, TILE), f32),
            shape((2, packed, TILE), bf16),
        )
        * tiles_each,
        in_specs=[full(SMEM), full(), full(pl.ANY), full(), full()] + [full(pl.ANY)] * len(parts),
        out_specs=(full(),) * (5 * tiles_each),
        scratch_shapes=[
            pltpu.VMEM((every, HD, lines), f32),
            pltpu.VMEM((every, 1, lines), f32),
            pltpu.VMEM((every, 1, lines), f32),
        ]
        + work(len(parts)),
        cost_estimate=cost(len(parts), 8 << 20),
        compiler_params=params(),
        name="last",
    )(meta, q_all, *state, *parts)

    swapped = []
    for j in range(tiles_each):
        swapped.append(lax.ppermute(last[5 * j + 4], "req", beside(1)))
    crossed = []
    for j in range(tiles_each):
        merged = pl.pallas_call(
            merge_kernel,
            out_shape=shape((packed, TILE), bf16),
            in_specs=[full()] * 3,
            out_specs=full(),
            cost_estimate=pl.CostEstimate(flops=1 << 20, bytes_accessed=1 << 20, transcendentals=0),
            compiler_params=params(),
            name="merge",
        )(last[5 * j + 2], last[5 * j + 3], swapped[j])
        crossed.append(lax.ppermute(merged, "req", beside(2)))
    near = []
    far = []
    for j in range(tiles_each):
        attn = pl.pallas_call(
            make_combine(j),
            out_shape=shape((TILE, heads * HD), bf16),
            in_specs=[full(SMEM)] + [full()] * 4,
            out_specs=full(),
            cost_estimate=pl.CostEstimate(flops=1 << 20, bytes_accessed=1 << 20, transcendentals=0),
            compiler_params=params(),
            name="combine",
        )(meta, last[5 * j], last[5 * j + 1], swapped[j], crossed[j])
        near.append(attn)
        far.append(lax.ppermute(attn, "tp", [(i, i ^ FAR) for i in range(ways)]))
    weight_theirs = lax.ppermute(weight_mine, "req", beside(1))
    shared = []
    paths = len(PATHS)
    for j in range(tiles_each):
        pieces = pl.pallas_call(
            project_kernel,
            out_shape=tuple(
                shape((TILE, columns), bf16 if k else f32) for k in range(paths)
            ),
            in_specs=[full(SMEM), full(), full()] + [full(pl.ANY)] * 3,
            out_specs=(full(),) * paths,
            scratch_shapes=[
                pltpu.VMEM((paths, heads * HD, columns), bf16),
                pltpu.VMEM((paths, heads * HD, columns), bf16),
                pltpu.SemaphoreType.DMA((2, paths)),
            ],
            cost_estimate=pl.CostEstimate(
                flops=2 * TILE * heads * HD * width,
                bytes_accessed=8 << 20,
                transcendentals=0,
            ),
            compiler_params=params(47),
            name="project",
        )(where, near[j], far[j], out_weight, weight_mine, weight_theirs)
        total = pieces[0]
        for k in range(1, paths):
            piece = lax.ppermute(pieces[k], "tp", [(i, i ^ k) for i in range(ways)])
            total = total + piece.astype(f32)
        shared.append(total)
    shared = jnp.concatenate(shared, axis=0)
    own_residual = lax.dynamic_slice_in_dim(residual, tensor * columns, columns, 1)
    hidden = (own_residual.astype(f32) + shared).astype(bf16)
    widened = hidden.astype(f32)
    squares = jnp.sum(widened * widened, axis=1).reshape(slots // HD, HD)
    squares = jnp.pad(squares, ((0, 8 - slots // HD), (0, 0)))
    spread = lax.all_to_all(jnp.broadcast_to(squares[None], (ways, 8, HD)), "tp", 0, 0)
    row_squares = jnp.sum(spread, axis=0)[: slots // HD].reshape(slots)
    scale_rows = lax.rsqrt(row_squares / width + EPSILON)
    normed = (widened * scale_rows[:, None] * norm_gain.astype(f32)[None, :]).astype(bf16)
    return (hidden, normed, cache_key)


def solution(mesh):
    return jax.shard_map(
        shards,
        mesh=mesh,
        in_specs=(
            P("req", "tp"),
            P("req", "tp"),
            P("req", "tp"),
            P("req", None, "tp"),
            P("req", None, "tp"),
            P("req", None),
            P("tp", None),
            P("tp"),
            P(),
            P(),
            P(),
            P(),
        ),
        out_specs=(P("req", "tp"), P("req", "tp"), P("req", "tp")),
        check_vma=False,
    )
```

```python
import jax
import jax.numpy as jnp
from jax import lax
from jax.experimental import pallas as pl
from jax.experimental.pallas import tpu as pltpu
from jax.sharding import PartitionSpec as P


HD = 128
GROUPS = 4
PLANE = 4
TILE = 128
THETA = 1000000.0
NEGATIVE = -1e30
EPSILON = 1e-06
LOG2E = 1.4426950408889634
PATHS = (2, 3, 1, 0)
FAR = 4


SMEM = pltpu.SMEM
VMEM = pltpu.VMEM


def full(space=VMEM):
    return pl.BlockSpec(memory_space=space)


def params(limit=26):
    return pltpu.CompilerParams(vmem_limit_bytes=limit * 1024 * 1024)


RATE = HD ** (-0.5) * LOG2E
NT = (((1,), (1,)), ((), ()))


def turn(x, cosines, sines):
    return x * cosines + pltpu.roll(x, HD // 2, 1) * sines


def turn_tiles(q_in, q_ref, at, cosines, sines):
    for j in range(q_in.shape[0] // TILE):
        rows = slice(j * TILE, (j + 1) * TILE)
        for h in range(q_ref.shape[1] // TILE):
            x = q_in[rows, h * HD : (h + 1) * HD].astype(jnp.float32)
            q_ref[at + j, h * TILE : (h + 1) * TILE] = turn(x, cosines[rows], sines[rows]).astype(
                jnp.bfloat16
            )


def spans(width):
    return [(low, min(low + 2 * TILE, width)) for low in range(0, width, 2 * TILE)]


def own_kernel(meta, q_in, k_in, v_in, cos_in, sin_in, q_out, key_out, acc_ref, max_ref, sum_ref):
    tiles, lines = q_out.shape[:2]
    slots = k_in.shape[0]
    length = meta[0]
    cosines = cos_in[...]
    sines = sin_in[...]
    turn_tiles(q_in, q_out, 0, cosines, sines)
    turned = turn(k_in[...].astype(jnp.float32), cosines, sines)
    place = lax.broadcasted_iota(jnp.int32, turned.shape, 0)
    key_out[...] = jnp.where(place < length, turned, 0.0).astype(jnp.bfloat16)
    k = key_out[...]
    v = v_in[...].T
    u = lax.broadcasted_iota(jnp.int32, (slots, TILE), 0)
    t = lax.broadcasted_iota(jnp.int32, (slots, TILE), 1)
    for j in range(tiles):
        visible = (u <= t + j * TILE) & (u < length)
        for low in range(0, lines, TILE):
            high = low + TILE
            scores = lax.dot_general(
                k, q_out[j, low:high], NT, preferred_element_type=jnp.float32
            )
            scores = jnp.where(visible, scores, NEGATIVE)
            top = jnp.max(scores, axis=0, keepdims=True)
            weights = jnp.exp2((scores - top) * RATE)
            max_ref[j, :, low:high] = top
            sum_ref[j, :, low:high] = jnp.sum(weights, axis=0, keepdims=True)
            acc_ref[j, :, low:high] = jnp.dot(
                v, weights.astype(jnp.bfloat16), preferred_element_type=jnp.float32
            )


def visit(meta, base, count, q_ref, kv_ref, vt_ref, s_ref, p_ref, top_ref, keep_ref, acc_ref, max_ref, sum_ref, items):
    spare = q_ref.shape[0] - 1
    tiles = spare // PLANE
    part = kv_ref.shape[2]
    cuts = spans(q_ref.shape[1])
    for e in range(count):
        vt_ref[e, :HD] = kv_ref[e, 1].T
        vt_ref[e, HD:] = jnp.ones((16, part), jnp.bfloat16)
    for x in range(2):
        items[x, 0] = 0
        items[x, 1] = spare
    n = jnp.int32(2)
    for e in range(count):
        for i in range(PLANE):
            for j in range(tiles):
                live = (meta[2 * PLANE + (base + e) * PLANE + i] == 1) & (j < meta[PLANE + i])

                @pl.when(live)
                def _(n=n, e=e, i=i, j=j):
                    items[n, 0] = e
                    items[n, 1] = i * tiles + j

                n = n + live.astype(jnp.int32)
    for x in range(4):
        items[n + x, 0] = 0
        items[n + x, 1] = spare

    def score(step, slot):
        k = kv_ref[items[step, 0], 0]
        at = items[step, 1]
        for low, high in cuts:
            scores = lax.dot_general(
                k, q_ref[at, low:high], NT, preferred_element_type=jnp.float32
            )
            s_ref[slot, :, low:high] = scores
            top_ref[slot, :, low:high] = jnp.max(scores, axis=0, keepdims=True)

    def weigh(step, slot):
        at = items[step, 1]
        old = max_ref[at]
        new = jnp.maximum(old, top_ref[slot])
        max_ref[at] = new
        keep_ref[slot] = jnp.exp2((old - new) * RATE)
        for low, high in cuts:
            p_ref[slot, :, low:high] = jnp.exp2(
                (s_ref[slot, :, low:high] - new[:, low:high]) * RATE
            ).astype(jnp.bfloat16)

    def gather(step, slot):
        v = vt_ref[items[step, 0]]
        at = items[step, 1]
        for low, high in cuts:
            keep = keep_ref[slot, :, low:high]
            mixed = jnp.dot(v, p_ref[slot, :, low:high], preferred_element_type=jnp.float32)
            acc_ref[at, :, low:high] = acc_ref[at, :, low:high] * keep + mixed[:HD]
            sum_ref[at, :, low:high] = sum_ref[at, :, low:high] * keep + mixed[HD : HD + 1]

    @pl.when(n > 2)
    def _():
        def body(t, carry):
            for x in range(2):
                step = 2 * t + x
                gather(step, x)
                weigh(step + 1, 1 - x)
                score(step + 2, x)
            return carry

        lax.fori_loop(0, (n + 1) // 2, body, 0)


def fetch(pairs, sems):
    copies = [
        pltpu.make_async_copy(source, target, sems.at[n])
        for n, (source, target) in enumerate(pairs)
    ]
    for copy in copies:
        copy.start()
    return copies


def make_first(base, count):
    def kernel(meta, q_own, acc_own, max_own, sum_own, q1, q2, q3, cos_in, sin_in, *rest):
        kv_in = rest[:count]
        q_ref, acc_ref, max_ref, sum_ref, sems, kv_ref, vt_ref, s_ref, p_ref, top_ref, keep_ref, items = rest[count:]
        copies = fetch([(kv, kv_ref.at[e]) for e, kv in enumerate(kv_in)], sems)
        tiles = q_own.shape[0]
        acc_ref[tiles:] = jnp.zeros_like(acc_ref[tiles:])
        max_ref[tiles:] = jnp.full_like(max_ref[tiles:], NEGATIVE)
        sum_ref[tiles:] = jnp.zeros_like(sum_ref[tiles:])
        q_ref[:tiles] = q_own[...]
        q_ref[PLANE * tiles] = q_own[0]
        acc_ref[:tiles] = acc_own[...]
        max_ref[:tiles] = max_own[...]
        sum_ref[:tiles] = sum_own[...]
        cosines = cos_in[...]
        sines = sin_in[...]
        for i, q_in in enumerate((q1, q2, q3)):
            turn_tiles(q_in, q_ref, (i + 1) * tiles, cosines, sines)
        for copy in copies:
            copy.wait()
        visit(meta, base, count, q_ref, kv_ref, vt_ref, s_ref, p_ref, top_ref, keep_ref, acc_ref, max_ref, sum_ref, items)

    return kernel


def make_middle(base, count):
    def kernel(meta, q_ref, acc_in, max_in, sum_in, *rest):
        kv_in = rest[:count]
        acc_ref, max_ref, sum_ref, sems, kv_ref, vt_ref, s_ref, p_ref, top_ref, keep_ref, items = rest[count:]
        pairs = [(kv, kv_ref.at[e]) for e, kv in enumerate(kv_in)]
        copies = fetch(pairs + [(acc_in, acc_ref)], sems)
        max_ref[...] = max_in[...]
        sum_ref[...] = sum_in[...]
        for copy in copies:
            copy.wait()
        visit(meta, base, count, q_ref, kv_ref, vt_ref, s_ref, p_ref, top_ref, keep_ref, acc_ref, max_ref, sum_ref, items)

    return kernel


def stack(maxima, sums):
    rows = []
    for line in (maxima, sums):
        heads = line.shape[1] // TILE
        rows += [line[:, h * TILE : (h + 1) * TILE] for h in range(heads)]
        rows.append(jnp.zeros((8 - heads, TILE), jnp.float32))
    return jnp.concatenate(rows, axis=0)


def pack(out, at, stats):
    high = stats.astype(jnp.bfloat16)
    left = stats - high.astype(jnp.float32)
    middle = left.astype(jnp.bfloat16)
    low = (left - middle.astype(jnp.float32)).astype(jnp.bfloat16)
    for n, piece in enumerate((high, middle, low)):
        out[at + 16 * n : at + 16 * (n + 1)] = piece


def unpack(part, at):
    pieces = [part[at + 16 * n : at + 16 * (n + 1)].astype(jnp.float32) for n in range(3)]
    stats = pieces[0] + pieces[1] + pieces[2]
    return stats[:8], stats[8:]


def safe(total):
    return jnp.where(total > 0, 1.0 / jnp.where(total > 0, total, 1.0), 0.0)


def make_last(base, count):
    def kernel(meta, q_ref, acc_in, max_in, sum_in, *rest):
        kv_in = rest[:count]
        tiles = (q_ref.shape[0] - 1) // PLANE
        outs = rest[count : count + 5 * tiles]
        acc_ref, max_ref, sum_ref, sems, kv_ref, vt_ref, s_ref, p_ref, top_ref, keep_ref, items = rest[count + 5 * tiles :]
        pairs = [(kv, kv_ref.at[e]) for e, kv in enumerate(kv_in)]
        copies = fetch(pairs + [(acc_in, acc_ref)], sems)
        max_ref[...] = max_in[...]
        sum_ref[...] = sum_in[...]
        for copy in copies:
            copy.wait()
        visit(meta, base, count, q_ref, kv_ref, vt_ref, s_ref, p_ref, top_ref, keep_ref, acc_ref, max_ref, sum_ref, items)
        heads = q_ref.shape[1] // TILE
        for j in range(tiles):
            acc_own, stats_own, acc_two, stats_two, swap = outs[5 * j : 5 * j + 5]
            acc_own[...] = acc_ref[j]
            stats_own[...] = stack(max_ref[j], sum_ref[j])
            two = 2 * tiles + j
            acc_two[...] = acc_ref[two]
            stats_two[...] = stack(max_ref[two], sum_ref[two])
            for slot, i in enumerate((1, 3)):
                at = i * tiles + j
                inverse = safe(sum_ref[at])
                for h in range(heads):
                    lanes = slice(h * TILE, (h + 1) * TILE)
                    swap[slot, h * HD : (h + 1) * HD] = (
                        acc_ref[at, :, lanes] * inverse[:, lanes]
                    ).astype(jnp.bfloat16)
                pack(swap.at[slot], heads * HD, stack(max_ref[at], sum_ref[at]))

    return kernel


def merge_kernel(acc_two, stats_two, swapped, out):
    heads = acc_two.shape[1] // TILE
    other = swapped.at[1]
    max_a, sum_a = stats_two[:8], stats_two[8:]
    max_b, sum_b = unpack(other, heads * HD)
    top = jnp.maximum(max_a, max_b)
    scale_a = jnp.exp2((max_a - top) * RATE)
    mass_b = sum_b * jnp.exp2((max_b - top) * RATE)
    total = sum_a * scale_a + mass_b
    inverse = safe(total)
    share_a = scale_a * inverse
    share_b = mass_b * inverse
    for h in range(heads):
        lanes = slice(h * TILE, (h + 1) * TILE)
        rows = slice(h * HD, (h + 1) * HD)
        value = acc_two[:, lanes] * share_a[h : h + 1]
        value = value + other[rows].astype(jnp.float32) * share_b[h : h + 1]
        out[rows] = value.astype(jnp.bfloat16)
    pack(out, heads * HD, jnp.concatenate([top, total], axis=0))


def make_combine(j):
    def kernel(meta, acc_own, stats_own, swapped, crossed, attn_ref):
        heads = acc_own.shape[1] // TILE
        parts = (swapped.at[0], crossed)
        maxima = [stats_own[:8]]
        sums = [stats_own[8:]]
        for part in parts:
            found = unpack(part, heads * HD)
            maxima.append(found[0])
            sums.append(found[1])
        top = jnp.maximum(jnp.maximum(maxima[0], maxima[1]), maxima[2])
        factor = [jnp.exp2((m - top) * RATE) for m in maxima]
        mass = [f * s for f, s in zip(factor, sums)]
        inverse = safe(mass[0] + mass[1] + mass[2])
        shares = [factor[0] * inverse] + [m * inverse for m in mass[1:]]
        live = lax.broadcasted_iota(jnp.int32, (HD, TILE), 1) + j * TILE < meta[0]
        for h in range(heads):
            lanes = slice(h * TILE, (h + 1) * TILE)
            value = acc_own[:, lanes] * shares[0][h : h + 1]
            for w, part in zip(shares[1:], parts):
                value = value + w[h : h + 1] * part[h * HD : (h + 1) * HD].astype(jnp.float32)
            value = jnp.transpose(jnp.where(live, value, 0.0))
            attn_ref[:, h * HD : (h + 1) * HD] = value.astype(jnp.bfloat16)

    return kernel


def project_kernel(where, attn_near, attn_far, weight_in, mine_in, theirs_in, *rest):
    paths = len(PATHS)
    outs = rest[:paths]
    near_ref, far_ref, sems = rest[paths:]
    columns = near_ref.shape[2]
    tensor, core = where[0], where[1]

    def copy_near(k):
        at = pl.multiple_of((tensor ^ k) * columns, HD)
        return pltpu.make_async_copy(weight_in.at[:, pl.ds(at, columns)], near_ref.at[k], sems.at[0, k])

    def copy_far(k, source):
        at = pl.multiple_of(((tensor ^ k) % 2) * columns, HD)
        return pltpu.make_async_copy(source.at[:, pl.ds(at, columns)], far_ref.at[k], sems.at[1, k])

    for k in PATHS:
        copy_near(k).start()
        same = ((tensor ^ k) % FAR) // 2 == core

        @pl.when(same)
        def _(k=k):
            copy_far(k, mine_in).start()

        @pl.when(jnp.logical_not(same))
        def _(k=k):
            copy_far(k, theirs_in).start()

    for k in PATHS:
        copy_near(k).wait()
        copy_far(k, mine_in).wait()
        total = jnp.dot(attn_near[...], near_ref[k], preferred_element_type=jnp.float32)
        total = total + jnp.dot(attn_far[...], far_ref[k], preferred_element_type=jnp.float32)
        outs[k][...] = total.astype(outs[k].dtype)


def cost(blocks, bytes_accessed):
    pairs = blocks * 1280 * 512
    return pl.CostEstimate(
        flops=4 * pairs * HD, bytes_accessed=bytes_accessed, transcendentals=pairs
    )


def shards(
    suffix_query,
    suffix_key,
    suffix_value,
    prefix_key,
    prefix_value,
    residual,
    out_weight,
    norm_gain,
    lengths,
    request_slot,
    prefix_owner,
    request_group,
):
    slots = suffix_query.shape[0]
    heads = suffix_query.shape[1] // HD
    devices = lax.axis_size("req")
    planes = devices // PLANE
    place = lax.axis_index("req")
    tensor = lax.axis_index("tp")
    ways = lax.axis_size("tp")
    per_group = devices // GROUPS
    block = prefix_key.shape[1]
    part = block // 2
    prefix_length = block * per_group
    bf16 = jnp.bfloat16
    f32 = jnp.float32

    def beside(k):
        return [(i, i ^ k) for i in range(devices)]

    up_pairs = [(i, (i + PLANE) % devices) for i in range(devices)]
    down_pairs = [(i, (i - PLANE) % devices) for i in range(devices)]

    core = place % 2
    width = residual.shape[1]
    columns = width // ways
    where = jnp.stack([tensor, core]).astype(jnp.int32)
    far_side = (tensor // FAR) ^ 1
    outgoing = lax.dynamic_slice_in_dim(
        out_weight, (far_side * FAR + 2 * core) * columns, 2 * columns, 1
    )
    weight_mine = lax.ppermute(outgoing, "tp", [(i, i ^ FAR) for i in range(ways)])
    both = jnp.concatenate([prefix_key, prefix_value], axis=0)
    mine = lax.dynamic_slice_in_dim(both, core * part, part, 1)
    theirs = lax.dynamic_slice_in_dim(both, (1 - core) * part, part, 1)
    lanes = [mine, lax.ppermute(theirs, "req", beside(1))]
    queries = []
    for k in range(1, PLANE):
        queries.append(lax.ppermute(suffix_query, "req", beside(k)))

    entries = {(0, 0): lanes[0], (0, 1): lanes[1]}
    half_way = planes // 2
    for lane in range(2):
        moving_up = lanes[lane]
        moving_down = lanes[lane]
        for step in range(1, half_way):
            moving_up = lax.ppermute(moving_up, "req", up_pairs)
            moving_down = lax.ppermute(moving_down, "req", down_pairs)
            entries[(-step, lane)] = moving_up
            entries[(step, lane)] = moving_down
        if lane == 0:
            entries[(-half_way, 0)] = lax.ppermute(moving_up, "req", up_pairs)
        else:
            entries[(half_way, 1)] = lax.ppermute(moving_down, "req", down_pairs)

    batches = [
        [(0, 0), (0, 1), (-1, 0), (1, 0), (-1, 1), (1, 1)],
        [(-2, 0), (2, 0), (-2, 1), (2, 1)],
        [(-3, 0), (3, 0), (-3, 1), (3, 1)],
        [(-half_way, 0), (half_way, 1)],
    ]
    order = [key for batch in batches for key in batch]

    numbers = jnp.arange(devices, dtype=jnp.int32)
    owner_match = prefix_owner[None, :] == numbers[:, None]
    holder_group = jnp.sum(jnp.where(owner_match, numbers[None, :], 0), axis=1) // per_group
    slot_match = request_slot[:, None] == numbers[None, :]
    asker_group = jnp.sum(jnp.where(slot_match, request_group[:, 0][None, :], 0), axis=1)
    asker_length = jnp.sum(jnp.where(slot_match, lengths[None, :], 0), axis=1)
    nearby = place ^ jnp.arange(PLANE, dtype=jnp.int32)
    near = nearby[:, None] == numbers[None, :]
    near_group = jnp.sum(jnp.where(near, asker_group[None, :], 0), axis=1)
    near_length = jnp.sum(jnp.where(near, asker_length[None, :], 0), axis=1)
    shift = jnp.array([key[0] for key in order], jnp.int32)
    twist = jnp.array([key[1] for key in order], jnp.int32)
    source = ((place // PLANE + shift) % planes) * PLANE + ((place % PLANE) ^ twist)
    from_there = source[:, None] == numbers[None, :]
    source_group = jnp.sum(jnp.where(from_there, holder_group[None, :], 0), axis=1)
    match = (source_group[:, None] == near_group[None, :]).astype(jnp.int32)
    tiles = (near_length + TILE - 1) // TILE
    meta = jnp.concatenate([near_length, tiles, match.reshape(-1)])

    half_dim = HD // 2
    positions = (prefix_length + jnp.arange(slots)).astype(f32)
    frequency = THETA ** (-(jnp.arange(half_dim).astype(f32) * 2.0 / HD))
    angles = positions[:, None] * frequency[None, :]
    cosines = jnp.cos(angles)
    sines = jnp.sin(angles)
    cosines = jnp.concatenate([cosines, cosines], axis=1)
    sines = jnp.concatenate([-sines, sines], axis=1)

    tiles_each = slots // TILE
    shape = jax.ShapeDtypeStruct
    q_own, cache_key, acc_own, max_own, sum_own = pl.pallas_call(
        own_kernel,
        out_shape=(
            shape((tiles_each, heads * TILE, HD), bf16),
            shape((slots, HD), bf16),
            shape((tiles_each, HD, heads * TILE), f32),
        shape((tiles_each, 1, heads * TILE), f32),
        shape((tiles_each, 1, heads * TILE), f32),
    ),
        in_specs=[full(SMEM)] + [full()] * 5,
        out_specs=(full(),) * 5,
        cost_estimate=cost(1, 3 << 20),
        compiler_params=params(),
        name="own",
    )(meta, suffix_query, suffix_key, suffix_value, cosines, sines)

    every = PLANE * tiles_each + 1
    lines = heads * TILE
    state_shapes = (
        shape((every, HD, lines), f32),
        shape((every, 1, lines), f32),
        shape((every, 1, lines), f32),
    )

    def work(count):
        return [
            pltpu.SemaphoreType.DMA((count + 1,)),
            pltpu.VMEM((count, 2, part, HD), bf16),
            pltpu.VMEM((count, HD + 16, part), bf16),
            pltpu.VMEM((2, part, lines), f32),
            pltpu.VMEM((2, part, lines), bf16),
            pltpu.VMEM((2, 1, lines), f32),
            pltpu.VMEM((2, 1, lines), f32),
            pltpu.SMEM((count * PLANE * tiles_each + 6, 2), jnp.int32),
        ]

    base = 0
    parts = [entries[key] for key in batches[0]]
    q_all, *state = pl.pallas_call(
        make_first(base, len(parts)),
        out_shape=(shape((every, lines, HD), bf16),) + state_shapes,
        in_specs=[full(SMEM)] + [full()] * 9 + [full(pl.ANY)] * len(parts),
        out_specs=(full(),) * 4,
        scratch_shapes=work(len(parts)),
        cost_estimate=cost(len(parts), 8 << 20),
        compiler_params=params(),
        name="first",
    )(meta, q_own, acc_own, max_own, sum_own, *queries, cosines, sines, *parts)
    base += len(parts)
    for batch in batches[1:-1]:
        parts = [entries[key] for key in batch]
        state = pl.pallas_call(
            make_middle(base, len(parts)),
            out_shape=state_shapes,
            in_specs=[full(SMEM), full(), full(pl.ANY), full(), full()] + [full(pl.ANY)] * len(parts),
            out_specs=(full(),) * 3,
            scratch_shapes=work(len(parts)),
            cost_estimate=cost(len(parts), 8 << 20),
            compiler_params=params(),
            name="middle",
        )(meta, q_all, *state, *parts)
        base += len(parts)
    parts = [entries[key] for key in batches[-1]]
    packed = heads * HD + 3 * 16
    last = pl.pallas_call(
        make_last(base, len(parts)),
        out_shape=(
            shape((HD, lines), f32),
            shape((16, TILE), f32),
            shape((HD, lines), f32),
            shape((16, TILE), f32),
            shape((2, packed, TILE), bf16),
        )
        * tiles_each,
        in_specs=[full(SMEM), full(), full(pl.ANY), full(), full()] + [full(pl.ANY)] * len(parts),
        out_specs=(full(),) * (5 * tiles_each),
        scratch_shapes=[
            pltpu.VMEM((every, HD, lines), f32),
            pltpu.VMEM((every, 1, lines), f32),
            pltpu.VMEM((every, 1, lines), f32),
        ]
        + work(len(parts)),
        cost_estimate=cost(len(parts), 8 << 20),
        compiler_params=params(),
        name="last",
    )(meta, q_all, *state, *parts)

    swapped = []
    for j in range(tiles_each):
        swapped.append(lax.ppermute(last[5 * j + 4], "req", beside(1)))
    crossed = []
    for j in range(tiles_each):
        merged = pl.pallas_call(
            merge_kernel,
            out_shape=shape((packed, TILE), bf16),
            in_specs=[full()] * 3,
            out_specs=full(),
            cost_estimate=pl.CostEstimate(flops=1 << 20, bytes_accessed=1 << 20, transcendentals=0),
            compiler_params=params(),
            name="merge",
        )(last[5 * j + 2], last[5 * j + 3], swapped[j])
        crossed.append(lax.ppermute(merged, "req", beside(2)))
    near = []
    far = []
    for j in range(tiles_each):
        attn = pl.pallas_call(
            make_combine(j),
            out_shape=shape((TILE, heads * HD), bf16),
            in_specs=[full(SMEM)] + [full()] * 4,
            out_specs=full(),
            cost_estimate=pl.CostEstimate(flops=1 << 20, bytes_accessed=1 << 20, transcendentals=0),
            compiler_params=params(),
            name="combine",
        )(meta, last[5 * j], last[5 * j + 1], swapped[j], crossed[j])
        near.append(attn)
        far.append(lax.ppermute(attn, "tp", [(i, i ^ FAR) for i in range(ways)]))
    weight_theirs = lax.ppermute(weight_mine, "req", beside(1))
    shared = []
    paths = len(PATHS)
    for j in range(tiles_each):
        pieces = pl.pallas_call(
            project_kernel,
            out_shape=tuple(
                shape((TILE, columns), bf16 if k else f32) for k in range(paths)
            ),
            in_specs=[full(SMEM), full(), full()] + [full(pl.ANY)] * 3,
            out_specs=(full(),) * paths,
            scratch_shapes=[
                pltpu.VMEM((paths, heads * HD, columns), bf16),
                pltpu.VMEM((paths, heads * HD, columns), bf16),
                pltpu.SemaphoreType.DMA((2, paths)),
            ],
            cost_estimate=pl.CostEstimate(
                flops=2 * TILE * heads * HD * width,
                bytes_accessed=8 << 20,
                transcendentals=0,
            ),
            compiler_params=params(50),
            name="project",
        )(where, near[j], far[j], out_weight, weight_mine, weight_theirs)
        total = pieces[0]
        for k in range(1, paths):
            piece = lax.ppermute(pieces[k], "tp", [(i, i ^ k) for i in range(ways)])
            total = total + piece.astype(f32)
        shared.append(total)
    shared = jnp.concatenate(shared, axis=0)
    own_residual = lax.dynamic_slice_in_dim(residual, tensor * columns, columns, 1)
    hidden = (own_residual.astype(f32) + shared).astype(bf16)
    widened = hidden.astype(f32)
    squares = jnp.sum(widened * widened, axis=1).reshape(slots // HD, HD)
    squares = jnp.pad(squares, ((0, 8 - slots // HD), (0, 0)))
    spread = squares
    for k in (2, 3, 1):
        spread = spread + lax.ppermute(squares, "tp", [(i, i ^ k) for i in range(ways)])
    spread = spread + lax.ppermute(spread, "tp", [(i, i ^ FAR) for i in range(ways)])
    row_squares = spread[: slots // HD].reshape(slots)
    scale_rows = lax.rsqrt(row_squares / width + EPSILON)
    normed = (widened * scale_rows[:, None] * norm_gain.astype(f32)[None, :]).astype(bf16)
    return (hidden, normed, cache_key)


def solution(mesh):
    return jax.shard_map(
        shards,
        mesh=mesh,
        in_specs=(
            P("req", "tp"),
            P("req", "tp"),
            P("req", "tp"),
            P("req", None, "tp"),
            P("req", None, "tp"),
            P("req", None),
            P("tp", None),
            P("tp"),
            P(),
            P(),
            P(),
            P(),
        ),
        out_specs=(P("req", "tp"), P("req", "tp"), P("req", "tp")),
        check_vma=False,
    )
```
